32 devices in a mesh: fsdp: 4 (over z), seq: 8 (over y, x, core).
Axes of the slice: x: 2, y: 2, z: 4, core: 2. Of those that a mesh axis runs over, the one named last changes fastest.
Arguments:
- block_input: bfloat16 [8, 1536, 1024], P('fsdp', 'seq'), may hold values from -6 to 6
- positions: int32 [8, 1536], P('fsdp'), may hold values from 0 to 1535, as said below
- cotangent: bfloat16 [8, 1536, 1024], P('fsdp', 'seq'), may hold values from -6 to 6
- attention_gain: bfloat16 [1024], P(('fsdp', 'seq')), may hold values from 0.099609375 to 1.8984375
- query_weight: bfloat16 [1024, 1024], P(('fsdp', 'seq')), may hold values from -0.1875 to 0.1875
- key_weight: bfloat16 [1024, 512], P(('fsdp', 'seq')), may hold values from -0.1875 to 0.1875
- value_weight: bfloat16 [1024, 512], P(('fsdp', 'seq')), may hold values from -0.1875 to 0.1875
- query_gain: bfloat16 [64], replicated, may hold values from 0.8 to 2
- key_gain: bfloat16 [64], replicated, may hold values from 0.8 to 2
- output_weight: bfloat16 [1024, 1024], P(('fsdp', 'seq')), may hold values from -0.75 to 0.75
- feedforward_gain: bfloat16 [1024], P(('fsdp', 'seq')), may hold values from 0.099609375 to 1.8984375
- gate_weight: bfloat16 [1024, 4608], P(('fsdp', 'seq')), may hold values from -0.1875 to 0.1875
- up_weight: bfloat16 [1024, 4608], P(('fsdp', 'seq')), may hold values from -0.1875 to 0.1875
- down_weight: bfloat16 [4608, 1024], P(('fsdp', 'seq')), may hold values from -0.09375 to 0.09375
Outputs:
- block_output: bfloat16 [8, 1536, 1024], P('fsdp', 'seq')
- input_grad: bfloat16 [8, 1536, 1024], P('fsdp', 'seq')
- attention_gain_grad: float32 [1024], P(('fsdp', 'seq'))
- query_grad: float32 [1024, 1024], P(('fsdp', 'seq'))
- key_grad: float32 [1024, 512], P(('fsdp', 'seq'))
- value_grad: float32 [1024, 512], P(('fsdp', 'seq'))
- query_gain_grad: float32 [64], replicated
- key_gain_grad: float32 [64], replicated
- output_grad: float32 [1024, 1024], P(('fsdp', 'seq'))
- feedforward_gain_grad: float32 [1024], P(('fsdp', 'seq'))
- gate_grad: float32 [1024, 4608], P(('fsdp', 'seq'))
- up_grad: float32 [1024, 4608], P(('fsdp', 'seq'))
- down_grad: float32 [4608, 1024], P(('fsdp', 'seq'))
The draws below stay inside these ranges and needn't reach their ends.
Inputs may be any that keep to these rules, and one draw needn't show every extreme that they name: In every sequence positions begin at 0, and each next one is one more or 0 (a new document); the first sequence is one document.
All inputs are finite; a program needn't handle non-finite values.
Results may differ from the reference program's by a relative error of at most 0.015.
Values may be sent and summed in bfloat16 or wider, within the bound.
No kernel may reach another device: no remote copies, remote signals or barrier semaphores. Data moves between devices by JAX's collectives and lax.ppermute only.
A program may use at most 256 MiB of HBM per device.

```python
import jax
import jax.numpy as jnp
from jax import lax

D = 1024
H = 16
KV = 8
HD = 64
FF = 4608
LEN = 1536
SEQS = 8


def draw_positions(key, part):
    marks = jax.random.randint(key, (SEQS, LEN), 0, LEN // 2 + 1) == 0
    index_row = jnp.arange(LEN, dtype=jnp.int32)
    starts = jnp.where(marks, index_row[None, :], 0).astype(jnp.int32)
    starts = starts.at[0].set(0)
    starts = lax.cummax(starts, axis=1)
    return (index_row[None, :] - starts).astype(jnp.int32)


def gain_values(key):
    values = jax.random.uniform(key, (HD,), jnp.float32, 0.8, 2.0)
    return values.astype(jnp.bfloat16)


def draw_query_gain(key, part):
    return gain_values(jax.random.fold_in(key, 11))


def draw_key_gain(key, part):
    return gain_values(jax.random.fold_in(key, 23))


def raised(entries, stream_key, source, target, blocks, factor):
    def block_of(axis_at):
        return (jnp.arange(entries.shape[axis_at]) // (entries.shape[axis_at] // blocks)).reshape((-1,) + (1,) * (entries.ndim - 1 - axis_at))

    first = jax.random.permutation(stream_key, blocks)[block_of(target)]
    second = (block_of(target) + blocks // 2) % blocks
    return jnp.where((block_of(source) == first) | (block_of(source) == second), factor * entries, entries)


def level_of(key, dims, split, smallest, high):
    def one(axis_at, parts):
        heights = jax.random.uniform(jax.random.fold_in(jax.random.fold_in(key, 6), axis_at), (parts,), jnp.float32, smallest / len(split), high / len(split))
        return jnp.repeat(jnp.exp(heights), dims[axis_at] // parts).reshape((-1,) + (1,) * (len(dims) - axis_at - 1))

    factor_of = one(*split[0])
    for cut in split[1:]:
        factor_of = factor_of * one(*cut)
    return factor_of


def centred(rng, dims, scale, reach, split=(), kind=jnp.bfloat16):
    drawn = scale * jax.random.normal(rng, dims, jnp.float32)
    if split:
        drawn = drawn * level_of(rng, dims, split, -0.22, 0.18)
    return jnp.clip(drawn, -reach, reach).astype(kind)


def bell_draw_with(stream_key, extent, spread, bound, cuts, heavy, kind=jnp.bfloat16):
    drawn = spread * jax.random.normal(stream_key, extent, jnp.float32)
    if cuts:
        drawn = drawn * level_of(stream_key, extent, cuts, -0.22, 0.18)
    return jnp.clip(raised(drawn, jax.random.fold_in(stream_key, 3), *heavy), -bound, bound).astype(kind)


def setup_inputs(seed: int = 0) -> dict:
    splits = jax.random.split(jax.random.key(seed), 15)
    block_input = bell_draw_with(splits[0], (SEQS, LEN, D), 1.0, 6.0, ((0, 4), (1, 8)), (1, 2, 8, 2.0))
    positions = draw_positions(jax.random.fold_in(splits[14], 71), 0)
    cotangent = centred(splits[2], (SEQS, LEN, D), 1.0, 6.0, ((0, 4), (1, 8)))
    attention_gain = jnp.clip(1.0 + 0.18 * jax.random.normal(splits[3], (D,), jnp.float32), 0.099609375, 1.8984375).astype(jnp.bfloat16)
    query_weight = centred(splits[4], (D, H * HD), D ** -0.5, 0.1875, ((0, 32),))
    key_weight = centred(splits[5], (D, KV * HD), D ** -0.5, 0.1875, ((0, 32),))
    value_weight = centred(splits[6], (D, KV * HD), D ** -0.5, 0.1875, ((0, 32),))
    query_gain = draw_query_gain(jax.random.fold_in(splits[14], 71), 0)
    key_gain = draw_key_gain(jax.random.fold_in(splits[14], 71), 0)
    output_weight = centred(splits[9], (H * HD, D), (H * HD // 16) ** -0.5, 0.75, ((0, 32),))
    feedforward_gain = jnp.clip(1.0 + 0.18 * jax.random.normal(splits[10], (D,), jnp.float32), 0.099609375, 1.8984375).astype(jnp.bfloat16)
    gate_weight = centred(splits[11], (D, FF), D ** -0.5, 0.1875, ((0, 32),))
    up_weight = centred(splits[12], (D, FF), D ** -0.5, 0.1875, ((0, 32),))
    down_weight = centred(splits[13], (FF, D), FF ** -0.5, 0.09375, ((0, 32),))
    return dict(block_input=block_input, positions=positions, cotangent=cotangent, attention_gain=attention_gain, query_weight=query_weight, key_weight=key_weight, value_weight=value_weight, query_gain=query_gain, key_gain=key_gain, output_weight=output_weight, feedforward_gain=feedforward_gain, gate_weight=gate_weight, up_weight=up_weight, down_weight=down_weight)


rope_base = 1000000.0
eps = 1e-05
masked = -1e+30

def contract(formula, left, right):
    return jnp.einsum(formula, left.astype(jnp.float32), right.astype(jnp.float32))

def matmul(left, right):
    return jnp.dot(left, right, preferred_element_type=jnp.float32)

def rope_tables(places, head_width):
    half_width = head_width // 2
    inverse = rope_base ** (-(jnp.arange(half_width, dtype=jnp.float32) * 2.0) / head_width)
    angles = places.astype(jnp.float32)[:, None] * inverse[None, :]
    return (jnp.cos(angles)[:, None, :], jnp.sin(angles)[:, None, :])

def head_prep(raw_rows, gain_row, cosine, sine, head_count):
    row_count = raw_rows.shape[0]
    split_rows = raw_rows.reshape(row_count, head_count, -1)
    factor = lax.rsqrt(lax.optimization_barrier(jnp.mean(split_rows * split_rows, axis=-1, keepdims=True)) + eps)
    normed = split_rows * factor * gain_row
    half_width = normed.shape[-1] // 2
    lower = normed[..., :half_width]
    upper = normed[..., half_width:]
    turned = jnp.concatenate([lower * cosine - upper * sine, upper * cosine + lower * sine], axis=-1)
    return turned.reshape(row_count, -1)

def norm_fwd(values, gain_row):
    factor = lax.rsqrt(lax.optimization_barrier(jnp.mean(values * values, axis=-1, keepdims=True)) + eps)
    return (values * factor * gain_row, factor)

def norm_bwd(values, factor, gain_row, grad_result):
    normed = values * factor
    grad_normed = grad_result * gain_row
    grad_values = factor * (grad_normed - normed * lax.optimization_barrier(jnp.mean(grad_normed * normed, axis=-1, keepdims=True)))
    return (grad_values, lax.optimization_barrier(jnp.sum(grad_result * normed, axis=0)))

def masked_scores(queries, key_rows, doc_start, begin_row, end_row, scaling):
    query_index = jnp.arange(begin_row, end_row, dtype=jnp.int32)
    key_index = jnp.arange(end_row, dtype=jnp.int32)
    allowed = (key_index[None, :] <= query_index[:, None]) & (key_index[None, :] >= doc_start[begin_row:end_row, None])
    scores = contract('qhd,khd->hqk', queries[begin_row:end_row], key_rows[:end_row]) * scaling
    return jnp.where(allowed[None, :, :], scores, masked)

def attend_fwd(queries, key_rows, value_rows, doc_start):
    seq_length, head_count, head_width = queries.shape
    block_rows = min(512, seq_length)
    scaling = head_width ** (-0.5)
    out_blocks = []
    total_blocks = []
    for begin_row in range(0, seq_length, block_rows):
        end_row = begin_row + block_rows
        scores = masked_scores(queries, key_rows, doc_start, begin_row, end_row, scaling)
        largest = lax.optimization_barrier(jnp.max(scores, axis=-1, keepdims=True))
        log_total = largest + jnp.log(lax.optimization_barrier(jnp.sum(jnp.exp(scores - largest), axis=-1, keepdims=True)))
        attn_prob = jnp.exp(scores - log_total).astype(jnp.bfloat16)
        out_blocks.append(contract('hqk,khd->qhd', attn_prob, value_rows[:end_row]).astype(jnp.bfloat16))
        total_blocks.append(log_total[..., 0])
    return (jnp.concatenate(out_blocks, axis=0), jnp.concatenate(total_blocks, axis=1))

def attend_bwd(queries, key_rows, value_rows, outputs, log_totals, grad_result, doc_start):
    seq_length, head_count, head_width = queries.shape
    block_rows = min(512, seq_length)
    scaling = head_width ** (-0.5)
    carried = lax.optimization_barrier(jnp.sum(grad_result.astype(jnp.float32) * outputs.astype(jnp.float32), axis=-1)).T
    grad_query = []
    grad_key = jnp.zeros((seq_length, head_count, head_width), jnp.float32)
    grad_value = jnp.zeros((seq_length, head_count, head_width), jnp.float32)
    for begin_row in range(0, seq_length, block_rows):
        end_row = begin_row + block_rows
        scores = masked_scores(queries, key_rows, doc_start, begin_row, end_row, scaling)
        attn_prob = jnp.exp(scores - log_totals[:, begin_row:end_row, None])
        prob_half = attn_prob.astype(jnp.bfloat16)
        grad_rows = grad_result[begin_row:end_row]
        grad_value = grad_value.at[:end_row].add(contract('hqk,qhd->khd', prob_half, grad_rows))
        grad_prob = contract('qhd,khd->hqk', grad_rows, value_rows[:end_row])
        grad_score = (attn_prob * (grad_prob - carried[:, begin_row:end_row, None]) * scaling).astype(jnp.bfloat16)
        grad_query.append(contract('hqk,khd->qhd', grad_score, key_rows[:end_row]))
        grad_key = grad_key.at[:end_row].add(contract('hqk,qhd->khd', grad_score, queries[begin_row:end_row]))
    return (jnp.concatenate(grad_query, axis=0).astype(jnp.bfloat16), grad_key.astype(jnp.bfloat16), grad_value.astype(jnp.bfloat16))

def layer_pass(rows_in, places, cot_rows, attention_gain, query_weight, key_weight, value_weight, query_gain, key_gain, output_weight, feedforward_gain, gate_weight, up_weight, down_weight):
    seq_length = rows_in.shape[0]
    group_size = H // KV
    gain_one = attention_gain.astype(jnp.float32)
    gain_two = feedforward_gain.astype(jnp.float32)
    query_scale = query_gain.astype(jnp.float32)
    key_scale = key_gain.astype(jnp.float32)
    residual_in = rows_in.astype(jnp.float32)
    normed_one, factor_one = norm_fwd(residual_in, gain_one)
    normed_in = normed_one.astype(jnp.bfloat16)
    query_raw = matmul(normed_in, query_weight)
    key_raw = matmul(normed_in, key_weight)
    value_rows = matmul(normed_in, value_weight).astype(jnp.bfloat16)
    cosine, sine = rope_tables(places, HD)

    def query_side(raw_rows, gain_row):
        return head_prep(raw_rows, gain_row, cosine, sine, H)

    def key_side(raw_rows, gain_row):
        return head_prep(raw_rows, gain_row, cosine, sine, KV)
    query_rows = query_side(query_raw, query_scale).astype(jnp.bfloat16)
    key_rows = key_side(key_raw, key_scale).astype(jnp.bfloat16)
    queries = query_rows.reshape(seq_length, H, HD)
    keys_full = jnp.repeat(key_rows.reshape(seq_length, KV, HD), group_size, axis=1)
    values_full = jnp.repeat(value_rows.reshape(seq_length, KV, HD), group_size, axis=1)
    doc_start = (jnp.arange(seq_length, dtype=jnp.int32) - places).astype(jnp.int32)
    outputs, log_totals = attend_fwd(queries, keys_full, values_full, doc_start)
    attn_out = outputs.reshape(seq_length, H * HD)
    residual_mid = residual_in + matmul(attn_out, output_weight)
    normed_two, factor_two = norm_fwd(residual_mid, gain_two)
    normed_mid = normed_two.astype(jnp.bfloat16)
    gate_rows = matmul(normed_mid, gate_weight)
    up_rows = matmul(normed_mid, up_weight)
    sigma = jax.nn.sigmoid(gate_rows)
    hidden = (gate_rows * sigma * up_rows).astype(jnp.bfloat16)
    result = residual_mid + matmul(hidden, down_weight)
    block_output = result.astype(jnp.bfloat16)
    down_grad = matmul(hidden.T, cot_rows)
    grad_hidden = matmul(cot_rows, down_weight.T)
    grad_gate = (grad_hidden * up_rows * sigma * (1.0 + gate_rows * (1.0 - sigma))).astype(jnp.bfloat16)
    grad_up = (grad_hidden * gate_rows * sigma).astype(jnp.bfloat16)
    gate_grad = matmul(normed_mid.T, grad_gate)
    up_grad = matmul(normed_mid.T, grad_up)
    grad_normed_mid = matmul(grad_gate, gate_weight.T) + matmul(grad_up, up_weight.T)
    grad_mid_norm, gain_two_grad = norm_bwd(residual_mid, factor_two, gain_two, grad_normed_mid)
    grad_mid = cot_rows.astype(jnp.float32) + grad_mid_norm
    grad_mid_half = grad_mid.astype(jnp.bfloat16)
    output_grad = matmul(attn_out.T, grad_mid_half)
    grad_attn_out = matmul(grad_mid_half, output_weight.T).astype(jnp.bfloat16)
    grad_query_heads, grad_key_heads, grad_value_heads = attend_bwd(queries, keys_full, values_full, outputs, log_totals, grad_attn_out.reshape(seq_length, H, HD), doc_start)
    grad_key_sum = lax.optimization_barrier(jnp.sum(grad_key_heads.astype(jnp.float32).reshape(seq_length, KV, group_size, HD), axis=2)).reshape(seq_length, KV * HD)
    grad_value_rows = lax.optimization_barrier(jnp.sum(grad_value_heads.astype(jnp.float32).reshape(seq_length, KV, group_size, HD), axis=2)).reshape(seq_length, KV * HD).astype(jnp.bfloat16)
    _, query_back = jax.vjp(query_side, query_raw, query_scale)
    grad_query_raw, query_gain_grad = query_back(grad_query_heads.reshape(seq_length, H * HD).astype(jnp.float32))
    _, key_back = jax.vjp(key_side, key_raw, key_scale)
    grad_key_raw, key_gain_grad = key_back(grad_key_sum)
    grad_query_half = grad_query_raw.astype(jnp.bfloat16)
    grad_key_half = grad_key_raw.astype(jnp.bfloat16)
    query_grad = matmul(normed_in.T, grad_query_half)
    key_grad = matmul(normed_in.T, grad_key_half)
    value_grad = matmul(normed_in.T, grad_value_rows)
    grad_normed_in = matmul(grad_query_half, query_weight.T) + matmul(grad_key_half, key_weight.T) + matmul(grad_value_rows, value_weight.T)
    grad_in_norm, gain_one_grad = norm_bwd(residual_in, factor_one, gain_one, grad_normed_in)
    input_grad = (grad_mid + grad_in_norm).astype(jnp.bfloat16)
    grads = (gain_one_grad, query_grad, key_grad, value_grad, query_gain_grad, key_gain_grad, output_grad, gain_two_grad, gate_grad, up_grad, down_grad)
    return (block_output, input_grad, grads)

def reference(block_input, positions, cotangent, attention_gain, query_weight, key_weight, value_weight, query_gain, key_gain, output_weight, feedforward_gain, gate_weight, up_weight, down_weight):

    def one_sequence(totals, items):
        rows_in, places, cot_rows = items
        out_rows, grad_rows, grads = layer_pass(rows_in, places, cot_rows, attention_gain, query_weight, key_weight, value_weight, query_gain, key_gain, output_weight, feedforward_gain, gate_weight, up_weight, down_weight)
        return (tuple((left + right for left, right in zip(totals, grads))), (out_rows, grad_rows))
    shapes = (attention_gain.shape, query_weight.shape, key_weight.shape, value_weight.shape, query_gain.shape, key_gain.shape, output_weight.shape, feedforward_gain.shape, gate_weight.shape, up_weight.shape, down_weight.shape)
    start_totals = tuple((jnp.zeros(shape_one, jnp.float32) for shape_one in shapes))
    totals, stacked = lax.scan(one_sequence, start_totals, (block_input, positions, cotangent))
    return (stacked[0], stacked[1], totals[0], totals[1], totals[2], totals[3], totals[4], totals[5], totals[6], totals[7], totals[8], totals[9], totals[10])
```

```python
import jax
import jax.numpy as jnp
from jax import lax
from jax.sharding import PartitionSpec as P

H = 16
KV = 8
HD = 64

rope_base = 1000000.0
eps = 1e-05
masked = -1e30
f32 = jnp.float32
bf16 = jnp.bfloat16


def contract(formula, left, right):
    return jnp.einsum(formula, left, right, preferred_element_type=f32)


def matmul(left, right):
    return jnp.dot(left, right, preferred_element_type=f32)


def matmul_nt(left, right):
    return lax.dot_general(left, right, (((1,), (1,)), ((), ())), preferred_element_type=f32)


def matmul_tn(left, right):
    return lax.dot_general(left, right, (((0,), (0,)), ((), ())), preferred_element_type=f32)


def rope_tables(places, head_width):
    half_width = head_width // 2
    inverse = rope_base ** (-(jnp.arange(half_width, dtype=f32) * 2.0) / head_width)
    angles = places.astype(f32)[:, None] * inverse[None, :]
    return (jnp.cos(angles)[:, None, :], jnp.sin(angles)[:, None, :])


def head_prep(raw_rows, gain_row, cosine, sine, head_count):
    row_count = raw_rows.shape[0]
    split_rows = raw_rows.reshape(row_count, head_count, -1)
    factor = lax.rsqrt(jnp.mean(split_rows * split_rows, axis=-1, keepdims=True) + eps)
    normed = split_rows * factor * gain_row
    half_width = normed.shape[-1] // 2
    lower = normed[..., :half_width]
    upper = normed[..., half_width:]
    turned = jnp.concatenate(
        [lower * cosine - upper * sine, upper * cosine + lower * sine], axis=-1
    )
    return turned.reshape(row_count, -1)


def inv_rms(values):
    return lax.rsqrt(jnp.mean(values * values, axis=-1, keepdims=True) + eps)


def norm_bwd(values, factor, gain_row, grad_result):
    normed = values * factor
    grad_normed = grad_result * gain_row
    return factor * (
        grad_normed - normed * jnp.mean(grad_normed * normed, axis=-1, keepdims=True)
    )


def masked_scores(queries, key_rows, doc_start, begin_row, end_row, scaling):
    query_index = jnp.arange(begin_row, end_row, dtype=jnp.int32)
    key_index = jnp.arange(end_row, dtype=jnp.int32)
    allowed = (key_index[None, :] <= query_index[:, None]) & (
        key_index[None, :] >= doc_start[begin_row:end_row, None]
    )
    scores = contract("qhd,khd->hqk", queries[begin_row:end_row], key_rows[:end_row]) * scaling
    return jnp.where(allowed[None, :, :], scores, masked)


def attend_fwd(queries, key_rows, value_rows, doc_start):
    seq_length, head_count, head_width = queries.shape
    block_rows = min(512, seq_length)
    scaling = head_width ** (-0.5)
    out_blocks = []
    total_blocks = []
    for begin_row in range(0, seq_length, block_rows):
        end_row = begin_row + block_rows
        scores = masked_scores(queries, key_rows, doc_start, begin_row, end_row, scaling)
        largest = jnp.max(scores, axis=-1, keepdims=True)
        log_total = largest + jnp.log(jnp.sum(jnp.exp(scores - largest), axis=-1, keepdims=True))
        attn_prob = jnp.exp(scores - log_total).astype(bf16)
        out_blocks.append(contract("hqk,khd->qhd", attn_prob, value_rows[:end_row]).astype(bf16))
        total_blocks.append(log_total[..., 0])
    return (jnp.concatenate(out_blocks, axis=0), jnp.concatenate(total_blocks, axis=1))


def attend_bwd(queries, key_rows, value_rows, outputs, log_totals, grad_result, doc_start):
    seq_length, head_count, head_width = queries.shape
    block_rows = min(512, seq_length)
    scaling = head_width ** (-0.5)
    carried = jnp.sum(grad_result.astype(f32) * outputs.astype(f32), axis=-1).T
    grad_query = []
    grad_key = jnp.zeros((seq_length, head_count, head_width), f32)
    grad_value = jnp.zeros((seq_length, head_count, head_width), f32)
    for begin_row in range(0, seq_length, block_rows):
        end_row = begin_row + block_rows
        scores = masked_scores(queries, key_rows, doc_start, begin_row, end_row, scaling)
        attn_prob = jnp.exp(scores - log_totals[:, begin_row:end_row, None])
        prob_half = attn_prob.astype(bf16)
        grad_rows = grad_result[begin_row:end_row]
        grad_value = grad_value.at[:end_row].add(contract("hqk,qhd->khd", prob_half, grad_rows))
        grad_prob = contract("qhd,khd->hqk", grad_rows, value_rows[:end_row])
        grad_score = (
            attn_prob * (grad_prob - carried[:, begin_row:end_row, None]) * scaling
        ).astype(bf16)
        grad_query.append(contract("hqk,khd->qhd", grad_score, key_rows[:end_row]))
        grad_key = grad_key.at[:end_row].add(
            contract("hqk,qhd->khd", grad_score, queries[begin_row:end_row])
        )
    return (
        jnp.concatenate(grad_query, axis=0).astype(bf16),
        grad_key.astype(bf16),
        grad_value.astype(bf16),
    )


def swap(array, mask):
    groups = lax.axis_size("seq")
    return lax.ppermute(array, "seq", [(i, i ^ mask) for i in range(groups)])


def partner_blocks(block):
    half = block.shape[0] // 2
    got = {0: block}
    got[2] = swap(block, 2)
    got[4] = swap(block, 4)
    got[1] = swap(block, 1)
    via_x = swap(got[4][:half], 2)
    via_y = swap(got[2][half:], 4)
    got[3] = swap(got[2], 1)
    got[5] = swap(got[4], 1)
    got[6] = jnp.concatenate([via_x, via_y], axis=0)
    got[7] = swap(got[6], 1)
    return [got[j] for j in range(8)]


def gather_seq(block, axis):
    if lax.axis_size("seq") != 8 or block.shape[0] % 2:
        return lax.all_gather(block, "seq", axis=axis, tiled=True)
    me = lax.axis_index("seq")
    width = block.shape[axis]
    shape = list(block.shape)
    shape[axis] = width * 8
    whole = jnp.zeros(shape, block.dtype)
    for j, part in enumerate(partner_blocks(block)):
        whole = lax.dynamic_update_slice_in_dim(whole, part, (me ^ j) * width, axis)
    return whole


def reduce_seq(partial, axis):
    groups = lax.axis_size("seq")
    width = partial.shape[axis] // groups
    if groups != 8 or partial.shape[0] % 2:
        return lax.psum_scatter(partial, "seq", scatter_dimension=axis, tiled=True).astype(f32)
    me = lax.axis_index("seq")
    half = partial.shape[0] // 2

    def piece(j):
        return lax.dynamic_slice_in_dim(partial, (me ^ j) * width, width, axis)

    got = swap(jnp.stack([piece(j) for j in (1, 3, 5, 7)]), 1)
    held = {j: piece(j).astype(f32) + got[j // 2].astype(f32) for j in (0, 2, 4, 6)}
    first = {j: held[j][:half] for j in held}
    second = {j: held[j][half:] for j in held}
    sent_x = swap(jnp.stack([first[2].astype(bf16), first[6].astype(bf16)]), 2)
    sent_y = swap(jnp.stack([second[4].astype(bf16), second[6].astype(bf16)]), 4)
    last_y = swap((first[4] + sent_x[1].astype(f32)).astype(bf16), 4)
    last_x = swap((second[2] + sent_y[1].astype(f32)).astype(bf16), 2)
    own_first = first[0] + sent_x[0].astype(f32) + last_y.astype(f32)
    own_second = second[0] + sent_y[0].astype(f32) + last_x.astype(f32)
    return jnp.concatenate([own_first, own_second], axis=0)


def line_step(array, step):
    size = lax.axis_size("fsdp")
    return lax.ppermute(
        array, "fsdp", [(i, i + step) for i in range(size) if 0 <= i + step < size]
    )


def gather_line(block):
    size = lax.axis_size("fsdp")
    if size != 4:
        return lax.all_gather(block, "fsdp", axis=0, tiled=False)
    me = lax.axis_index("fsdp")
    below, above = [block], [block]
    for _ in range(size - 1):
        below.append(line_step(below[-1], 1))
        above.append(line_step(above[-1], -1))
    whole = jnp.zeros((size,) + block.shape, block.dtype)
    whole = lax.dynamic_update_index_in_dim(whole, block, me, 0)
    for k in range(1, size):
        part = below[k] + above[size - k]
        whole = lax.dynamic_update_index_in_dim(whole, part, lax.rem(me - k + size, size), 0)
    return whole


def reduce_line(partial):
    size = lax.axis_size("fsdp")
    if size != 4:
        return lax.psum_scatter(
            partial.astype(bf16), "fsdp", scatter_dimension=0, tiled=False
        ).astype(f32)
    me = lax.axis_index("fsdp")

    def entry(k):
        return lax.dynamic_index_in_dim(
            partial, lax.rem(me + k + size, size), 0, keepdims=False
        ).astype(f32)

    up, down = entry(size - 1), entry(1 - size)
    for k in range(size - 2, -1, -1):
        got_up = line_step(up.astype(bf16), 1).astype(f32)
        got_down = line_step(down.astype(bf16), -1).astype(f32)
        if k:
            up, down = entry(k) + got_up, entry(-k) + got_down
    return entry(0) + got_up + got_down


def spread(blocks):
    return lax.all_to_all(blocks, "seq", split_axis=0, concat_axis=0, tiled=True)


def sum_everywhere(vector):
    groups, size = lax.axis_size("seq"), lax.axis_size("fsdp")
    if groups != 8 or size != 4:
        return lax.psum(vector, ("fsdp", "seq"))
    for mask in (1, 2, 4):
        vector = vector + swap(vector, mask)
    for mask in (1, 2):
        vector = vector + lax.ppermute(vector, "fsdp", [(i, i ^ mask) for i in range(size)])
    return vector


def body(
    block_input,
    positions,
    cotangent,
    attention_gain,
    query_weight,
    key_weight,
    value_weight,
    query_gain,
    key_gain,
    output_weight,
    feedforward_gain,
    gate_weight,
    up_weight,
    down_weight,
):
    seq_count, span, width = block_input.shape
    groups = lax.axis_size("seq")
    size = lax.axis_size("fsdp")
    me = lax.axis_index("seq")
    length = span * groups
    rows = seq_count * length
    own_rows = seq_count * span
    shard = query_weight.shape[0]
    heads = H // groups
    kv_heads = max(1, KV // groups)
    copies = max(1, groups // KV)
    q_cols, k_cols = heads * HD, kv_heads * HD
    qkv_cols = q_cols + 2 * k_cols
    part = gate_weight.shape[1] // (groups * size)
    hidden_cols = part * size

    x_full = gather_seq(block_input, 1)

    def columns(weight, col_copies):
        shaped = weight.reshape(shard, -1, 1, HD)
        shaped = jnp.broadcast_to(shaped, (shard, shaped.shape[1], col_copies, HD))
        return shaped.reshape(shard, groups, -1)

    packed = jnp.concatenate(
        [
            columns(query_weight, 1),
            columns(key_weight, copies),
            columns(value_weight, copies),
        ],
        axis=2,
    ).transpose(1, 0, 2)
    gains = jnp.concatenate([attention_gain, feedforward_gain])
    gain_rows = jnp.zeros((16, qkv_cols), bf16).at[0, : 2 * shard].set(gains)
    packed = jnp.concatenate(
        [packed, jnp.broadcast_to(gain_rows[None], (groups, 16, qkv_cols))], axis=1
    )
    packed = gather_line(spread(packed))
    w_qkv = packed[:, :, :shard, :].reshape(width, qkv_cols)
    gain_one = packed[:, :, shard, :shard].reshape(width).astype(f32)
    gain_two = packed[:, :, shard, shard : 2 * shard].reshape(width).astype(f32)

    out_full = lax.all_gather(output_weight, ("fsdp", "seq"), axis=0, tiled=True)

    def ff_columns(weight):
        shaped = weight.reshape(shard, size, groups, part)
        return shaped.transpose(2, 0, 1, 3).reshape(groups, shard, hidden_cols)

    w_gate_up = gather_line(
        spread(jnp.concatenate([ff_columns(gate_weight), ff_columns(up_weight)], axis=2))
    ).reshape(width, 2 * hidden_cols)
    w_gate = w_gate_up[:, :hidden_cols]
    w_up = w_gate_up[:, hidden_cols:]
    w_down = gather_line(down_weight).reshape(hidden_cols, width)

    cot_full = gather_seq(cotangent, 1).reshape(rows, width)

    residual_in = x_full.reshape(rows, width).astype(f32)
    factor_one = inv_rms(residual_in)
    normed_in = (residual_in * factor_one * gain_one).astype(bf16)
    qkv_raw = matmul(normed_in, w_qkv)
    query_raw = qkv_raw[:, :q_cols]
    key_raw = qkv_raw[:, q_cols : q_cols + k_cols]
    value_rows = qkv_raw[:, q_cols + k_cols :].astype(bf16)
    cosine, sine = rope_tables(positions.reshape(rows), HD)
    query_scale = query_gain.astype(f32)
    key_scale = key_gain.astype(f32)

    def query_side(raw_rows, gain_row):
        return head_prep(raw_rows, gain_row, cosine, sine, heads)

    def key_side(raw_rows, gain_row):
        return head_prep(raw_rows, gain_row, cosine, sine, kv_heads)

    def head_view(packed_rows):
        shaped = packed_rows.reshape(seq_count, length, -1, HD)
        return jnp.repeat(shaped, heads // shaped.shape[2], axis=2)

    queries = query_side(query_raw, query_scale).astype(bf16).reshape(seq_count, length, heads, HD)
    keys = head_view(key_side(key_raw, key_scale).astype(bf16))
    values = head_view(value_rows)
    doc_start = jnp.arange(length, dtype=jnp.int32)[None, :] - positions
    outputs, log_totals = jax.vmap(attend_fwd)(queries, keys, values, doc_start)

    attn_full = gather_seq(outputs.reshape(seq_count, length, q_cols), 2)
    attn_rows = attn_full.reshape(rows, width)
    residual_mid = residual_in + matmul(attn_rows, out_full)
    factor_two = inv_rms(residual_mid)
    normed_mid = (residual_mid * factor_two * gain_two).astype(bf16)

    def own(array):
        shaped = array.reshape(seq_count, length, -1)
        return lax.dynamic_slice_in_dim(shaped, me * span, span, 1).reshape(own_rows, -1)

    gate_rows = matmul(normed_mid, w_gate)
    up_rows = matmul(normed_mid, w_up)
    sigma = jax.nn.sigmoid(gate_rows)
    hidden = (gate_rows * sigma * up_rows).astype(bf16)
    grad_hidden = matmul_nt(cot_full, w_down)
    grad_gate = (grad_hidden * up_rows * sigma * (1.0 + gate_rows * (1.0 - sigma))).astype(bf16)
    grad_up = (grad_hidden * gate_rows * sigma).astype(bf16)
    grad_normed_part = (matmul_nt(grad_gate, w_gate) + matmul_nt(grad_up, w_up)).astype(bf16)
    grad_normed_mid = reduce_seq(grad_normed_part.reshape(seq_count, length, width), 1)
    grad_normed_mid = grad_normed_mid.reshape(own_rows, width)

    residual_own = own(residual_mid)
    cot_rows = cotangent.reshape(own_rows, width).astype(f32)
    grad_mid = cot_rows + norm_bwd(residual_own, own(factor_two), gain_two, grad_normed_mid)
    grad_mid_half = grad_mid.astype(bf16)
    grad_attn_out = matmul_nt(grad_mid_half, out_full).astype(bf16)
    grad_heads = lax.all_to_all(
        grad_attn_out.reshape(seq_count, span, width), "seq", split_axis=2, concat_axis=1, tiled=True
    )

    grad_query_heads, grad_key_heads, grad_value_heads = jax.vmap(attend_bwd)(
        queries,
        keys,
        values,
        outputs,
        log_totals,
        grad_heads.reshape(seq_count, length, heads, HD),
        doc_start,
    )

    def fold(packed_rows):
        shaped = packed_rows.reshape(rows, kv_heads, -1, HD).astype(f32)
        return jnp.sum(shaped, axis=2).reshape(rows, k_cols)

    _, query_back = jax.vjp(query_side, query_raw, query_scale)
    grad_query_raw, query_gain_term = query_back(grad_query_heads.reshape(rows, q_cols).astype(f32))
    _, key_back = jax.vjp(key_side, key_raw, key_scale)
    grad_key_raw, key_gain_term = key_back(fold(grad_key_heads))
    grad_qkv = jnp.concatenate(
        [
            grad_query_raw.astype(bf16),
            grad_key_raw.astype(bf16),
            fold(grad_value_heads).astype(bf16),
        ],
        axis=1,
    )
    grad_in_part = matmul_nt(grad_qkv, w_qkv).astype(bf16)
    grad_normed_in = reduce_seq(grad_in_part.reshape(seq_count, length, width), 1)
    grad_normed_in = grad_normed_in.reshape(own_rows, width)
    own_in = block_input.reshape(own_rows, width).astype(f32)
    input_grad = (
        (grad_mid + norm_bwd(own_in, inv_rms(own_in), gain_one, grad_normed_in))
        .astype(bf16)
        .reshape(seq_count, span, width)
    )

    result_part = matmul(hidden, w_down).astype(bf16).reshape(seq_count, length, width)
    block_output = (
        (residual_own + reduce_seq(result_part, 1).reshape(own_rows, width))
        .astype(bf16)
        .reshape(seq_count, span, width)
    )

    down_grad = reduce_line(matmul_tn(hidden, cot_full).reshape(size, part, width))
    gate_up_term = matmul_tn(normed_mid, jnp.concatenate([grad_gate, grad_up], axis=1))
    gate_up_term = reduce_line(gate_up_term.reshape(size, groups * shard, 2 * hidden_cols))
    gate_up_home = spread(gate_up_term.astype(bf16).reshape(groups, shard, 2 * hidden_cols))

    def ff_home(columns_home):
        shaped = columns_home.astype(f32).reshape(groups, shard, size, part)
        return shaped.transpose(1, 2, 0, 3).reshape(shard, groups * size * part)

    gate_grad = ff_home(gate_up_home[:, :, :hidden_cols])
    up_grad = ff_home(gate_up_home[:, :, hidden_cols:])

    output_term = matmul_tn(own(attn_rows), grad_mid_half).astype(bf16)
    output_grad = lax.psum_scatter(
        output_term, ("fsdp", "seq"), scatter_dimension=0, tiled=True
    ).astype(f32)

    qkv_term = reduce_line(matmul_tn(normed_in, grad_qkv).reshape(size, groups * shard, qkv_cols))
    qkv_home = spread(qkv_term.astype(bf16).reshape(groups, shard, qkv_cols)).astype(f32)

    def home(block, col_copies):
        shaped = block.transpose(1, 0, 2).reshape(shard, -1, col_copies, HD)
        return jnp.sum(shaped, axis=2).reshape(shard, -1)

    query_grad = home(qkv_home[:, :, :q_cols], 1)
    key_grad = home(qkv_home[:, :, q_cols : q_cols + k_cols], copies)
    value_grad = home(qkv_home[:, :, q_cols + k_cols :], copies)

    def weighted(weight, grad):
        return jnp.sum(weight.astype(f32) * grad, axis=1)

    gain_one_grad = (
        weighted(query_weight, query_grad)
        + weighted(key_weight, key_grad)
        + weighted(value_weight, value_grad)
    ) / attention_gain.astype(f32)
    gain_two_grad = (
        weighted(gate_weight, gate_grad) + weighted(up_weight, up_grad)
    ) / feedforward_gain.astype(f32)

    head_gains = sum_everywhere(jnp.concatenate([query_gain_term, key_gain_term])[None])[0]
    return (
        block_output,
        input_grad,
        gain_one_grad,
        query_grad,
        key_grad,
        value_grad,
        head_gains[:HD],
        head_gains[HD:],
        output_grad,
        gain_two_grad,
        gate_grad,
        up_grad,
        down_grad,
    )


def solution(mesh):
    shards = P(("fsdp", "seq"), None)
    vector = P(("fsdp", "seq"))
    tokens = P("fsdp", "seq", None)
    return jax.shard_map(
        body,
        mesh=mesh,
        in_specs=(
            tokens,
            P("fsdp", None),
            tokens,
            vector,
            shards,
            shards,
            shards,
            P(),
            P(),
            shards,
            vector,
            shards,
            shards,
            shards,
        ),
        out_specs=(
            tokens,
            tokens,
            vector,
            shards,
            shards,
            shards,
            P(),
            P(),
            shards,
            vector,
            shards,
            shards,
            shards,
        ),
        check_vma=False,
    )
```

```python
import functools

import jax
import jax.numpy as jnp
from jax import lax
from jax.experimental import pallas as pl
from jax.experimental.pallas import tpu as pltpu
from jax.sharding import PartitionSpec as P

H = 16
KV = 8
HD = 64

rope_base = 1000000.0
eps = 1e-05
masked = -1e30
f32 = jnp.float32
bf16 = jnp.bfloat16


def contract(formula, left, right):
    return jnp.einsum(formula, left, right, preferred_element_type=f32)


def matmul(left, right):
    return jnp.dot(left, right, preferred_element_type=f32)


def matmul_nt(left, right):
    return lax.dot_general(left, right, (((1,), (1,)), ((), ())), preferred_element_type=f32)


def matmul_tn(left, right):
    return lax.dot_general(left, right, (((0,), (0,)), ((), ())), preferred_element_type=f32)


def rope_tables(places, head_width):
    half_width = head_width // 2
    inverse = rope_base ** (-(jnp.arange(half_width, dtype=f32) * 2.0) / head_width)
    angles = places.astype(f32)[:, None] * inverse[None, :]
    return (jnp.cos(angles)[:, None, :], jnp.sin(angles)[:, None, :])


def head_prep(raw_rows, gain_row, cosine, sine, head_count):
    row_count = raw_rows.shape[0]
    split_rows = raw_rows.reshape(row_count, head_count, -1)
    factor = lax.rsqrt(jnp.mean(split_rows * split_rows, axis=-1, keepdims=True) + eps)
    normed = split_rows * factor * gain_row
    half_width = normed.shape[-1] // 2
    lower = normed[..., :half_width]
    upper = normed[..., half_width:]
    turned = jnp.concatenate(
        [lower * cosine - upper * sine, upper * cosine + lower * sine], axis=-1
    )
    return turned.reshape(row_count, -1)


def inv_rms(values):
    return lax.rsqrt(jnp.mean(values * values, axis=-1, keepdims=True) + eps)


def norm_bwd(values, factor, gain_row, grad_result):
    normed = values * factor
    grad_normed = grad_result * gain_row
    return factor * (
        grad_normed - normed * jnp.mean(grad_normed * normed, axis=-1, keepdims=True)
    )


def masked_scores(queries, key_rows, doc_start, begin_row, end_row, scaling):
    query_index = jnp.arange(begin_row, end_row, dtype=jnp.int32)
    key_index = jnp.arange(end_row, dtype=jnp.int32)
    allowed = (key_index[None, :] <= query_index[:, None]) & (
        key_index[None, :] >= doc_start[begin_row:end_row, None]
    )
    scores = contract("qhd,khd->hqk", queries[begin_row:end_row], key_rows[:end_row]) * scaling
    return jnp.where(allowed[None, :, :], scores, masked)


def attend_fwd(queries, key_rows, value_rows, doc_start):
    seq_length, head_count, head_width = queries.shape
    block_rows = min(512, seq_length)
    scaling = head_width ** (-0.5)
    out_blocks = []
    total_blocks = []
    for begin_row in range(0, seq_length, block_rows):
        end_row = begin_row + block_rows
        scores = masked_scores(queries, key_rows, doc_start, begin_row, end_row, scaling)
        largest = jnp.max(scores, axis=-1, keepdims=True)
        log_total = largest + jnp.log(jnp.sum(jnp.exp(scores - largest), axis=-1, keepdims=True))
        attn_prob = jnp.exp(scores - log_total).astype(bf16)
        out_blocks.append(contract("hqk,khd->qhd", attn_prob, value_rows[:end_row]).astype(bf16))
        total_blocks.append(log_total[..., 0])
    return (jnp.concatenate(out_blocks, axis=0), jnp.concatenate(total_blocks, axis=1))


def attend_bwd(queries, key_rows, value_rows, outputs, log_totals, grad_result, doc_start):
    seq_length, head_count, head_width = queries.shape
    block_rows = min(512, seq_length)
    scaling = head_width ** (-0.5)
    carried = jnp.sum(grad_result.astype(f32) * outputs.astype(f32), axis=-1).T
    grad_query = []
    grad_key = jnp.zeros((seq_length, head_count, head_width), f32)
    grad_value = jnp.zeros((seq_length, head_count, head_width), f32)
    for begin_row in range(0, seq_length, block_rows):
        end_row = begin_row + block_rows
        scores = masked_scores(queries, key_rows, doc_start, begin_row, end_row, scaling)
        attn_prob = jnp.exp(scores - log_totals[:, begin_row:end_row, None])
        prob_half = attn_prob.astype(bf16)
        grad_rows = grad_result[begin_row:end_row]
        grad_value = grad_value.at[:end_row].add(contract("hqk,qhd->khd", prob_half, grad_rows))
        grad_prob = contract("qhd,khd->hqk", grad_rows, value_rows[:end_row])
        grad_score = (
            attn_prob * (grad_prob - carried[:, begin_row:end_row, None]) * scaling
        ).astype(bf16)
        grad_query.append(contract("hqk,khd->qhd", grad_score, key_rows[:end_row]))
        grad_key = grad_key.at[:end_row].add(
            contract("hqk,qhd->khd", grad_score, queries[begin_row:end_row])
        )
    return (
        jnp.concatenate(grad_query, axis=0).astype(bf16),
        grad_key.astype(bf16),
        grad_value.astype(bf16),
    )


def swap(array, mask):
    groups = lax.axis_size("seq")
    return lax.ppermute(array, "seq", [(i, i ^ mask) for i in range(groups)])


def partner_blocks(block):
    half = block.shape[0] // 2
    got = {0: block}
    got[2] = swap(block, 2)
    got[4] = swap(block, 4)
    got[1] = swap(block, 1)
    via_x = swap(got[4][:half], 2)
    via_y = swap(got[2][half:], 4)
    got[3] = swap(got[2], 1)
    got[5] = swap(got[4], 1)
    got[6] = jnp.concatenate([via_x, via_y], axis=0)
    got[7] = swap(got[6], 1)
    return [got[j] for j in range(8)]


def gather_seq(block, axis):
    if lax.axis_size("seq") != 8 or block.shape[0] % 2:
        return lax.all_gather(block, "seq", axis=axis, tiled=True)
    me = lax.axis_index("seq")
    width = block.shape[axis]
    shape = list(block.shape)
    shape[axis] = width * 8
    whole = jnp.zeros(shape, block.dtype)
    for j, part in enumerate(partner_blocks(block)):
        whole = lax.dynamic_update_slice_in_dim(whole, part, (me ^ j) * width, axis)
    return whole


def reduce_seq(partial, axis):
    groups = lax.axis_size("seq")
    width = partial.shape[axis] // groups
    if groups != 8 or partial.shape[0] % 2:
        return lax.psum_scatter(partial, "seq", scatter_dimension=axis, tiled=True).astype(f32)
    me = lax.axis_index("seq")
    half = partial.shape[0] // 2

    def piece(j):
        return lax.dynamic_slice_in_dim(partial, (me ^ j) * width, width, axis)

    got = swap(jnp.stack([piece(j) for j in (1, 3, 5, 7)]), 1)
    held = {j: piece(j).astype(f32) + got[j // 2].astype(f32) for j in (0, 2, 4, 6)}
    first = {j: held[j][:half] for j in held}
    second = {j: held[j][half:] for j in held}
    sent_x = swap(jnp.stack([first[2].astype(bf16), first[6].astype(bf16)]), 2)
    sent_y = swap(jnp.stack([second[4].astype(bf16), second[6].astype(bf16)]), 4)
    last_y = swap((first[4] + sent_x[1].astype(f32)).astype(bf16), 4)
    last_x = swap((second[2] + sent_y[1].astype(f32)).astype(bf16), 2)
    own_first = first[0] + sent_x[0].astype(f32) + last_y.astype(f32)
    own_second = second[0] + sent_y[0].astype(f32) + last_x.astype(f32)
    return jnp.concatenate([own_first, own_second], axis=0)


def line_step(array, step):
    size = lax.axis_size("fsdp")
    return lax.ppermute(
        array, "fsdp", [(i, i + step) for i in range(size) if 0 <= i + step < size]
    )


def gather_line(block):
    size = lax.axis_size("fsdp")
    if size != 4:
        return lax.all_gather(block, "fsdp", axis=0, tiled=False)
    me = lax.axis_index("fsdp")
    below, above = [block], [block]
    for _ in range(size - 1):
        below.append(line_step(below[-1], 1))
        above.append(line_step(above[-1], -1))
    whole = jnp.zeros((size,) + block.shape, block.dtype)
    whole = lax.dynamic_update_index_in_dim(whole, block, me, 0)
    for k in range(1, size):
        part = below[k] + above[size - k]
        whole = lax.dynamic_update_index_in_dim(whole, part, lax.rem(me - k + size, size), 0)
    return whole


def reduce_line(partial):
    size = lax.axis_size("fsdp")
    if size != 4:
        return lax.psum_scatter(
            partial.astype(bf16), "fsdp", scatter_dimension=0, tiled=False
        ).astype(f32)
    me = lax.axis_index("fsdp")

    def entry(k):
        return lax.dynamic_index_in_dim(
            partial, lax.rem(me + k + size, size), 0, keepdims=False
        ).astype(f32)

    up, down = entry(size - 1), entry(1 - size)
    for k in range(size - 2, -1, -1):
        got_up = line_step(up.astype(bf16), 1).astype(f32)
        got_down = line_step(down.astype(bf16), -1).astype(f32)
        if k:
            up, down = entry(k) + got_up, entry(-k) + got_down
    return entry(0) + got_up + got_down


def spread(blocks):
    return lax.all_to_all(blocks, "seq", split_axis=0, concat_axis=0, tiled=True)


def sum_everywhere(vector):
    groups, size = lax.axis_size("seq"), lax.axis_size("fsdp")
    if groups != 8 or size != 4:
        return lax.psum(vector, ("fsdp", "seq"))
    for mask in (1, 2, 4):
        vector = vector + swap(vector, mask)
    for mask in (1, 2):
        vector = vector + lax.ppermute(vector, "fsdp", [(i, i ^ mask) for i in range(size)])
    return vector


exact = lax.Precision.HIGHEST


def dot_nt(left, right, precision=None):
    return lax.dot_general(left, right, (((1,), (1,)), ((), ())), precision=precision, preferred_element_type=f32)


def dot_tn(left, right):
    return lax.dot_general(left, right, (((0,), (0,)), ((), ())), preferred_element_type=f32)


def head_mean():
    row = lax.broadcasted_iota(jnp.int32, (128, 128), 0) // HD
    col = lax.broadcasted_iota(jnp.int32, (128, 128), 1) // HD
    return jnp.where(row == col, 1.0 / HD, 0.0).astype(f32)


def lane_index(rows):
    return lax.broadcasted_iota(jnp.int32, (rows, 128), 1)


def half_turn(array, back):
    low = (lane_index(array.shape[0]) % HD) < HD // 2
    ahead = pltpu.roll(array, 128 - HD // 2, 1)
    behind = pltpu.roll(array, HD // 2, 1)
    return jnp.where(low, ahead, -behind) if back else jnp.where(low, -ahead, behind)


def attn_fwd_kernel(block, q_ref, kv_ref, start_ref, out_ref, lse_ref):
    step = pl.program_id(1)
    steps = kv_ref.shape[1] // block
    lanes = lane_index(block)

    for at in range(steps):
        end = (at + 1) * block

        @pl.when(step == at)
        def _(at=at, end=end):
            k = kv_ref[0, :end, :HD]
            v = kv_ref[0, :end, HD:]
            q_index = at * block + lax.broadcasted_iota(jnp.int32, (block, end), 0)
            k_index = lax.broadcasted_iota(jnp.int32, (block, end), 1)
            allowed = (k_index <= q_index) & (k_index >= start_ref[0][:, :1])
            outs, totals = [], []
            for head in range(2):
                q = q_ref[0, :, head * HD : (head + 1) * HD] * jnp.array(HD ** -0.5, bf16)
                scores = jnp.where(allowed, dot_nt(q, k), masked)
                largest = jnp.max(scores, axis=-1, keepdims=True)
                weights = jnp.exp(scores - largest)
                total = jnp.sum(weights, axis=-1, keepdims=True)
                out = jnp.dot(weights.astype(bf16), v, preferred_element_type=f32) / total
                outs.append(out.astype(bf16))
                totals.append(largest + jnp.log(total))
            out_ref[0] = jnp.concatenate(outs, axis=1)
            lse_ref[0] = jnp.where(lanes < HD, totals[0], totals[1])


def attn_fwd(q, kv, starts, span):
    seqs, length, _ = q.shape
    block = 2 * span
    rows = lambda b, i: (b, i, 0)
    whole = lambda b, i: (b, 0, 0)
    return pl.pallas_call(
        functools.partial(attn_fwd_kernel, block),
        grid=(seqs, length // block),
        in_specs=[
            pl.BlockSpec((1, block, 128), rows),
            pl.BlockSpec((1, length, 128), whole),
            pl.BlockSpec((1, block, 128), rows),
        ],
        out_specs=[pl.BlockSpec((1, block, 128), rows), pl.BlockSpec((1, block, 128), rows)],
        out_shape=[
            jax.ShapeDtypeStruct((seqs, length, 128), bf16),
            jax.ShapeDtypeStruct((seqs, length, 128), f32),
        ],
        compiler_params=pltpu.CompilerParams(vmem_limit_bytes=48 << 20),
        cost_estimate=pl.CostEstimate(flops=seqs * length * length * 256, bytes_accessed=seqs * length * 1792, transcendentals=seqs * length * length),
        name="attn_fwd",
    )(q, kv, starts)


def attn_bwd_kernel(block, q_ref, kv_ref, do_ref, o_ref, lse_ref, start_ref, *refs):
    dq_ref, dkv_ref, dk_acc, dv_acc = refs[-4:]
    step = pl.program_id(1)
    steps = kv_ref.shape[1] // block

    @pl.when(step == 0)
    def _():
        dk_acc[...] = jnp.zeros_like(dk_acc)
        dv_acc[...] = jnp.zeros_like(dv_acc)

    for at in range(steps):
        end = (at + 1) * block

        @pl.when(step == at)
        def _(at=at, end=end):
            k = kv_ref[0, :end, :HD]
            v = kv_ref[0, :end, HD:]
            k_index = lax.broadcasted_iota(jnp.int32, (end, block), 0)
            q_index = at * block + lax.broadcasted_iota(jnp.int32, (end, block), 1)
            allowed = (k_index <= q_index) & (k_index >= start_ref[0, 0:1, :])
            do_rows = do_ref[...].reshape(block, 128)
            product = do_rows.astype(f32) * o_ref[0].astype(f32)
            dqs = []
            for head in range(2):
                cut = slice(head * HD, (head + 1) * HD)
                q = q_ref[0, :, cut] * jnp.array(HD ** -0.5, bf16)
                do = do_rows[:, cut]
                delta = dot_nt(jnp.ones((8, HD), f32), product[:, cut], exact)[0:1, :]
                scores = jnp.where(allowed, dot_nt(k, q), masked)
                prob = jnp.exp(scores - lse_ref[0, head : head + 1, :])
                dv_acc[:end, :] += jnp.dot(prob.astype(bf16), do, preferred_element_type=f32)
                dscore = (prob * (dot_nt(v, do) - delta)).astype(bf16)
                dk_acc[:end, :] += jnp.dot(dscore, q, preferred_element_type=f32)
                dqs.append(dot_tn(dscore, k) * (HD ** -0.5))
            dq_ref[0] = jnp.concatenate(dqs, axis=1)

    @pl.when(step == steps - 1)
    def _():
        dkv_ref[0] = jnp.concatenate([dk_acc[...], dv_acc[...]], axis=1)


def attn_bwd(q, kv, do, out, lse, starts, span, earlier):
    seqs, length, _ = q.shape
    block = 2 * span
    rows = lambda b, i: (b, i, 0)
    cols = lambda b, i: (b, 0, i)
    whole = lambda b, i: (b, 0, 0)
    return pl.pallas_call(
        functools.partial(attn_bwd_kernel, block),
        grid=(seqs, length // block),
        in_specs=[
            pl.BlockSpec((1, block, 128), rows),
            pl.BlockSpec((1, length, 128), whole),
            pl.BlockSpec((2, 1, span, 128), lambda b, i: (i, b, 0, 0)),
            pl.BlockSpec((1, block, 128), rows),
            pl.BlockSpec((1, 8, block), cols),
            pl.BlockSpec((1, 8, block), cols),
        ]
        + [pl.BlockSpec(memory_space=pl.ANY)] * len(earlier),
        out_specs=[pl.BlockSpec((1, block, 128), rows), pl.BlockSpec((1, length, 128), whole)],
        out_shape=[
            jax.ShapeDtypeStruct((seqs, length, 128), f32),
            jax.ShapeDtypeStruct((seqs, length, 128), f32),
        ],
        scratch_shapes=[pltpu.VMEM((length, HD), f32), pltpu.VMEM((length, HD), f32)],
        compiler_params=pltpu.CompilerParams(vmem_limit_bytes=56 << 20),
        cost_estimate=pl.CostEstimate(flops=seqs * length * length * 640, bytes_accessed=seqs * length * 2560, transcendentals=seqs * length * length),
        name="attn_bwd",
    )(q, kv, do, out, lse, starts, *earlier)


def any_space(count):
    return [pl.BlockSpec(memory_space=pl.ANY)] * count


def pack_kernel(groups, part, gate_ref, up_ref, out_ref):
    size = gate_ref.shape[1] // (groups * part)
    for at, ref in ((0, gate_ref), (size * part, up_ref)):
        whole = ref[...].astype(f32)
        for g in range(groups):
            cuts = [whole[:, (f * groups + g) * part : (f * groups + g + 1) * part] for f in range(size)]
            out_ref[g, :, at : at + size * part] = jnp.concatenate(cuts, axis=1).astype(bf16)


def pack_columns(gate, up, groups, part):
    shard, total = gate.shape
    return pl.pallas_call(
        functools.partial(pack_kernel, groups, part),
        out_shape=jax.ShapeDtypeStruct((groups, shard, 2 * total // groups), bf16),
        name="pack",
    )(gate, up)


def unpack_kernel(part, home_ref, gate_w_ref, up_w_ref, gate_ref, up_ref, sum_ref):
    groups, _, shard, hidden = home_ref.shape
    size = hidden // part
    for which, ref in ((0, gate_ref), (1, up_ref)):
        rows = [home_ref[g, which].astype(f32) for g in range(groups)]
        cuts = [rows[g][:, f * part : (f + 1) * part] for f in range(size) for g in range(groups)]
        ref[...] = jnp.concatenate(cuts, axis=1)
    total = jnp.sum(gate_w_ref[...].astype(f32) * gate_ref[...], axis=1, keepdims=True)
    total += jnp.sum(up_w_ref[...].astype(f32) * up_ref[...], axis=1, keepdims=True)
    sum_ref[...] = jnp.broadcast_to(total, sum_ref.shape)


def unpack_columns(home, gate_w, up_w, part):
    shape = gate_w.shape
    return pl.pallas_call(
        functools.partial(unpack_kernel, part),
        out_shape=[
            jax.ShapeDtypeStruct(shape, f32),
            jax.ShapeDtypeStruct(shape, f32),
            jax.ShapeDtypeStruct((shape[0], 128), f32),
        ],
        name="unpack",
    )(home, gate_w, up_w)


def unpack_heads_kernel(home_ref, q_w_ref, k_w_ref, v_w_ref, q_ref, k_ref, v_ref, sum_ref):
    blocks = [home_ref[g].astype(f32) for g in range(home_ref.shape[0])]
    q_ref[...] = jnp.concatenate([block[:, : 2 * HD] for block in blocks], axis=1)
    k_ref[...] = jnp.concatenate([block[:, 2 * HD : 3 * HD] for block in blocks], axis=1)
    v_ref[...] = jnp.concatenate([block[:, 3 * HD :] for block in blocks], axis=1)
    total = 0.0
    for weight, grad in ((q_w_ref, q_ref), (k_w_ref, k_ref), (v_w_ref, v_ref)):
        total += jnp.sum(weight[...].astype(f32) * grad[...], axis=1, keepdims=True)
    sum_ref[...] = jnp.broadcast_to(total, sum_ref.shape)


def unpack_heads(home, q_w, k_w, v_w):
    return pl.pallas_call(
        unpack_heads_kernel,
        out_shape=[jax.ShapeDtypeStruct(w.shape, f32) for w in (q_w, k_w, v_w)]
        + [jax.ShapeDtypeStruct((q_w.shape[0], 128), f32)],
        name="unpack_heads",
    )(home, q_w, k_w, v_w)


def qkv_fwd_kernel(at_ref, *refs):
    x_refs, w_refs = refs[:8], refs[8:12]
    gain_ref, scale_ref, cos_ref, sin_ref, x_out, nm_ref, raw_ref, q_ref, kv_ref, w_ref = refs[12:]
    step = pl.program_id(0)
    shard = w_ref.shape[0] // 32

    @pl.when(step == 0)
    def _():
        for m in range(4):
            for g in range(8):
                row = pl.multiple_of(((at_ref[1] ^ m) * 8 + g) * shard, shard)
                w_ref[pl.ds(row, shard), :] = w_refs[m][g, :shard, :]

    for j in range(8):

        @pl.when(step == j)
        def _(j=j):
            x_out[...] = x_refs[j][...]

    x = x_out[...].reshape(-1, x_out.shape[-1]).astype(f32)
    factor = lax.rsqrt(jnp.mean(x * x, axis=-1, keepdims=True) + eps)
    nm = (x * factor * gain_ref[...]).astype(bf16)
    nm_ref[...] = nm.reshape(nm_ref.shape)
    raw = jnp.dot(nm, w_ref[...], preferred_element_type=f32)
    raw_ref[...] = raw.reshape(raw_ref.shape)
    cos = cos_ref[...].reshape(-1, 128)
    sin = sin_ref[...].reshape(-1, 128)
    mean = head_mean()

    def prepared(part, scale):
        inv = lax.rsqrt(jnp.dot(part * part, mean, precision=exact, preferred_element_type=f32) + eps)
        normed = part * inv * scale
        return normed * cos + half_turn(normed, False) * sin

    q = prepared(raw[:, :128], scale_ref[0:1, :])
    kv = prepared(raw[:, 128:], scale_ref[1:2, :])
    kv = jnp.where(lane_index(kv.shape[0]) < HD, kv, raw[:, 128:])
    q_ref[...] = q.astype(bf16).reshape(q_ref.shape)
    kv_ref[...] = kv.astype(bf16).reshape(kv_ref.shape)


def qkv_fwd(at, x_blocks, w_blocks, gain, scales, cosine, sine, earlier):
    seqs, span, width = x_blocks[0].shape
    length = 8 * span
    home = lambda j, m: (0, m[0] ^ j, 0)
    fixed = lambda j, m: (0, 0)
    once = dict(pipeline_mode=pl.Buffered(1))

    def kernel(at_ref, *refs):
        qkv_fwd_kernel(at_ref, *refs[:16], *refs[16 + len(earlier) :])

    return pl.pallas_call(
        kernel,
        grid_spec=pltpu.PrefetchScalarGridSpec(
            num_scalar_prefetch=1,
            grid=(8,),
            in_specs=[pl.BlockSpec((seqs, span, width), lambda j, m: (0, 0, 0), **once)] * 8
            + [pl.BlockSpec(w_blocks[0].shape, lambda j, m: (0, 0, 0), **once)] * 4
            + [
                pl.BlockSpec((1, width), fixed, **once),
                pl.BlockSpec((8, 128), fixed, **once),
                pl.BlockSpec((seqs, span, 128), home),
                pl.BlockSpec((seqs, span, 128), home),
            ]
            + any_space(len(earlier)),
            out_specs=[
                pl.BlockSpec((seqs, span, width), home),
                pl.BlockSpec((seqs, span, width), home),
                pl.BlockSpec((seqs, span, 256), home),
                pl.BlockSpec((seqs, span, 128), home),
                pl.BlockSpec((seqs, span, 128), home),
                pl.BlockSpec((width, 256), fixed),
            ],
        ),
        out_shape=[
            jax.ShapeDtypeStruct((seqs, length, width), bf16),
            jax.ShapeDtypeStruct((seqs, length, width), bf16),
            jax.ShapeDtypeStruct((seqs, length, 256), f32),
            jax.ShapeDtypeStruct((seqs, length, 128), bf16),
            jax.ShapeDtypeStruct((seqs, length, 128), bf16),
            jax.ShapeDtypeStruct((width, 256), bf16),
        ],
        compiler_params=pltpu.CompilerParams(vmem_limit_bytes=40 << 20),
        cost_estimate=pl.CostEstimate(flops=16 * seqs * length * width * 256, bytes_accessed=seqs * length * width * 6, transcendentals=0),
        name="qkv_fwd",
    )(at, *x_blocks, *w_blocks, gain, scales, cosine, sine, *earlier)


def halves_spec(seqs, span, width):
    return pl.BlockSpec((1, seqs, span, width), lambda t, m: ((m[0] ^ t) >> 1, 0, 0, 0))


def store_halves(me, step, value, even_ref, odd_ref):
    odd = ((me ^ step) & 1) == 1

    @pl.when(odd)
    def _():
        odd_ref[...] = value.reshape(odd_ref.shape)

    @pl.when(jnp.logical_not(odd))
    def _():
        even_ref[...] = value.reshape(even_ref.shape)


def ffn_kernel(hidden, padded, at_ref, *refs):
    parts, wgu_refs, wd_refs = refs[:8], refs[8:12], refs[12:16]
    (x_ref, cot_ref, wo_ref, gain_ref, attn_ref, mid_ref, nm_ref, hid_ref, grads_ref) = refs[16:25]
    gnm_even, gnm_odd, out_even, out_odd, wgu, wd = refs[25:]
    step = pl.program_id(0)

    @pl.when(step == 0)
    def _():
        rows = wgu.shape[0] // 4
        part = hidden // 4
        wgu[...] = jnp.zeros_like(wgu)
        wd[hidden:, :] = jnp.zeros((padded - hidden, wd.shape[1]), bf16)
        for m in range(4):
            from_f = at_ref[1] ^ m
            block = wgu_refs[m][...].reshape(rows, 2 * hidden)
            at = pl.ds(pl.multiple_of(from_f * rows, rows), rows)
            wgu[at, :hidden] = block[:, :hidden]
            wgu[at, padded : padded + hidden] = block[:, hidden:]
            wd[pl.ds(pl.multiple_of(from_f * part, 16), part), :] = wd_refs[m][...]

    tile = attn_ref.shape[0] * attn_ref.shape[1]
    width = wo_ref.shape[0]
    for j in range(8):
        at = pl.multiple_of((at_ref[0] ^ j) * 128, 128)
        attn_ref[:, :, pl.ds(at, 128)] = parts[j][...]
    attn = attn_ref[...].reshape(tile, width)
    mid = x_ref[...].reshape(tile, width).astype(f32) + jnp.dot(attn, wo_ref[...], preferred_element_type=f32)
    mid_ref[...] = mid.reshape(mid_ref.shape)
    factor = lax.rsqrt(jnp.mean(mid * mid, axis=-1, keepdims=True) + eps)
    nm = (mid * factor * gain_ref[...]).astype(bf16)
    nm_ref[...] = nm.reshape(nm_ref.shape)
    both = jnp.dot(nm, wgu[...], preferred_element_type=f32)
    gate, up = both[:, :padded], both[:, padded:]
    sigma = jax.nn.sigmoid(gate)
    hid = (gate * sigma * up).astype(bf16)
    hid_ref[...] = hid.reshape(hid_ref.shape)
    grad_hidden = dot_nt(cot_ref[...].reshape(tile, width), wd[...])
    grad_gate = (grad_hidden * up * sigma * (1.0 + gate * (1.0 - sigma))).astype(bf16)
    grad_up = (grad_hidden * gate * sigma).astype(bf16)
    grads = jnp.concatenate([grad_gate, grad_up], axis=1)
    grads_ref[...] = grads.reshape(grads_ref.shape)
    store_halves(at_ref[0], step, dot_nt(grads, wgu[...]).astype(bf16), gnm_even, gnm_odd)
    out = jnp.dot(hid, wd[...], preferred_element_type=f32).astype(bf16)
    store_halves(at_ref[0], step, out, out_even, out_odd)


def ffn(at, parts, wgu_blocks, wd_blocks, x, cot, w_out, gain):
    seqs, length, width = x.shape
    span = length // 8
    hidden = 4 * wd_blocks[0].shape[0]
    padded = -(-hidden // 128) * 128
    home = lambda t, m: (0, t, 0)
    fixed = lambda t, m: (0, 0)
    once = dict(pipeline_mode=pl.Buffered(1))
    tokens = lambda cols: pl.BlockSpec((seqs, span, cols), home)
    shape = lambda cols, kind: jax.ShapeDtypeStruct((seqs, length, cols), kind)
    half = jax.ShapeDtypeStruct((4, seqs, span, width), bf16)
    return pl.pallas_call(
        functools.partial(ffn_kernel, hidden, padded),
        grid_spec=pltpu.PrefetchScalarGridSpec(
            num_scalar_prefetch=1,
            grid=(8,),
            in_specs=[tokens(128)] * 8
            + [pl.BlockSpec(wgu_blocks[0].shape, lambda t, m: (0, 0, 0), **once)] * 4
            + [pl.BlockSpec(wd_blocks[0].shape, fixed, **once)] * 4
            + [
                tokens(width),
                tokens(width),
                pl.BlockSpec((width, width), fixed, **once),
                pl.BlockSpec((1, width), fixed, **once),
            ],
            out_specs=[tokens(width), tokens(width), tokens(width), tokens(padded), tokens(2 * padded)]
            + [halves_spec(seqs, span, width)] * 4,
            scratch_shapes=[pltpu.VMEM((width, 2 * padded), bf16), pltpu.VMEM((padded, width), bf16)],
        ),
        out_shape=[shape(width, bf16), shape(width, f32), shape(width, bf16), shape(padded, bf16), shape(2 * padded, bf16)]
        + [half] * 4,
        compiler_params=pltpu.CompilerParams(vmem_limit_bytes=60 << 20),
        cost_estimate=pl.CostEstimate(flops=seqs * length * width * (2 * width + 12 * padded), bytes_accessed=seqs * length * width * 20, transcendentals=seqs * length * padded),
        name="ffn",
    )(at, *parts, *wgu_blocks, *wd_blocks, x, cot, w_out, gain)


def product_kernel(cuts, left_ref, right_ref, *refs):
    out_ref, total = refs[-2:]
    step = pl.program_id(0)
    value = dot_tn(left_ref[...], right_ref[...])

    @pl.when(step == 0)
    def _():
        total[...] = value

    @pl.when(step > 0)
    def _():
        total[...] += value

    @pl.when(step == pl.num_programs(0) - 1)
    def _():
        for i, (begin, end) in enumerate(cuts):
            out_ref[i] = total[: out_ref.shape[1], begin:end].astype(bf16)


def product(left, right, out_rows, cuts, earlier=()):
    rows = left.shape[0]
    tile = 512
    at = lambda i: (i, 0)
    return pl.pallas_call(
        functools.partial(product_kernel, cuts),
        grid=(rows // tile,),
        in_specs=[pl.BlockSpec((tile, left.shape[1]), at), pl.BlockSpec((tile, right.shape[1]), at)]
        + any_space(len(earlier)),
        out_specs=pl.BlockSpec((len(cuts), out_rows, cuts[0][1] - cuts[0][0]), lambda i: (0, 0, 0)),
        out_shape=jax.ShapeDtypeStruct((len(cuts), out_rows, cuts[0][1] - cuts[0][0]), bf16),
        scratch_shapes=[pltpu.VMEM((left.shape[1], right.shape[1]), f32)],
        compiler_params=pltpu.CompilerParams(vmem_limit_bytes=48 << 20),
        cost_estimate=pl.CostEstimate(flops=2 * rows * left.shape[1] * right.shape[1], bytes_accessed=2 * rows * (left.shape[1] + right.shape[1]), transcendentals=0),
        name="product",
    )(left, right, *earlier)


def mid_kernel(at_ref, mid_ref, cot_ref, gain_ref, wo_ref, even_ref, got_ref, sent_x, sent_y, last_x, last_y, grad_ref, half_ref, out_ref):
    seqs, span, width = cot_ref.shape
    grad_nm = even_ref[0].astype(f32) + got_ref[0].astype(f32)
    more = [sent_x[0].astype(f32) + last_y[...].astype(f32), sent_y[0].astype(f32) + last_x[...].astype(f32)]
    grad_nm = (grad_nm + jnp.concatenate(more, axis=0)).reshape(seqs * span, width)
    mid = mid_ref[...].reshape(seqs * span, width)
    factor = lax.rsqrt(jnp.mean(mid * mid, axis=-1, keepdims=True) + eps)
    normed = mid * factor
    scaled = grad_nm * gain_ref[...]
    grad = cot_ref[...].reshape(seqs * span, width).astype(f32) + factor * (
        scaled - normed * jnp.mean(scaled * normed, axis=-1, keepdims=True)
    )
    grad_ref[...] = grad
    half = grad.astype(bf16)
    half_ref[...] = half
    out = dot_nt(half, wo_ref[...]).astype(bf16)
    for g in range(8):
        out_ref[g] = out[:, g * 128 : (g + 1) * 128].reshape(seqs, span, 128)


def mid_bwd(at, mid, cot, gain, w_out, even, stages):
    seqs, span, width = cot.shape
    got, sent_x, sent_y, last_x, last_y = stages
    half = seqs // 2
    first = lambda *s: pl.BlockSpec((1,) + s, lambda i, m: (0,) * (len(s) + 1))
    full = lambda *s: pl.BlockSpec(s, lambda i, m: (0,) * len(s))
    rows = seqs * span
    return pl.pallas_call(
        mid_kernel,
        grid_spec=pltpu.PrefetchScalarGridSpec(
            num_scalar_prefetch=1,
            grid=(1,),
            in_specs=[
                pl.BlockSpec((seqs, span, width), lambda i, m: (0, m[0], 0)),
                full(seqs, span, width),
                full(1, width),
                full(width, width),
                first(seqs, span, width),
                first(seqs, span, width),
                first(half, span, width),
                first(half, span, width),
                full(half, span, width),
                full(half, span, width),
            ],
            out_specs=[full(rows, width), full(rows, width), full(8, seqs, span, 128)],
        ),
        out_shape=[
            jax.ShapeDtypeStruct((rows, width), f32),
            jax.ShapeDtypeStruct((rows, width), bf16),
            jax.ShapeDtypeStruct((8, seqs, span, 128), bf16),
        ],
        compiler_params=pltpu.CompilerParams(vmem_limit_bytes=40 << 20),
        cost_estimate=pl.CostEstimate(flops=2 * rows * width * width, bytes_accessed=rows * width * 20, transcendentals=0),
        name="mid_bwd",
    )(at, mid, cot, gain, w_out, even, got, sent_x, sent_y, last_x, last_y)


def qkv_bwd_kernel(at_ref, dq_ref, dkv_ref, raw_ref, nm_ref, w_ref, scale_ref, cos_ref, sin_ref, *refs):
    even_ref, odd_ref, dw_ref, dscale_ref, dw_acc = refs[-5:]
    step = pl.program_id(0)
    seqs, span, width = nm_ref.shape
    tile = seqs * span

    @pl.when(step == 0)
    def _():
        dw_acc[...] = jnp.zeros_like(dw_acc)
        dscale_ref[...] = jnp.zeros_like(dscale_ref)

    cos, sin = cos_ref[...].reshape(tile, 128), sin_ref[...].reshape(tile, 128)
    mean = head_mean()

    def average(array):
        return jnp.dot(array, mean, precision=exact, preferred_element_type=f32)

    def back(raw, grad, scale):
        inv = lax.rsqrt(average(raw * raw) + eps)
        normed = raw * inv
        turned = grad * cos + half_turn(grad * sin, True)
        grad_normed = turned * scale
        grad_raw = inv * (grad_normed - normed * average(grad_normed * normed))
        return grad_raw, jnp.sum(turned * normed, axis=0, keepdims=True)

    raw = raw_ref[...].reshape(tile, 256)
    grad_kv = dkv_ref[...].reshape(tile, 128)
    dq, q_scale = back(raw[:, :128], dq_ref[...].reshape(tile, 128), scale_ref[0:1, :])
    dkv, k_scale = back(raw[:, 128:], grad_kv, scale_ref[1:2, :])
    dkv = jnp.where(lane_index(tile) < HD, dkv, grad_kv)
    grad = jnp.concatenate([dq.astype(bf16), dkv.astype(bf16)], axis=1)
    dscale_ref[0:1, :] += q_scale
    dscale_ref[1:2, :] += k_scale
    store_halves(at_ref[0], step, dot_nt(grad, w_ref[...]).astype(bf16), even_ref, odd_ref)
    dw_acc[...] += dot_tn(nm_ref[...].reshape(tile, width), grad)

    @pl.when(step == pl.num_programs(0) - 1)
    def _():
        dw_ref[...] = dw_acc[...].astype(bf16)


def qkv_bwd(at, dq, dkv, raw, nm, w_qkv, scales, cosine, sine, earlier):
    seqs, length, width = nm.shape
    span = length // 8
    tokens = lambda cols: pl.BlockSpec((seqs, span, cols), lambda t, m: (0, t, 0))
    fixed = lambda t, m: (0, 0)
    half = jax.ShapeDtypeStruct((4, seqs, span, width), bf16)
    return pl.pallas_call(
        qkv_bwd_kernel,
        grid_spec=pltpu.PrefetchScalarGridSpec(
            num_scalar_prefetch=1,
            grid=(8,),
            in_specs=[
                tokens(128),
                tokens(128),
                tokens(256),
                tokens(width),
                pl.BlockSpec((width, 256), fixed),
                pl.BlockSpec((8, 128), fixed),
                tokens(128),
                tokens(128),
            ]
            + any_space(len(earlier)),
            out_specs=[halves_spec(seqs, span, width)] * 2
            + [pl.BlockSpec((width, 256), fixed), pl.BlockSpec((8, 128), fixed)],
            scratch_shapes=[pltpu.VMEM((width, 256), f32)],
        ),
        out_shape=[
            half,
            half,
            jax.ShapeDtypeStruct((width, 256), bf16),
            jax.ShapeDtypeStruct((8, 128), f32),
        ],
        compiler_params=pltpu.CompilerParams(vmem_limit_bytes=48 << 20),
        cost_estimate=pl.CostEstimate(flops=16 * seqs * length * width * 256, bytes_accessed=seqs * length * width * 6, transcendentals=0),
        name="qkv_bwd",
    )(at, dq, dkv, raw, nm, w_qkv, scales, cosine, sine, *earlier)


def plain_body(
    block_input,
    positions,
    cotangent,
    attention_gain,
    query_weight,
    key_weight,
    value_weight,
    query_gain,
    key_gain,
    output_weight,
    feedforward_gain,
    gate_weight,
    up_weight,
    down_weight,
):
    seq_count, span, width = block_input.shape
    groups = lax.axis_size("seq")
    size = lax.axis_size("fsdp")
    me = lax.axis_index("seq")
    length = span * groups
    rows = seq_count * length
    own_rows = seq_count * span
    shard = query_weight.shape[0]
    heads = H // groups
    kv_heads = max(1, KV // groups)
    copies = max(1, groups // KV)
    q_cols, k_cols = heads * HD, kv_heads * HD
    qkv_cols = q_cols + 2 * k_cols
    part = gate_weight.shape[1] // (groups * size)
    hidden_cols = part * size

    x_full = gather_seq(block_input, 1)

    def columns(weight, col_copies):
        shaped = weight.reshape(shard, -1, 1, HD)
        shaped = jnp.broadcast_to(shaped, (shard, shaped.shape[1], col_copies, HD))
        return shaped.reshape(shard, groups, -1)

    packed = jnp.concatenate(
        [
            columns(query_weight, 1),
            columns(key_weight, copies),
            columns(value_weight, copies),
        ],
        axis=2,
    ).transpose(1, 0, 2)
    gains = jnp.concatenate([attention_gain, feedforward_gain])
    gain_rows = jnp.zeros((16, qkv_cols), bf16).at[0, : 2 * shard].set(gains)
    packed = jnp.concatenate(
        [packed, jnp.broadcast_to(gain_rows[None], (groups, 16, qkv_cols))], axis=1
    )
    packed = gather_line(spread(packed))
    w_qkv = packed[:, :, :shard, :].reshape(width, qkv_cols)
    gain_one = packed[:, :, shard, :shard].reshape(width).astype(f32)
    gain_two = packed[:, :, shard, shard : 2 * shard].reshape(width).astype(f32)

    out_full = lax.all_gather(output_weight, ("fsdp", "seq"), axis=0, tiled=True)

    def ff_columns(weight):
        shaped = weight.reshape(shard, size, groups, part)
        return shaped.transpose(2, 0, 1, 3).reshape(groups, shard, hidden_cols)

    w_gate_up = gather_line(
        spread(jnp.concatenate([ff_columns(gate_weight), ff_columns(up_weight)], axis=2))
    ).reshape(width, 2 * hidden_cols)
    w_gate = w_gate_up[:, :hidden_cols]
    w_up = w_gate_up[:, hidden_cols:]
    w_down = gather_line(down_weight).reshape(hidden_cols, width)

    cot_full = gather_seq(cotangent, 1).reshape(rows, width)

    residual_in = x_full.reshape(rows, width).astype(f32)
    factor_one = inv_rms(residual_in)
    normed_in = (residual_in * factor_one * gain_one).astype(bf16)
    qkv_raw = matmul(normed_in, w_qkv)
    query_raw = qkv_raw[:, :q_cols]
    key_raw = qkv_raw[:, q_cols : q_cols + k_cols]
    value_rows = qkv_raw[:, q_cols + k_cols :].astype(bf16)
    cosine, sine = rope_tables(positions.reshape(rows), HD)
    query_scale = query_gain.astype(f32)
    key_scale = key_gain.astype(f32)

    def query_side(raw_rows, gain_row):
        return head_prep(raw_rows, gain_row, cosine, sine, heads)

    def key_side(raw_rows, gain_row):
        return head_prep(raw_rows, gain_row, cosine, sine, kv_heads)

    def head_view(packed_rows):
        shaped = packed_rows.reshape(seq_count, length, -1, HD)
        return jnp.repeat(shaped, heads // shaped.shape[2], axis=2)

    queries = query_side(query_raw, query_scale).astype(bf16).reshape(seq_count, length, heads, HD)
    keys = head_view(key_side(key_raw, key_scale).astype(bf16))
    values = head_view(value_rows)
    doc_start = jnp.arange(length, dtype=jnp.int32)[None, :] - positions
    outputs, log_totals = jax.vmap(attend_fwd)(queries, keys, values, doc_start)

    attn_full = gather_seq(outputs.reshape(seq_count, length, q_cols), 2)
    attn_rows = attn_full.reshape(rows, width)
    residual_mid = residual_in + matmul(attn_rows, out_full)
    factor_two = inv_rms(residual_mid)
    normed_mid = (residual_mid * factor_two * gain_two).astype(bf16)

    def own(array):
        shaped = array.reshape(seq_count, length, -1)
        return lax.dynamic_slice_in_dim(shaped, me * span, span, 1).reshape(own_rows, -1)

    gate_rows = matmul(normed_mid, w_gate)
    up_rows = matmul(normed_mid, w_up)
    sigma = jax.nn.sigmoid(gate_rows)
    hidden = (gate_rows * sigma * up_rows).astype(bf16)
    grad_hidden = matmul_nt(cot_full, w_down)
    grad_gate = (grad_hidden * up_rows * sigma * (1.0 + gate_rows * (1.0 - sigma))).astype(bf16)
    grad_up = (grad_hidden * gate_rows * sigma).astype(bf16)
    grad_normed_part = (matmul_nt(grad_gate, w_gate) + matmul_nt(grad_up, w_up)).astype(bf16)
    grad_normed_mid = reduce_seq(grad_normed_part.reshape(seq_count, length, width), 1)
    grad_normed_mid = grad_normed_mid.reshape(own_rows, width)

    residual_own = own(residual_mid)
    cot_rows = cotangent.reshape(own_rows, width).astype(f32)
    grad_mid = cot_rows + norm_bwd(residual_own, own(factor_two), gain_two, grad_normed_mid)
    grad_mid_half = grad_mid.astype(bf16)
    grad_attn_out = matmul_nt(grad_mid_half, out_full).astype(bf16)
    grad_heads = lax.all_to_all(
        grad_attn_out.reshape(seq_count, span, width), "seq", split_axis=2, concat_axis=1, tiled=True
    )

    grad_query_heads, grad_key_heads, grad_value_heads = jax.vmap(attend_bwd)(
        queries,
        keys,
        values,
        outputs,
        log_totals,
        grad_heads.reshape(seq_count, length, heads, HD),
        doc_start,
    )

    def fold(packed_rows):
        shaped = packed_rows.reshape(rows, kv_heads, -1, HD).astype(f32)
        return jnp.sum(shaped, axis=2).reshape(rows, k_cols)

    _, query_back = jax.vjp(query_side, query_raw, query_scale)
    grad_query_raw, query_gain_term = query_back(grad_query_heads.reshape(rows, q_cols).astype(f32))
    _, key_back = jax.vjp(key_side, key_raw, key_scale)
    grad_key_raw, key_gain_term = key_back(fold(grad_key_heads))
    grad_qkv = jnp.concatenate(
        [
            grad_query_raw.astype(bf16),
            grad_key_raw.astype(bf16),
            fold(grad_value_heads).astype(bf16),
        ],
        axis=1,
    )
    grad_in_part = matmul_nt(grad_qkv, w_qkv).astype(bf16)
    grad_normed_in = reduce_seq(grad_in_part.reshape(seq_count, length, width), 1)
    grad_normed_in = grad_normed_in.reshape(own_rows, width)
    own_in = block_input.reshape(own_rows, width).astype(f32)
    input_grad = (
        (grad_mid + norm_bwd(own_in, inv_rms(own_in), gain_one, grad_normed_in))
        .astype(bf16)
        .reshape(seq_count, span, width)
    )

    result_part = matmul(hidden, w_down).astype(bf16).reshape(seq_count, length, width)
    block_output = (
        (residual_own + reduce_seq(result_part, 1).reshape(own_rows, width))
        .astype(bf16)
        .reshape(seq_count, span, width)
    )

    down_grad = reduce_line(matmul_tn(hidden, cot_full).reshape(size, part, width))
    gate_up_term = matmul_tn(normed_mid, jnp.concatenate([grad_gate, grad_up], axis=1))
    gate_up_term = reduce_line(gate_up_term.reshape(size, groups * shard, 2 * hidden_cols))
    gate_up_home = spread(gate_up_term.astype(bf16).reshape(groups, shard, 2 * hidden_cols))

    def ff_home(columns_home):
        shaped = columns_home.astype(f32).reshape(groups, shard, size, part)
        return shaped.transpose(1, 2, 0, 3).reshape(shard, groups * size * part)

    gate_grad = ff_home(gate_up_home[:, :, :hidden_cols])
    up_grad = ff_home(gate_up_home[:, :, hidden_cols:])

    output_term = matmul_tn(own(attn_rows), grad_mid_half).astype(bf16)
    output_grad = lax.psum_scatter(
        output_term, ("fsdp", "seq"), scatter_dimension=0, tiled=True
    ).astype(f32)

    qkv_term = reduce_line(matmul_tn(normed_in, grad_qkv).reshape(size, groups * shard, qkv_cols))
    qkv_home = spread(qkv_term.astype(bf16).reshape(groups, shard, qkv_cols)).astype(f32)

    def home(block, col_copies):
        shaped = block.transpose(1, 0, 2).reshape(shard, -1, col_copies, HD)
        return jnp.sum(shaped, axis=2).reshape(shard, -1)

    query_grad = home(qkv_home[:, :, :q_cols], 1)
    key_grad = home(qkv_home[:, :, q_cols : q_cols + k_cols], copies)
    value_grad = home(qkv_home[:, :, q_cols + k_cols :], copies)

    def weighted(weight, grad):
        return jnp.sum(weight.astype(f32) * grad, axis=1)

    gain_one_grad = (
        weighted(query_weight, query_grad)
        + weighted(key_weight, key_grad)
        + weighted(value_weight, value_grad)
    ) / attention_gain.astype(f32)
    gain_two_grad = (
        weighted(gate_weight, gate_grad) + weighted(up_weight, up_grad)
    ) / feedforward_gain.astype(f32)

    head_gains = sum_everywhere(jnp.concatenate([query_gain_term, key_gain_term])[None])[0]
    return (
        block_output,
        input_grad,
        gain_one_grad,
        query_grad,
        key_grad,
        value_grad,
        head_gains[:HD],
        head_gains[HD:],
        output_grad,
        gain_two_grad,
        gate_grad,
        up_grad,
        down_grad,
    )


def after(array, earlier):
    first = earlier.reshape(-1)[0] if earlier.ndim == 1 else earlier[(0,) * earlier.ndim]
    return array + jnp.minimum(jnp.abs(first), 0).astype(array.dtype)


def swap_line(array, mask):
    size = lax.axis_size("fsdp")
    return lax.ppermute(array, "fsdp", [(i, i ^ mask) for i in range(size)])


def line_blocks(block):
    return [block] + [swap_line(block, m) for m in (1, 2, 3)]


def line_parts(block_of):
    me = lax.axis_index("fsdp")
    return [swap_line(block_of(me ^ m), m) for m in (1, 2, 3)]


def add_up(own, others):
    total = own.astype(f32)
    for other in others:
        total = total + other.astype(f32)
    return total


def reduce_stages(even, odd):
    half = even.shape[1] // 2
    got = swap(odd, 1)

    def held(i, low):
        cut = slice(0, half) if low else slice(half, None)
        return even[i, cut].astype(f32) + got[i, cut].astype(f32)

    sent_x = swap(jnp.stack([held(1, True), held(3, True)]).astype(bf16), 2)
    sent_y = swap(jnp.stack([held(2, False), held(3, False)]).astype(bf16), 4)
    last_y = swap((held(2, True) + sent_x[1].astype(f32)).astype(bf16), 4)
    last_x = swap((held(1, False) + sent_y[1].astype(f32)).astype(bf16), 2)
    return got, sent_x, sent_y, last_x, last_y


def own_sum(even, stages):
    got, sent_x, sent_y, last_x, last_y = stages
    low = sent_x[0].astype(f32) + last_y.astype(f32)
    high = sent_y[0].astype(f32) + last_x.astype(f32)
    return even[0].astype(f32) + got[0].astype(f32) + jnp.concatenate([low, high], axis=0)


def body(
    block_input,
    positions,
    cotangent,
    attention_gain,
    query_weight,
    key_weight,
    value_weight,
    query_gain,
    key_gain,
    output_weight,
    feedforward_gain,
    gate_weight,
    up_weight,
    down_weight,
):
    seqs, span, width = block_input.shape
    groups = lax.axis_size("seq")
    size = lax.axis_size("fsdp")
    if not (groups == 8 and size == 4 and seqs % 2 == 0 and span % 64 == 0):
        return plain_body(
            block_input,
            positions,
            cotangent,
            attention_gain,
            query_weight,
            key_weight,
            value_weight,
            query_gain,
            key_gain,
            output_weight,
            feedforward_gain,
            gate_weight,
            up_weight,
            down_weight,
        )
    me = lax.axis_index("seq")
    me_line = lax.axis_index("fsdp")
    at = jnp.stack([me, me_line]).astype(jnp.int32)
    length = span * groups
    rows = seqs * length
    own_rows = seqs * span
    shard = query_weight.shape[0]
    part = gate_weight.shape[1] // (groups * size)
    hidden_cols = part * size
    padded = -(-hidden_cols // 128) * 128

    x_blocks = partner_blocks(block_input)
    packed = jnp.concatenate(
        [
            query_weight.reshape(shard, groups, 2 * HD),
            key_weight.reshape(shard, groups, HD),
            value_weight.reshape(shard, groups, HD),
        ],
        axis=2,
    ).transpose(1, 0, 2)
    gains = jnp.concatenate([attention_gain, feedforward_gain])
    gain_rows = jnp.zeros((16, 4 * HD), bf16).at[0, : 2 * shard].set(gains)
    packed = jnp.concatenate(
        [packed, jnp.broadcast_to(gain_rows[None], (groups, 16, 4 * HD))], axis=1
    )
    qkv_blocks = line_blocks(spread(packed))
    gains = jnp.stack([block[:, shard, : 2 * shard] for block in qkv_blocks])
    gains = jnp.take(gains, me_line ^ jnp.arange(size), axis=0).astype(f32)
    gain_one = gains[:, :, :shard].reshape(1, width)
    gain_two = gains[:, :, shard:].reshape(1, width)

    down_blocks = line_blocks(down_weight)
    gate_up = spread(after(pack_columns(gate_weight, up_weight, groups, part), x_blocks[6]))
    gate_up_blocks = line_blocks(gate_up)
    w_out = lax.all_gather(output_weight, ("fsdp", "seq"), axis=0, tiled=True)
    cot_full = lax.all_gather(cotangent, "seq", axis=1, tiled=True)

    inverse = rope_base ** (-(jnp.arange(HD // 2, dtype=f32) * 2.0) / HD)
    angles = positions.astype(f32)[:, :, None] * jnp.tile(inverse, 4)[None, None, :]
    cosine, sine = jnp.cos(angles), jnp.sin(angles)
    scales = jnp.concatenate(
        [jnp.tile(query_gain, 2)[None], jnp.tile(key_gain, 2)[None], jnp.zeros((6, 128), bf16)]
    ).astype(f32)
    starts = jnp.arange(length, dtype=jnp.int32)[None, :] - positions
    x_full, normed_in, qkv_raw, q_rows, kv_rows, w_qkv = qkv_fwd(
        at, x_blocks, qkv_blocks, gain_one, scales, cosine, sine, [gate_up]
    )
    starts_wide = jnp.broadcast_to(starts[:, :, None], (seqs, length, 128))
    outputs, totals = attn_fwd(q_rows, kv_rows, starts_wide, span)

    attn_rows, residual_mid, normed_mid, hidden, ff_grads, gnm_even, gnm_odd, out_even, out_odd = ffn(
        at, partner_blocks(outputs), gate_up_blocks, down_blocks, x_full, cot_full, w_out, gain_two
    )
    flat = lambda array: array.reshape(rows, -1)

    mid_stages = reduce_stages(gnm_even, gnm_odd)
    down_term = product(flat(hidden), flat(cot_full), hidden_cols, ((0, width),), [mid_stages[0]])[0]
    cuts = ((0, hidden_cols), (padded, padded + hidden_cols))
    gate_up_term = product(flat(normed_mid), flat(ff_grads), width, cuts, [down_term])
    grad_mid, grad_mid_half, grad_attn_out = mid_bwd(
        at, residual_mid, cotangent, gain_two, w_out, gnm_even, mid_stages
    )
    grad_heads = spread(grad_attn_out)

    def block_rows(term, f, count):
        return lax.dynamic_slice_in_dim(term, f * count, count, term.ndim - 2)

    down_parts = line_parts(lambda f: block_rows(down_term, f, part))
    gate_up_parts = line_parts(lambda f: block_rows(gate_up_term, f, groups * shard))
    out_stages = reduce_stages(out_even, after(out_odd, grad_mid_half))

    totals_row = jnp.stack([totals[:, :, 0], totals[:, :, HD]], axis=1)
    totals_row = jnp.concatenate([totals_row, jnp.zeros((seqs, 6, length), f32)], axis=1)
    starts_row = jnp.broadcast_to(starts[:, None, :], (seqs, 8, length))
    grad_q, grad_kv = attn_bwd(
        q_rows, kv_rows, grad_heads, outputs, totals_row, starts_row, span, [gate_up_term, out_stages[0]]
    )
    gin_even, gin_odd, qkv_term, head_gains = qkv_bwd(
        at, grad_q, grad_kv, qkv_raw, normed_in, w_qkv, scales, cosine, sine,
        [out_stages[1], out_stages[2]] + down_parts + gate_up_parts,
    )
    in_stages = reduce_stages(gin_even, gin_odd)
    own_in = block_input.reshape(own_rows, width).astype(f32)
    grad_normed_in = own_sum(gin_even, in_stages).reshape(own_rows, width)
    input_grad = (
        (grad_mid + norm_bwd(own_in, inv_rms(own_in), gain_one, grad_normed_in))
        .astype(bf16)
        .reshape(seqs, span, width)
    )

    residual_own = lax.dynamic_slice_in_dim(residual_mid, me * span, span, 1)
    block_output = (residual_own + own_sum(out_even, out_stages)).astype(bf16)

    down_grad = add_up(block_rows(down_term, me_line, part), down_parts)
    gate_up_sum = add_up(block_rows(gate_up_term, me_line, groups * shard), gate_up_parts)
    gate_up_sum = gate_up_sum.astype(bf16).reshape(2, groups, shard, hidden_cols).transpose(1, 0, 2, 3)
    gate_grad, up_grad, gain_two_sum = unpack_columns(spread(gate_up_sum), gate_weight, up_weight, part)

    attn_own = lax.dynamic_slice_in_dim(attn_rows, me * span, span, 1).reshape(own_rows, width)
    output_term = matmul_tn(attn_own, grad_mid_half).astype(bf16)
    output_term = reduce_seq(output_term.reshape(size, groups * shard, width), 1).astype(bf16)
    output_grad = add_up(
        lax.dynamic_index_in_dim(output_term, me_line, 0, keepdims=False),
        line_parts(lambda f: lax.dynamic_index_in_dim(output_term, f, 0, keepdims=False)),
    )

    qkv_parts = line_parts(lambda f: block_rows(qkv_term, f, groups * shard))
    qkv_sum = add_up(block_rows(qkv_term, me_line, groups * shard), qkv_parts).astype(bf16)
    query_grad, key_grad, value_grad, gain_one_sum = unpack_heads(
        spread(qkv_sum.reshape(groups, shard, 4 * HD)), query_weight, key_weight, value_weight
    )

    gain_one_grad = gain_one_sum[:, 0] / attention_gain.astype(f32)
    gain_two_grad = gain_two_sum[:, 0] / feedforward_gain.astype(f32)

    head_gains = sum_everywhere(head_gains)
    return (
        block_output,
        input_grad,
        gain_one_grad,
        query_grad,
        key_grad,
        value_grad,
        head_gains[0, :HD] + head_gains[0, HD:],
        head_gains[1, :HD],
        output_grad,
        gain_two_grad,
        gate_grad,
        up_grad,
        down_grad,
    )


def solution(mesh):
    shards = P(("fsdp", "seq"), None)
    vector = P(("fsdp", "seq"))
    tokens = P("fsdp", "seq", None)
    return jax.shard_map(
        body,
        mesh=mesh,
        in_specs=(
            tokens,
            P("fsdp", None),
            tokens,
            vector,
            shards,
            shards,
            shards,
            P(),
            P(),
            shards,
            vector,
            shards,
            shards,
            shards,
        ),
        out_specs=(
            tokens,
            tokens,
            vector,
            shards,
            shards,
            shards,
            P(),
            P(),
            shards,
            vector,
            shards,
            shards,
            shards,
        ),
        check_vma=False,
    )
```

```python
import functools

import jax
import jax.numpy as jnp
from jax import lax
from jax.experimental import pallas as pl
from jax.experimental.pallas import tpu as pltpu
from jax.sharding import PartitionSpec as P

H = 16
KV = 8
HD = 64

rope_base = 1000000.0
eps = 1e-05
masked = -1e30
f32 = jnp.float32
bf16 = jnp.bfloat16


def contract(formula, left, right):
    return jnp.einsum(formula, left, right, preferred_element_type=f32)


def matmul(left, right):
    return jnp.dot(left, right, preferred_element_type=f32)


def matmul_nt(left, right):
    return lax.dot_general(left, right, (((1,), (1,)), ((), ())), preferred_element_type=f32)


def matmul_tn(left, right):
    return lax.dot_general(left, right, (((0,), (0,)), ((), ())), preferred_element_type=f32)


def rope_tables(places, head_width):
    half_width = head_width // 2
    inverse = rope_base ** (-(jnp.arange(half_width, dtype=f32) * 2.0) / head_width)
    angles = places.astype(f32)[:, None] * inverse[None, :]
    return (jnp.cos(angles)[:, None, :], jnp.sin(angles)[:, None, :])


def head_prep(raw_rows, gain_row, cosine, sine, head_count):
    row_count = raw_rows.shape[0]
    split_rows = raw_rows.reshape(row_count, head_count, -1)
    factor = lax.rsqrt(jnp.mean(split_rows * split_rows, axis=-1, keepdims=True) + eps)
    normed = split_rows * factor * gain_row
    half_width = normed.shape[-1] // 2
    lower = normed[..., :half_width]
    upper = normed[..., half_width:]
    turned = jnp.concatenate(
        [lower * cosine - upper * sine, upper * cosine + lower * sine], axis=-1
    )
    return turned.reshape(row_count, -1)


def inv_rms(values):
    return lax.rsqrt(jnp.mean(values * values, axis=-1, keepdims=True) + eps)


def norm_bwd(values, factor, gain_row, grad_result):
    normed = values * factor
    grad_normed = grad_result * gain_row
    return factor * (
        grad_normed - normed * jnp.mean(grad_normed * normed, axis=-1, keepdims=True)
    )


def masked_scores(queries, key_rows, doc_start, begin_row, end_row, scaling):
    query_index = jnp.arange(begin_row, end_row, dtype=jnp.int32)
    key_index = jnp.arange(end_row, dtype=jnp.int32)
    allowed = (key_index[None, :] <= query_index[:, None]) & (
        key_index[None, :] >= doc_start[begin_row:end_row, None]
    )
    scores = contract("qhd,khd->hqk", queries[begin_row:end_row], key_rows[:end_row]) * scaling
    return jnp.where(allowed[None, :, :], scores, masked)


def attend_fwd(queries, key_rows, value_rows, doc_start):
    seq_length, head_count, head_width = queries.shape
    block_rows = min(512, seq_length)
    scaling = head_width ** (-0.5)
    out_blocks = []
    total_blocks = []
    for begin_row in range(0, seq_length, block_rows):
        end_row = begin_row + block_rows
        scores = masked_scores(queries, key_rows, doc_start, begin_row, end_row, scaling)
        largest = jnp.max(scores, axis=-1, keepdims=True)
        log_total = largest + jnp.log(jnp.sum(jnp.exp(scores - largest), axis=-1, keepdims=True))
        attn_prob = jnp.exp(scores - log_total).astype(bf16)
        out_blocks.append(contract("hqk,khd->qhd", attn_prob, value_rows[:end_row]).astype(bf16))
        total_blocks.append(log_total[..., 0])
    return (jnp.concatenate(out_blocks, axis=0), jnp.concatenate(total_blocks, axis=1))


def attend_bwd(queries, key_rows, value_rows, outputs, log_totals, grad_result, doc_start):
    seq_length, head_count, head_width = queries.shape
    block_rows = min(512, seq_length)
    scaling = head_width ** (-0.5)
    carried = jnp.sum(grad_result.astype(f32) * outputs.astype(f32), axis=-1).T
    grad_query = []
    grad_key = jnp.zeros((seq_length, head_count, head_width), f32)
    grad_value = jnp.zeros((seq_length, head_count, head_width), f32)
    for begin_row in range(0, seq_length, block_rows):
        end_row = begin_row + block_rows
        scores = masked_scores(queries, key_rows, doc_start, begin_row, end_row, scaling)
        attn_prob = jnp.exp(scores - log_totals[:, begin_row:end_row, None])
        prob_half = attn_prob.astype(bf16)
        grad_rows = grad_result[begin_row:end_row]
        grad_value = grad_value.at[:end_row].add(contract("hqk,qhd->khd", prob_half, grad_rows))
        grad_prob = contract("qhd,khd->hqk", grad_rows, value_rows[:end_row])
        grad_score = (
            attn_prob * (grad_prob - carried[:, begin_row:end_row, None]) * scaling
        ).astype(bf16)
        grad_query.append(contract("hqk,khd->qhd", grad_score, key_rows[:end_row]))
        grad_key = grad_key.at[:end_row].add(
            contract("hqk,qhd->khd", grad_score, queries[begin_row:end_row])
        )
    return (
        jnp.concatenate(grad_query, axis=0).astype(bf16),
        grad_key.astype(bf16),
        grad_value.astype(bf16),
    )


def swap(array, mask):
    groups = lax.axis_size("seq")
    return lax.ppermute(array, "seq", [(i, i ^ mask) for i in range(groups)])


def partner_blocks(block):
    got = {0: block, 2: swap(block, 2), 4: swap(block, 4)}
    got[6] = swap(got[4], 2)
    for mask in (0, 2, 4, 6):
        got[mask + 1] = swap(got[mask], 1)
    return [got[j] for j in range(8)]


def gather_seq(block, axis):
    if lax.axis_size("seq") != 8 or block.shape[0] % 2:
        return lax.all_gather(block, "seq", axis=axis, tiled=True)
    me = lax.axis_index("seq")
    width = block.shape[axis]
    shape = list(block.shape)
    shape[axis] = width * 8
    whole = jnp.zeros(shape, block.dtype)
    for j, part in enumerate(partner_blocks(block)):
        whole = lax.dynamic_update_slice_in_dim(whole, part, (me ^ j) * width, axis)
    return whole


def reduce_seq(partial, axis):
    groups = lax.axis_size("seq")
    width = partial.shape[axis] // groups
    if groups != 8 or partial.shape[0] % 2:
        return lax.psum_scatter(partial, "seq", scatter_dimension=axis, tiled=True).astype(f32)
    me = lax.axis_index("seq")
    half = partial.shape[0] // 2

    def piece(j):
        return lax.dynamic_slice_in_dim(partial, (me ^ j) * width, width, axis)

    got = swap(jnp.stack([piece(j) for j in (1, 3, 5, 7)]), 1)
    held = {j: piece(j).astype(f32) + got[j // 2].astype(f32) for j in (0, 2, 4, 6)}
    first = {j: held[j][:half] for j in held}
    second = {j: held[j][half:] for j in held}
    sent_x = swap(jnp.stack([first[2].astype(bf16), first[6].astype(bf16)]), 2)
    sent_y = swap(jnp.stack([second[4].astype(bf16), second[6].astype(bf16)]), 4)
    last_y = swap((first[4] + sent_x[1].astype(f32)).astype(bf16), 4)
    last_x = swap((second[2] + sent_y[1].astype(f32)).astype(bf16), 2)
    own_first = first[0] + sent_x[0].astype(f32) + last_y.astype(f32)
    own_second = second[0] + sent_y[0].astype(f32) + last_x.astype(f32)
    return jnp.concatenate([own_first, own_second], axis=0)


def line_step(array, step):
    size = lax.axis_size("fsdp")
    return lax.ppermute(
        array, "fsdp", [(i, i + step) for i in range(size) if 0 <= i + step < size]
    )


def gather_line(block):
    size = lax.axis_size("fsdp")
    if size != 4:
        return lax.all_gather(block, "fsdp", axis=0, tiled=False)
    me = lax.axis_index("fsdp")
    below, above = [block], [block]
    for _ in range(size - 1):
        below.append(line_step(below[-1], 1))
        above.append(line_step(above[-1], -1))
    whole = jnp.zeros((size,) + block.shape, block.dtype)
    whole = lax.dynamic_update_index_in_dim(whole, block, me, 0)
    for k in range(1, size):
        part = below[k] + above[size - k]
        whole = lax.dynamic_update_index_in_dim(whole, part, lax.rem(me - k + size, size), 0)
    return whole


def reduce_line(partial):
    size = lax.axis_size("fsdp")
    if size != 4:
        return lax.psum_scatter(
            partial.astype(bf16), "fsdp", scatter_dimension=0, tiled=False
        ).astype(f32)
    me = lax.axis_index("fsdp")

    def entry(k):
        return lax.dynamic_index_in_dim(
            partial, lax.rem(me + k + size, size), 0, keepdims=False
        ).astype(f32)

    up, down = entry(size - 1), entry(1 - size)
    for k in range(size - 2, -1, -1):
        got_up = line_step(up.astype(bf16), 1).astype(f32)
        got_down = line_step(down.astype(bf16), -1).astype(f32)
        if k:
            up, down = entry(k) + got_up, entry(-k) + got_down
    return entry(0) + got_up + got_down


def spread(blocks):
    return lax.all_to_all(blocks, "seq", split_axis=0, concat_axis=0, tiled=True)


def sum_everywhere(vector):
    groups, size = lax.axis_size("seq"), lax.axis_size("fsdp")
    if groups != 8 or size != 4:
        return lax.psum(vector, ("fsdp", "seq"))
    for mask in (1, 2, 4):
        vector = vector + swap(vector, mask)
    for mask in (1, 2):
        vector = vector + lax.ppermute(vector, "fsdp", [(i, i ^ mask) for i in range(size)])
    return vector


exact = lax.Precision.HIGHEST


def dot_nt(left, right, precision=None):
    return lax.dot_general(left, right, (((1,), (1,)), ((), ())), precision=precision, preferred_element_type=f32)


def dot_tn(left, right):
    return lax.dot_general(left, right, (((0,), (0,)), ((), ())), preferred_element_type=f32)


def head_mean():
    row = lax.broadcasted_iota(jnp.int32, (128, 128), 0) // HD
    col = lax.broadcasted_iota(jnp.int32, (128, 128), 1) // HD
    return jnp.where(row == col, 1.0 / HD, 0.0).astype(bf16)


def head_average(array):
    high = array.astype(bf16)
    low = (array - high.astype(f32)).astype(bf16)
    mean = head_mean()
    return jnp.dot(high, mean, preferred_element_type=f32) + jnp.dot(low, mean, preferred_element_type=f32)


def lane_index(rows):
    return lax.broadcasted_iota(jnp.int32, (rows, 128), 1)


def half_turn(array, back):
    low = (lane_index(array.shape[0]) % HD) < HD // 2
    ahead = pltpu.roll(array, 128 - HD // 2, 1)
    behind = pltpu.roll(array, HD // 2, 1)
    return jnp.where(low, ahead, -behind) if back else jnp.where(low, -ahead, behind)


def attn_fwd_kernel(block, q_ref, kv_ref, start_ref, *refs):
    out_ref, lse_ref = refs[-2:]
    step = pl.program_id(1)
    steps = kv_ref.shape[1] // block
    lanes = lane_index(block)

    for at in range(steps):
        end = (at + 1) * block

        @pl.when(step == at)
        def _(at=at, end=end):
            k = kv_ref[0, :end, :HD]
            v = kv_ref[0, :end, HD:]
            q_index = at * block + lax.broadcasted_iota(jnp.int32, (block, end), 0)
            k_index = lax.broadcasted_iota(jnp.int32, (block, end), 1)
            allowed = (k_index <= q_index) & (k_index >= start_ref[0][:, :1])
            outs, totals = [], []
            for head in range(2):
                q = q_ref[0, :, head * HD : (head + 1) * HD] * jnp.array(HD ** -0.5, bf16)
                scores = jnp.where(allowed, dot_nt(q, k), masked)
                largest = jnp.max(scores, axis=-1, keepdims=True)
                weights = jnp.exp(scores - largest)
                total = jnp.sum(weights, axis=-1, keepdims=True)
                out = jnp.dot(weights.astype(bf16), v, preferred_element_type=f32) / total
                outs.append(out.astype(bf16))
                totals.append(largest + jnp.log(total))
            out_ref[0] = jnp.concatenate(outs, axis=1)
            lse_ref[0] = jnp.where(lanes < HD, totals[0], totals[1])


def attn_fwd(q, kv, starts, span, earlier):
    seqs, length, _ = q.shape
    block = 2 * span
    rows = lambda b, i: (b, i, 0)
    whole = lambda b, i: (b, 0, 0)
    return pl.pallas_call(
        functools.partial(attn_fwd_kernel, block),
        grid=(seqs, length // block),
        in_specs=[
            pl.BlockSpec((1, block, 128), rows),
            pl.BlockSpec((1, length, 128), whole),
            pl.BlockSpec((1, block, 128), rows),
        ]
        + [pl.BlockSpec(memory_space=pl.ANY)] * len(earlier),
        out_specs=[pl.BlockSpec((1, block, 128), rows), pl.BlockSpec((1, block, 128), rows)],
        out_shape=[
            jax.ShapeDtypeStruct((seqs, length, 128), bf16),
            jax.ShapeDtypeStruct((seqs, length, 128), f32),
        ],
        compiler_params=pltpu.CompilerParams(vmem_limit_bytes=48 << 20),
        cost_estimate=pl.CostEstimate(flops=seqs * length * length * 256, bytes_accessed=seqs * length * 1792, transcendentals=seqs * length * length),
        name="attn_fwd",
    )(q, kv, starts, *earlier)


def attn_bwd_kernel(block, q_ref, kv_ref, do_ref, o_ref, lse_ref, start_ref, *refs):
    dq_ref, dkv_ref, dk_acc, dv_acc = refs[-4:]
    step = pl.program_id(1)
    steps = kv_ref.shape[1] // block

    @pl.when(step == 0)
    def _():
        dk_acc[...] = jnp.zeros_like(dk_acc)
        dv_acc[...] = jnp.zeros_like(dv_acc)

    for at in range(steps):
        end = (at + 1) * block

        @pl.when(step == at)
        def _(at=at, end=end):
            k = kv_ref[0, :end, :HD]
            v = kv_ref[0, :end, HD:]
            k_index = lax.broadcasted_iota(jnp.int32, (end, block), 0)
            q_index = at * block + lax.broadcasted_iota(jnp.int32, (end, block), 1)
            allowed = (k_index <= q_index) & (k_index >= start_ref[0, 0:1, :])
            do_rows = do_ref[...].reshape(block, 128)
            product = do_rows.astype(f32) * o_ref[0].astype(f32)
            dqs = []
            for head in range(2):
                cut = slice(head * HD, (head + 1) * HD)
                q = q_ref[0, :, cut] * jnp.array(HD ** -0.5, bf16)
                do = do_rows[:, cut]
                delta = dot_nt(jnp.ones((8, HD), f32), product[:, cut], exact)[0:1, :]
                scores = jnp.where(allowed, dot_nt(k, q), masked)
                prob = jnp.exp(scores - lse_ref[0, head : head + 1, :])
                dv_acc[:end, :] += jnp.dot(prob.astype(bf16), do, preferred_element_type=f32)
                dscore = (prob * (dot_nt(v, do) - delta)).astype(bf16)
                dk_acc[:end, :] += jnp.dot(dscore, q, preferred_element_type=f32)
                dqs.append(dot_tn(dscore, k) * (HD ** -0.5))
            dq_ref[0] = jnp.concatenate(dqs, axis=1)

    @pl.when(step == steps - 1)
    def _():
        dkv_ref[0] = jnp.concatenate([dk_acc[...], dv_acc[...]], axis=1)


def attn_bwd(q, kv, do, out, lse, starts, span, earlier):
    seqs, length, _ = q.shape
    block = 2 * span
    rows = lambda b, i: (b, i, 0)
    cols = lambda b, i: (b, 0, i)
    whole = lambda b, i: (b, 0, 0)
    return pl.pallas_call(
        functools.partial(attn_bwd_kernel, block),
        grid=(seqs, length // block),
        in_specs=[
            pl.BlockSpec((1, block, 128), rows),
            pl.BlockSpec((1, length, 128), whole),
            pl.BlockSpec((2, 1, span, 128), lambda b, i: (i, b, 0, 0)),
            pl.BlockSpec((1, block, 128), rows),
            pl.BlockSpec((1, 8, block), cols),
            pl.BlockSpec((1, 8, block), cols),
        ]
        + [pl.BlockSpec(memory_space=pl.ANY)] * len(earlier),
        out_specs=[pl.BlockSpec((1, block, 128), rows), pl.BlockSpec((1, length, 128), whole)],
        out_shape=[
            jax.ShapeDtypeStruct((seqs, length, 128), f32),
            jax.ShapeDtypeStruct((seqs, length, 128), f32),
        ],
        scratch_shapes=[pltpu.VMEM((length, HD), f32), pltpu.VMEM((length, HD), f32)],
        compiler_params=pltpu.CompilerParams(vmem_limit_bytes=56 << 20),
        cost_estimate=pl.CostEstimate(flops=seqs * length * length * 640, bytes_accessed=seqs * length * 2560, transcendentals=seqs * length * length),
        name="attn_bwd",
    )(q, kv, do, out, lse, starts, *earlier)


def any_space(count):
    return [pl.BlockSpec(memory_space=pl.ANY)] * count


def pack_kernel(groups, part, gate_ref, up_ref, q_ref, k_ref, v_ref, gain_ref, out_ref):
    size = gate_ref.shape[1] // (groups * part)
    hidden = size * part
    for at, ref in ((0, gate_ref), (hidden, up_ref)):
        whole = ref[...].astype(f32)
        for g in range(groups):
            cuts = [whole[:, (f * groups + g) * part : (f * groups + g + 1) * part] for f in range(size)]
            out_ref[g, :, at : at + hidden] = jnp.concatenate(cuts, axis=1).astype(bf16)
    k, v = k_ref[...].astype(f32), v_ref[...].astype(f32)
    for g in range(groups):
        at = slice(g * HD, (g + 1) * HD)
        out_ref[g, :, 2 * hidden : 2 * hidden + 128] = q_ref[:, g * 128 : (g + 1) * 128]
        both = jnp.concatenate([k[:, at], v[:, at]], axis=1)
        out_ref[g, :, 2 * hidden + 128 : 2 * hidden + 256] = both.astype(bf16)
        out_ref[g, :, 2 * hidden + 256 :] = gain_ref[...]


def pack_columns(gate, up, query, key, value, gains, groups, part):
    shard, total = gate.shape
    return pl.pallas_call(
        functools.partial(pack_kernel, groups, part),
        out_shape=jax.ShapeDtypeStruct((groups, shard, 2 * total // groups + 384), bf16),
        name="pack",
    )(gate, up, query, key, value, gains)


def unpack_kernel(part, home_ref, gate_w_ref, up_w_ref, _, gate_ref, up_ref, sum_ref):
    groups, _, shard, hidden = home_ref.shape
    size = hidden // part
    for which, ref in ((0, gate_ref), (1, up_ref)):
        rows = [home_ref[g, which].astype(f32) for g in range(groups)]
        cuts = [rows[g][:, f * part : (f + 1) * part] for f in range(size) for g in range(groups)]
        ref[...] = jnp.concatenate(cuts, axis=1)
    total = jnp.sum(gate_w_ref[...].astype(f32) * gate_ref[...], axis=1, keepdims=True)
    total += jnp.sum(up_w_ref[...].astype(f32) * up_ref[...], axis=1, keepdims=True)
    sum_ref[...] = jnp.broadcast_to(total, sum_ref.shape)


def unpack_columns(home, gate_w, up_w, part, earlier):
    shape = gate_w.shape
    return pl.pallas_call(
        functools.partial(unpack_kernel, part),
        in_specs=[pl.BlockSpec(memory_space=pltpu.VMEM)] * 3 + any_space(1),
        out_shape=[
            jax.ShapeDtypeStruct(shape, f32),
            jax.ShapeDtypeStruct(shape, f32),
            jax.ShapeDtypeStruct((shape[0], 128), f32),
        ],
        name="unpack",
    )(home, gate_w, up_w, earlier)


def unpack_heads_kernel(home_ref, q_w_ref, k_w_ref, v_w_ref, q_ref, k_ref, v_ref, sum_ref, gain_ref):
    groups, shard = home_ref.shape[0], q_ref.shape[0]
    blocks = [home_ref[g].astype(f32) for g in range(groups)]
    q_ref[...] = jnp.concatenate([block[:shard, : 2 * HD] for block in blocks], axis=1)
    k_ref[...] = jnp.concatenate([block[:shard, 2 * HD : 3 * HD] for block in blocks], axis=1)
    v_ref[...] = jnp.concatenate([block[:shard, 3 * HD :] for block in blocks], axis=1)
    total = 0.0
    for weight, grad in ((q_w_ref, q_ref), (k_w_ref, k_ref), (v_w_ref, v_ref)):
        total += jnp.sum(weight[...].astype(f32) * grad[...], axis=1, keepdims=True)
    sum_ref[...] = jnp.broadcast_to(total, sum_ref.shape)
    gain_ref[...] = sum(block[shard : shard + 8] for block in blocks)


def unpack_heads(home, q_w, k_w, v_w):
    return pl.pallas_call(
        unpack_heads_kernel,
        out_shape=[jax.ShapeDtypeStruct(w.shape, f32) for w in (q_w, k_w, v_w)]
        + [jax.ShapeDtypeStruct((q_w.shape[0], 128), f32), jax.ShapeDtypeStruct((8, home.shape[2]), f32)],
        name="unpack_heads",
    )(home, q_w, k_w, v_w)


def qkv_fwd_kernel(at_ref, *refs):
    x_refs, w_refs = refs[:8], refs[8:12]
    gain_ref, scale_ref, cos_ref, sin_ref, x_out, nm_ref, raw_ref, q_ref, kv_ref, w_ref = refs[12:]
    step = pl.program_id(0)
    shard = w_ref.shape[0] // 32

    @pl.when(step == 0)
    def _():
        for m in range(4):
            for g in range(8):
                row = pl.multiple_of(((at_ref[1] ^ m) * 8 + g) * shard, shard)
                w_ref[pl.ds(row, shard), :] = w_refs[m][g, :, :256]

    for j in range(8):

        @pl.when(step == j)
        def _(j=j):
            x_out[...] = x_refs[j][...]

    x = x_out[...].reshape(-1, x_out.shape[-1]).astype(f32)
    factor = lax.rsqrt(jnp.mean(x * x, axis=-1, keepdims=True) + eps)
    nm = (x * factor * gain_ref[...]).astype(bf16)
    nm_ref[...] = nm.reshape(nm_ref.shape)
    raw = jnp.dot(nm, w_ref[...], preferred_element_type=f32)
    raw_ref[...] = raw.reshape(raw_ref.shape)
    cos = cos_ref[...].reshape(-1, 128)
    sin = sin_ref[...].reshape(-1, 128)

    def prepared(part, scale):
        inv = lax.rsqrt(head_average(part * part) + eps)
        normed = part * inv * scale
        return normed * cos + half_turn(normed, False) * sin

    q = prepared(raw[:, :128], scale_ref[0:1, :])
    kv = prepared(raw[:, 128:], scale_ref[1:2, :])
    kv = jnp.where(lane_index(kv.shape[0]) < HD, kv, raw[:, 128:])
    q_ref[...] = q.astype(bf16).reshape(q_ref.shape)
    kv_ref[...] = kv.astype(bf16).reshape(kv_ref.shape)


def qkv_fwd(at, x_blocks, w_blocks, gain, scales, cosine, sine, earlier):
    seqs, span, width = x_blocks[0].shape
    length = 8 * span
    home = lambda j, m: (0, m[0] ^ j, 0)
    fixed = lambda j, m: (0, 0)
    once = dict(pipeline_mode=pl.Buffered(1))

    def kernel(at_ref, *refs):
        qkv_fwd_kernel(at_ref, *refs[:16], *refs[16 + len(earlier) :])

    return pl.pallas_call(
        kernel,
        grid_spec=pltpu.PrefetchScalarGridSpec(
            num_scalar_prefetch=1,
            grid=(8,),
            in_specs=[pl.BlockSpec((seqs, span, width), lambda j, m: (0, 0, 0), **once)] * 8
            + [pl.BlockSpec(w_blocks[0].shape, lambda j, m: (0, 0, 0), **once)] * 4
            + [
                pl.BlockSpec((1, width), fixed, **once),
                pl.BlockSpec((8, 128), fixed, **once),
                pl.BlockSpec((seqs, span, 128), home),
                pl.BlockSpec((seqs, span, 128), home),
            ]
            + any_space(len(earlier)),
            out_specs=[
                pl.BlockSpec((seqs, span, width), home),
                pl.BlockSpec((seqs, span, width), home),
                pl.BlockSpec((seqs, span, 256), home),
                pl.BlockSpec((seqs, span, 128), home),
                pl.BlockSpec((seqs, span, 128), home),
                pl.BlockSpec((width, 256), fixed),
            ],
        ),
        out_shape=[
            jax.ShapeDtypeStruct((seqs, length, width), bf16),
            jax.ShapeDtypeStruct((seqs, length, width), bf16),
            jax.ShapeDtypeStruct((seqs, length, 256), f32),
            jax.ShapeDtypeStruct((seqs, length, 128), bf16),
            jax.ShapeDtypeStruct((seqs, length, 128), bf16),
            jax.ShapeDtypeStruct((width, 256), bf16),
        ],
        compiler_params=pltpu.CompilerParams(vmem_limit_bytes=40 << 20),
        cost_estimate=pl.CostEstimate(flops=16 * seqs * length * width * 256, bytes_accessed=seqs * length * width * 6, transcendentals=0),
        name="qkv_fwd",
    )(at, *x_blocks, *w_blocks, gain, scales, cosine, sine, *earlier)


def halves_spec(seqs, span, width):
    return pl.BlockSpec((1, seqs, span, width), lambda t, m: ((m[0] ^ t) >> 1, 0, 0, 0))


def store_halves(me, step, value, even_ref, odd_ref):
    odd = ((me ^ step) & 1) == 1

    @pl.when(odd)
    def _():
        odd_ref[...] = value.reshape(odd_ref.shape)

    @pl.when(jnp.logical_not(odd))
    def _():
        even_ref[...] = value.reshape(even_ref.shape)


def ffn_kernel(hidden, padded, at_ref, *refs):
    parts, cot_refs, wd_parts = refs[:8], refs[8:16], refs[16]
    (x_ref, wo_parts, wgu_ref, gain_ref, attn_ref, mid_ref, nm_ref, hid_ref, grads_ref) = refs[17:26]
    gnm_even, gnm_odd, out_even, out_odd, cot_ref, wo_ref, wgu, wd = refs[26:]
    step = pl.program_id(0)

    @pl.when(step == 0)
    def _():
        shard = wo_parts.shape[2]
        part = wd_parts.shape[1] - shard
        wgu[...] = jnp.zeros_like(wgu)
        wgu[:, :hidden] = wgu_ref[:, :hidden]
        wgu[:, padded : padded + hidden] = wgu_ref[:, hidden:]
        wd[hidden:, :] = jnp.zeros((padded - hidden, wd.shape[1]), bf16)
        for f in range(wd_parts.shape[0]):
            wd[f * part : (f + 1) * part, :] = wd_parts[f, :part, :]
            for g in range(8):
                row = (f * 8 + g) * shard
                wo_ref[row : row + shard, :] = wo_parts[g, f]

    for j in range(8):

        @pl.when((at_ref[0] ^ step) == j)
        def _(j=j):
            cot_ref[...] = cot_refs[j][...]

    tile = attn_ref.shape[0] * attn_ref.shape[1]
    width = wo_ref.shape[0]
    for j in range(8):
        at = pl.multiple_of((at_ref[0] ^ j) * 128, 128)
        attn_ref[:, :, pl.ds(at, 128)] = parts[j][...]
    attn = attn_ref[...].reshape(tile, width)
    mid = x_ref[...].reshape(tile, width).astype(f32) + jnp.dot(attn, wo_ref[...], preferred_element_type=f32)
    mid_ref[...] = mid.reshape(mid_ref.shape)
    factor = lax.rsqrt(jnp.mean(mid * mid, axis=-1, keepdims=True) + eps)
    nm = (mid * factor * gain_ref[...]).astype(bf16)
    nm_ref[...] = nm.reshape(nm_ref.shape)
    both = jnp.dot(nm, wgu[...], preferred_element_type=f32)
    gate, up = both[:, :padded], both[:, padded:]
    sigma = jax.nn.sigmoid(gate)
    hid = (gate * sigma * up).astype(bf16)
    hid_ref[...] = hid.reshape(hid_ref.shape)
    grad_hidden = dot_nt(cot_ref[...].reshape(tile, width), wd[...])
    grad_gate = (grad_hidden * up * sigma * (1.0 + gate * (1.0 - sigma))).astype(bf16)
    grad_up = (grad_hidden * gate * sigma).astype(bf16)
    grads = jnp.concatenate([grad_gate, grad_up], axis=1)
    grads_ref[...] = grads.reshape(grads_ref.shape)
    store_halves(at_ref[0], step, dot_nt(grads, wgu[...]).astype(bf16), gnm_even, gnm_odd)
    out = jnp.dot(hid, wd[...], preferred_element_type=f32).astype(bf16)
    store_halves(at_ref[0], step, out, out_even, out_odd)


def ffn(at, parts, cot_blocks, wd_parts, x, wo_parts, w_gate_up, gain):
    seqs, length, width = x.shape
    span = length // 8
    hidden = w_gate_up.shape[1] // 2
    padded = -(-hidden // 128) * 128
    home = lambda t, m: (0, t, 0)
    fixed = lambda t, m: (0, 0)
    once = dict(pipeline_mode=pl.Buffered(1))
    tokens = lambda cols: pl.BlockSpec((seqs, span, cols), home)
    shape = lambda cols, kind: jax.ShapeDtypeStruct((seqs, length, cols), kind)
    half = jax.ShapeDtypeStruct((4, seqs, span, width), bf16)
    return pl.pallas_call(
        functools.partial(ffn_kernel, hidden, padded),
        grid_spec=pltpu.PrefetchScalarGridSpec(
            num_scalar_prefetch=1,
            grid=(8,),
            in_specs=[tokens(128)] * 8
            + [pl.BlockSpec((seqs, span, width), lambda t, m: (0, 0, 0), **once)] * 8
            + [pl.BlockSpec(wd_parts.shape, lambda t, m: (0, 0, 0), **once)]
            + [
                tokens(width),
                pl.BlockSpec(wo_parts.shape, lambda t, m: (0, 0, 0, 0), **once),
                pl.BlockSpec((width, 2 * hidden), fixed, **once),
                pl.BlockSpec((1, width), fixed, **once),
            ],
            out_specs=[tokens(width), tokens(width), tokens(width), tokens(padded), tokens(2 * padded)]
            + [halves_spec(seqs, span, width)] * 4
            + [tokens(width), pl.BlockSpec((width, width), fixed)],
            scratch_shapes=[pltpu.VMEM((width, 2 * padded), bf16), pltpu.VMEM((padded, width), bf16)],
        ),
        out_shape=[shape(width, bf16), shape(width, f32), shape(width, bf16), shape(padded, bf16), shape(2 * padded, bf16)]
        + [half] * 4
        + [shape(width, bf16), jax.ShapeDtypeStruct((width, width), bf16)],
        compiler_params=pltpu.CompilerParams(vmem_limit_bytes=60 << 20),
        cost_estimate=pl.CostEstimate(flops=seqs * length * width * (2 * width + 12 * padded), bytes_accessed=seqs * length * width * 20, transcendentals=seqs * length * padded),
        name="ffn",
    )(at, *parts, *cot_blocks, wd_parts, x, wo_parts, w_gate_up, gain)


def product_kernel(cuts, left_ref, right_ref, *refs):
    out_ref, total = refs[-2:]
    step = pl.program_id(0)
    value = dot_tn(left_ref[...], right_ref[...])

    @pl.when(step == 0)
    def _():
        total[...] = value

    @pl.when(step > 0)
    def _():
        total[...] += value

    @pl.when(step == pl.num_programs(0) - 1)
    def _():
        size, blocks, _, count, _ = out_ref.shape
        for f in range(size):
            for g in range(blocks):
                row = (f * blocks + g) * count
                for i, (begin, end) in enumerate(cuts):
                    out_ref[f, g, i] = total[row : row + count, begin:end].astype(bf16)


def product(left, right, split, cuts, earlier=()):
    rows = left.shape[0]
    shape = (split[0], split[1], len(cuts), split[2], cuts[0][1] - cuts[0][0])
    tile = 512
    at = lambda i: (i, 0)
    return pl.pallas_call(
        functools.partial(product_kernel, cuts),
        grid=(rows // tile,),
        in_specs=[pl.BlockSpec((tile, left.shape[1]), at), pl.BlockSpec((tile, right.shape[1]), at)]
        + any_space(len(earlier)),
        out_specs=pl.BlockSpec(shape, lambda i: (0, 0, 0, 0, 0)),
        out_shape=jax.ShapeDtypeStruct(shape, bf16),
        scratch_shapes=[pltpu.VMEM((left.shape[1], right.shape[1]), f32)],
        compiler_params=pltpu.CompilerParams(vmem_limit_bytes=48 << 20),
        cost_estimate=pl.CostEstimate(flops=2 * rows * left.shape[1] * right.shape[1], bytes_accessed=2 * rows * (left.shape[1] + right.shape[1]), transcendentals=0),
        name="product",
    )(left, right, *earlier)


def mid_kernel(at_ref, mid_ref, cot_ref, gain_ref, wo_ref, even_ref, got_ref, *refs):
    grad_ref, half_ref, out_ref = refs[-3:]
    seqs, span, width = cot_ref.shape
    grad_nm = even_ref[0].astype(f32) + got_ref[0].astype(f32)
    for part_ref in refs[:3]:
        grad_nm += part_ref[...].astype(f32)
    grad_nm = grad_nm.reshape(seqs * span, width)
    mid = mid_ref[...].reshape(seqs * span, width)
    factor = lax.rsqrt(jnp.mean(mid * mid, axis=-1, keepdims=True) + eps)
    normed = mid * factor
    scaled = grad_nm * gain_ref[...]
    grad = cot_ref[...].reshape(seqs * span, width).astype(f32) + factor * (
        scaled - normed * jnp.mean(scaled * normed, axis=-1, keepdims=True)
    )
    grad_ref[...] = grad
    half = grad.astype(bf16)
    half_ref[...] = half
    out = dot_nt(half, wo_ref[...]).astype(bf16)
    for g in range(8):
        out_ref[g] = out[:, g * 128 : (g + 1) * 128].reshape(seqs, span, 128)


def mid_bwd(at, mid, cot, gain, w_out, even, stages, earlier):
    seqs, span, width = cot.shape
    first = lambda *s: pl.BlockSpec((1,) + s, lambda i, m: (0,) * (len(s) + 1))
    full = lambda *s: pl.BlockSpec(s, lambda i, m: (0,) * len(s))
    rows = seqs * span
    return pl.pallas_call(
        mid_kernel,
        grid_spec=pltpu.PrefetchScalarGridSpec(
            num_scalar_prefetch=1,
            grid=(1,),
            in_specs=[
                pl.BlockSpec((seqs, span, width), lambda i, m: (0, m[0], 0)),
                full(seqs, span, width),
                full(1, width),
                full(width, width),
                first(seqs, span, width),
                first(seqs, span, width),
                full(seqs, span, width),
                full(seqs, span, width),
                full(seqs, span, width),
            ]
            + any_space(len(earlier)),
            out_specs=[full(rows, width), full(rows, width), full(8, seqs, span, 128)],
        ),
        out_shape=[
            jax.ShapeDtypeStruct((rows, width), f32),
            jax.ShapeDtypeStruct((rows, width), bf16),
            jax.ShapeDtypeStruct((8, seqs, span, 128), bf16),
        ],
        compiler_params=pltpu.CompilerParams(vmem_limit_bytes=40 << 20),
        cost_estimate=pl.CostEstimate(flops=2 * rows * width * width, bytes_accessed=rows * width * 20, transcendentals=0),
        name="mid_bwd",
    )(at, mid, cot, gain, w_out, even, *stages, *earlier)


def qkv_bwd_kernel(at_ref, dq_ref, dkv_ref, raw_ref, nm_ref, w_ref, scale_ref, cos_ref, sin_ref, *refs):
    even_ref, odd_ref, dw_ref, dscale_ref, dw_acc = refs[-5:]
    step = pl.program_id(0)
    seqs, span, width = nm_ref.shape
    tile = seqs * span

    @pl.when(step == 0)
    def _():
        dw_acc[...] = jnp.zeros_like(dw_acc)
        dscale_ref[...] = jnp.zeros_like(dscale_ref)

    cos, sin = cos_ref[...].reshape(tile, 128), sin_ref[...].reshape(tile, 128)
    def back(raw, grad, scale):
        inv = lax.rsqrt(head_average(raw * raw) + eps)
        normed = raw * inv
        turned = grad * cos + half_turn(grad * sin, True)
        grad_normed = turned * scale
        grad_raw = inv * (grad_normed - normed * head_average(grad_normed * normed))
        return grad_raw, jnp.sum(turned * normed, axis=0, keepdims=True)

    raw = raw_ref[...].reshape(tile, 256)
    grad_kv = dkv_ref[...].reshape(tile, 128)
    dq, q_scale = back(raw[:, :128], dq_ref[...].reshape(tile, 128), scale_ref[0:1, :])
    dkv, k_scale = back(raw[:, 128:], grad_kv, scale_ref[1:2, :])
    dkv = jnp.where(lane_index(tile) < HD, dkv, grad_kv)
    grad = jnp.concatenate([dq.astype(bf16), dkv.astype(bf16)], axis=1)
    dscale_ref[0:1, :] += q_scale
    dscale_ref[1:2, :] += k_scale
    store_halves(at_ref[0], step, dot_nt(grad, w_ref[...]).astype(bf16), even_ref, odd_ref)
    dw_acc[...] += dot_tn(nm_ref[...].reshape(tile, width), grad)

    @pl.when(step == pl.num_programs(0) - 1)
    def _():
        dw_ref[...] = dw_acc[...].astype(bf16)


def qkv_bwd(at, dq, dkv, raw, nm, w_qkv, scales, cosine, sine, earlier):
    seqs, length, width = nm.shape
    span = length // 8
    tokens = lambda cols: pl.BlockSpec((seqs, span, cols), lambda t, m: (0, t, 0))
    fixed = lambda t, m: (0, 0)
    half = jax.ShapeDtypeStruct((4, seqs, span, width), bf16)
    return pl.pallas_call(
        qkv_bwd_kernel,
        grid_spec=pltpu.PrefetchScalarGridSpec(
            num_scalar_prefetch=1,
            grid=(8,),
            in_specs=[
                tokens(128),
                tokens(128),
                tokens(256),
                tokens(width),
                pl.BlockSpec((width, 256), fixed),
                pl.BlockSpec((8, 128), fixed),
                tokens(128),
                tokens(128),
            ]
            + any_space(len(earlier)),
            out_specs=[halves_spec(seqs, span, width)] * 2
            + [pl.BlockSpec((width, 256), fixed), pl.BlockSpec((8, 128), fixed)],
            scratch_shapes=[pltpu.VMEM((width, 256), f32)],
        ),
        out_shape=[
            half,
            half,
            jax.ShapeDtypeStruct((width, 256), bf16),
            jax.ShapeDtypeStruct((8, 128), f32),
        ],
        compiler_params=pltpu.CompilerParams(vmem_limit_bytes=48 << 20),
        cost_estimate=pl.CostEstimate(flops=16 * seqs * length * width * 256, bytes_accessed=seqs * length * width * 6, transcendentals=0),
        name="qkv_bwd",
    )(at, dq, dkv, raw, nm, w_qkv, scales, cosine, sine, *earlier)


def plain_body(
    block_input,
    positions,
    cotangent,
    attention_gain,
    query_weight,
    key_weight,
    value_weight,
    query_gain,
    key_gain,
    output_weight,
    feedforward_gain,
    gate_weight,
    up_weight,
    down_weight,
):
    seq_count, span, width = block_input.shape
    groups = lax.axis_size("seq")
    size = lax.axis_size("fsdp")
    me = lax.axis_index("seq")
    length = span * groups
    rows = seq_count * length
    own_rows = seq_count * span
    shard = query_weight.shape[0]
    heads = H // groups
    kv_heads = max(1, KV // groups)
    copies = max(1, groups // KV)
    q_cols, k_cols = heads * HD, kv_heads * HD
    qkv_cols = q_cols + 2 * k_cols
    part = gate_weight.shape[1] // (groups * size)
    hidden_cols = part * size

    x_full = gather_seq(block_input, 1)

    def columns(weight, col_copies):
        shaped = weight.reshape(shard, -1, 1, HD)
        shaped = jnp.broadcast_to(shaped, (shard, shaped.shape[1], col_copies, HD))
        return shaped.reshape(shard, groups, -1)

    packed = jnp.concatenate(
        [
            columns(query_weight, 1),
            columns(key_weight, copies),
            columns(value_weight, copies),
        ],
        axis=2,
    ).transpose(1, 0, 2)
    gains = jnp.concatenate([attention_gain, feedforward_gain])
    gain_rows = jnp.zeros((16, qkv_cols), bf16).at[0, : 2 * shard].set(gains)
    packed = jnp.concatenate(
        [packed, jnp.broadcast_to(gain_rows[None], (groups, 16, qkv_cols))], axis=1
    )
    packed = gather_line(spread(packed))
    w_qkv = packed[:, :, :shard, :].reshape(width, qkv_cols)
    gain_one = packed[:, :, shard, :shard].reshape(width).astype(f32)
    gain_two = packed[:, :, shard, shard : 2 * shard].reshape(width).astype(f32)

    out_full = lax.all_gather(output_weight, ("fsdp", "seq"), axis=0, tiled=True)

    def ff_columns(weight):
        shaped = weight.reshape(shard, size, groups, part)
        return shaped.transpose(2, 0, 1, 3).reshape(groups, shard, hidden_cols)

    w_gate_up = gather_line(
        spread(jnp.concatenate([ff_columns(gate_weight), ff_columns(up_weight)], axis=2))
    ).reshape(width, 2 * hidden_cols)
    w_gate = w_gate_up[:, :hidden_cols]
    w_up = w_gate_up[:, hidden_cols:]
    w_down = gather_line(down_weight).reshape(hidden_cols, width)

    cot_full = gather_seq(cotangent, 1).reshape(rows, width)

    residual_in = x_full.reshape(rows, width).astype(f32)
    factor_one = inv_rms(residual_in)
    normed_in = (residual_in * factor_one * gain_one).astype(bf16)
    qkv_raw = matmul(normed_in, w_qkv)
    query_raw = qkv_raw[:, :q_cols]
    key_raw = qkv_raw[:, q_cols : q_cols + k_cols]
    value_rows = qkv_raw[:, q_cols + k_cols :].astype(bf16)
    cosine, sine = rope_tables(positions.reshape(rows), HD)
    query_scale = query_gain.astype(f32)
    key_scale = key_gain.astype(f32)

    def query_side(raw_rows, gain_row):
        return head_prep(raw_rows, gain_row, cosine, sine, heads)

    def key_side(raw_rows, gain_row):
        return head_prep(raw_rows, gain_row, cosine, sine, kv_heads)

    def head_view(packed_rows):
        shaped = packed_rows.reshape(seq_count, length, -1, HD)
        return jnp.repeat(shaped, heads // shaped.shape[2], axis=2)

    queries = query_side(query_raw, query_scale).astype(bf16).reshape(seq_count, length, heads, HD)
    keys = head_view(key_side(key_raw, key_scale).astype(bf16))
    values = head_view(value_rows)
    doc_start = jnp.arange(length, dtype=jnp.int32)[None, :] - positions
    outputs, log_totals = jax.vmap(attend_fwd)(queries, keys, values, doc_start)

    attn_full = gather_seq(outputs.reshape(seq_count, length, q_cols), 2)
    attn_rows = attn_full.reshape(rows, width)
    residual_mid = residual_in + matmul(attn_rows, out_full)
    factor_two = inv_rms(residual_mid)
    normed_mid = (residual_mid * factor_two * gain_two).astype(bf16)

    def own(array):
        shaped = array.reshape(seq_count, length, -1)
        return lax.dynamic_slice_in_dim(shaped, me * span, span, 1).reshape(own_rows, -1)

    gate_rows = matmul(normed_mid, w_gate)
    up_rows = matmul(normed_mid, w_up)
    sigma = jax.nn.sigmoid(gate_rows)
    hidden = (gate_rows * sigma * up_rows).astype(bf16)
    grad_hidden = matmul_nt(cot_full, w_down)
    grad_gate = (grad_hidden * up_rows * sigma * (1.0 + gate_rows * (1.0 - sigma))).astype(bf16)
    grad_up = (grad_hidden * gate_rows * sigma).astype(bf16)
    grad_normed_part = (matmul_nt(grad_gate, w_gate) + matmul_nt(grad_up, w_up)).astype(bf16)
    grad_normed_mid = reduce_seq(grad_normed_part.reshape(seq_count, length, width), 1)
    grad_normed_mid = grad_normed_mid.reshape(own_rows, width)

    residual_own = own(residual_mid)
    cot_rows = cotangent.reshape(own_rows, width).astype(f32)
    grad_mid = cot_rows + norm_bwd(residual_own, own(factor_two), gain_two, grad_normed_mid)
    grad_mid_half = grad_mid.astype(bf16)
    grad_attn_out = matmul_nt(grad_mid_half, out_full).astype(bf16)
    grad_heads = lax.all_to_all(
        grad_attn_out.reshape(seq_count, span, width), "seq", split_axis=2, concat_axis=1, tiled=True
    )

    grad_query_heads, grad_key_heads, grad_value_heads = jax.vmap(attend_bwd)(
        queries,
        keys,
        values,
        outputs,
        log_totals,
        grad_heads.reshape(seq_count, length, heads, HD),
        doc_start,
    )

    def fold(packed_rows):
        shaped = packed_rows.reshape(rows, kv_heads, -1, HD).astype(f32)
        return jnp.sum(shaped, axis=2).reshape(rows, k_cols)

    _, query_back = jax.vjp(query_side, query_raw, query_scale)
    grad_query_raw, query_gain_term = query_back(grad_query_heads.reshape(rows, q_cols).astype(f32))
    _, key_back = jax.vjp(key_side, key_raw, key_scale)
    grad_key_raw, key_gain_term = key_back(fold(grad_key_heads))
    grad_qkv = jnp.concatenate(
        [
            grad_query_raw.astype(bf16),
            grad_key_raw.astype(bf16),
            fold(grad_value_heads).astype(bf16),
        ],
        axis=1,
    )
    grad_in_part = matmul_nt(grad_qkv, w_qkv).astype(bf16)
    grad_normed_in = reduce_seq(grad_in_part.reshape(seq_count, length, width), 1)
    grad_normed_in = grad_normed_in.reshape(own_rows, width)
    own_in = block_input.reshape(own_rows, width).astype(f32)
    input_grad = (
        (grad_mid + norm_bwd(own_in, inv_rms(own_in), gain_one, grad_normed_in))
        .astype(bf16)
        .reshape(seq_count, span, width)
    )

    result_part = matmul(hidden, w_down).astype(bf16).reshape(seq_count, length, width)
    block_output = (
        (residual_own + reduce_seq(result_part, 1).reshape(own_rows, width))
        .astype(bf16)
        .reshape(seq_count, span, width)
    )

    down_grad = reduce_line(matmul_tn(hidden, cot_full).reshape(size, part, width))
    gate_up_term = matmul_tn(normed_mid, jnp.concatenate([grad_gate, grad_up], axis=1))
    gate_up_term = reduce_line(gate_up_term.reshape(size, groups * shard, 2 * hidden_cols))
    gate_up_home = spread(gate_up_term.astype(bf16).reshape(groups, shard, 2 * hidden_cols))

    def ff_home(columns_home):
        shaped = columns_home.astype(f32).reshape(groups, shard, size, part)
        return shaped.transpose(1, 2, 0, 3).reshape(shard, groups * size * part)

    gate_grad = ff_home(gate_up_home[:, :, :hidden_cols])
    up_grad = ff_home(gate_up_home[:, :, hidden_cols:])

    output_term = matmul_tn(own(attn_rows), grad_mid_half).astype(bf16)
    output_grad = lax.psum_scatter(
        output_term, ("fsdp", "seq"), scatter_dimension=0, tiled=True
    ).astype(f32)

    qkv_term = reduce_line(matmul_tn(normed_in, grad_qkv).reshape(size, groups * shard, qkv_cols))
    qkv_home = spread(qkv_term.astype(bf16).reshape(groups, shard, qkv_cols)).astype(f32)

    def home(block, col_copies):
        shaped = block.transpose(1, 0, 2).reshape(shard, -1, col_copies, HD)
        return jnp.sum(shaped, axis=2).reshape(shard, -1)

    query_grad = home(qkv_home[:, :, :q_cols], 1)
    key_grad = home(qkv_home[:, :, q_cols : q_cols + k_cols], copies)
    value_grad = home(qkv_home[:, :, q_cols + k_cols :], copies)

    def weighted(weight, grad):
        return jnp.sum(weight.astype(f32) * grad, axis=1)

    gain_one_grad = (
        weighted(query_weight, query_grad)
        + weighted(key_weight, key_grad)
        + weighted(value_weight, value_grad)
    ) / attention_gain.astype(f32)
    gain_two_grad = (
        weighted(gate_weight, gate_grad) + weighted(up_weight, up_grad)
    ) / feedforward_gain.astype(f32)

    head_gains = sum_everywhere(jnp.concatenate([query_gain_term, key_gain_term])[None])[0]
    return (
        block_output,
        input_grad,
        gain_one_grad,
        query_grad,
        key_grad,
        value_grad,
        head_gains[:HD],
        head_gains[HD:],
        output_grad,
        gain_two_grad,
        gate_grad,
        up_grad,
        down_grad,
    )


def after(array, earlier):
    first = earlier.reshape(-1)[0] if earlier.ndim == 1 else earlier[(0,) * earlier.ndim]
    return array + jnp.minimum(jnp.abs(first), 0).astype(array.dtype)


def swap_line(array, mask):
    size = lax.axis_size("fsdp")
    return lax.ppermute(array, "fsdp", [(i, i ^ mask) for i in range(size)])


def line_blocks(block):
    return [block] + [swap_line(block, m) for m in (1, 2, 3)]


def line_parts(block_of):
    me = lax.axis_index("fsdp")
    return [swap_line(block_of(me ^ m), m) for m in (1, 2, 3)]


def add_up(own, others):
    total = own.astype(f32)
    for other in others:
        total = total + other.astype(f32)
    return total


def reduce_stages(even, odd, earlier=None):
    got = swap(odd, 1)

    def sent(i):
        total = even[i].astype(f32) + got[i].astype(f32)
        return swap((total if earlier is None else after(total, earlier)).astype(bf16), 2 * i)

    return got, sent(1), sent(2), sent(3)


def own_sum(even, stages):
    total = even[0].astype(f32) + stages[0][0].astype(f32)
    for part in stages[1:]:
        total = total + part.astype(f32)
    return total


def body(
    block_input,
    positions,
    cotangent,
    attention_gain,
    query_weight,
    key_weight,
    value_weight,
    query_gain,
    key_gain,
    output_weight,
    feedforward_gain,
    gate_weight,
    up_weight,
    down_weight,
):
    seqs, span, width = block_input.shape
    groups = lax.axis_size("seq")
    size = lax.axis_size("fsdp")
    if not (groups == 8 and size == 4 and seqs % 2 == 0 and span % 64 == 0):
        return plain_body(
            block_input,
            positions,
            cotangent,
            attention_gain,
            query_weight,
            key_weight,
            value_weight,
            query_gain,
            key_gain,
            output_weight,
            feedforward_gain,
            gate_weight,
            up_weight,
            down_weight,
        )
    me = lax.axis_index("seq")
    me_line = lax.axis_index("fsdp")
    at = jnp.stack([me, me_line]).astype(jnp.int32)
    length = span * groups
    rows = seqs * length
    own_rows = seqs * span
    shard = query_weight.shape[0]
    part = gate_weight.shape[1] // (groups * size)
    hidden_cols = part * size
    padded = -(-hidden_cols // 128) * 128

    gains = jnp.concatenate([attention_gain, feedforward_gain])
    gains = jnp.zeros((shard, 128), bf16).at[0, : 2 * shard].set(gains)
    packed = spread(
        pack_columns(gate_weight, up_weight, query_weight, key_weight, value_weight, gains, groups, part)
    )
    x_blocks = partner_blocks(block_input)
    qkv_blocks = line_blocks(packed[:, :, 2 * hidden_cols :])
    gains = [block[:, 0, 256 : 256 + 2 * shard].astype(f32) for block in qkv_blocks]
    gains = jnp.stack(
        [sum(jnp.where((me_line ^ m) == f, gains[m], 0.0) for m in range(size)) for f in range(size)]
    )
    gain_one = gains[:, :, :shard].reshape(1, width)
    gain_two = gains[:, :, shard:].reshape(1, width)
    down_parts = lax.all_gather(
        jnp.concatenate([down_weight, output_weight], axis=0), "fsdp", axis=0, tiled=False
    )
    wo_parts = lax.all_gather(down_parts[:, part:], "seq", axis=0, tiled=False)
    w_gate_up = packed[:, :, : 2 * hidden_cols]
    for block in qkv_blocks[1:]:
        w_gate_up = after(w_gate_up, block)
    w_gate_up = lax.all_gather(w_gate_up, "fsdp", axis=0, tiled=False).reshape(width, 2 * hidden_cols)
    cot_blocks = {0: cotangent}
    for mask in (2, 4):
        cot_blocks[mask] = swap(after(cotangent, x_blocks[6]), mask)
    cot_blocks[6] = swap(cot_blocks[2], 4)
    for mask in (0, 2, 4, 6):
        cot_blocks[mask + 1] = swap(cot_blocks[mask], 1)

    inverse = rope_base ** (-(jnp.arange(HD // 2, dtype=f32) * 2.0) / HD)
    angles = positions.astype(f32)[:, :, None] * jnp.tile(inverse, 4)[None, None, :]
    cosine, sine = jnp.cos(angles), jnp.sin(angles)
    scales = jnp.concatenate(
        [jnp.tile(query_gain, 2)[None], jnp.tile(key_gain, 2)[None], jnp.zeros((6, 128), bf16)]
    ).astype(f32)
    starts = jnp.arange(length, dtype=jnp.int32)[None, :] - positions
    x_full, normed_in, qkv_raw, q_rows, kv_rows, w_qkv = qkv_fwd(
        at, x_blocks, qkv_blocks, gain_one, scales, cosine, sine, []
    )
    starts_wide = jnp.broadcast_to(starts[:, :, None], (seqs, length, 128))
    outputs, totals = attn_fwd(q_rows, kv_rows, starts_wide, span, [cot_blocks[2], cot_blocks[4]])

    (attn_rows, residual_mid, normed_mid, hidden, ff_grads, gnm_even, gnm_odd, out_even, out_odd, cot_full, w_out) = ffn(
        at,
        partner_blocks(outputs),
        [cot_blocks[j] for j in range(8)],
        down_parts,
        x_full,
        wo_parts,
        w_gate_up,
        gain_two,
    )
    flat = lambda array: array.reshape(rows, -1)

    mid_stages = reduce_stages(gnm_even, gnm_odd)
    cuts = ((0, hidden_cols), (padded, padded + hidden_cols))
    gate_up_term = product(flat(normed_mid), flat(ff_grads), (size, groups, shard), cuts)
    waits = [mid_stages[0], gate_up_term]
    down_term = product(flat(hidden), flat(cot_full), (size, 1, part), ((0, width),), waits)
    grad_mid, grad_mid_half, grad_attn_out = mid_bwd(
        at, residual_mid, cotangent, gain_two, w_out, gnm_even, mid_stages, [down_term, gate_up_term]
    )
    grad_heads = spread(grad_attn_out)

    def block_rows(term, f, count):
        return lax.dynamic_slice_in_dim(term, f * count, count, term.ndim - 2)

    gate_up_sum = lax.psum_scatter(gate_up_term, "fsdp", scatter_dimension=0, tiled=False)
    down_sum = lax.psum_scatter(down_term, "fsdp", scatter_dimension=0, tiled=False)
    attn_own = lax.dynamic_slice_in_dim(attn_rows, me * span, span, 1).reshape(own_rows, width)
    output_term = matmul_tn(attn_own, grad_mid_half).astype(bf16)
    output_term = output_term.reshape(size, groups, shard, width).transpose(1, 0, 2, 3)
    output_term = lax.psum_scatter(output_term, "seq", scatter_dimension=0, tiled=False)
    output_sum = lax.psum_scatter(output_term, "fsdp", scatter_dimension=0, tiled=False)
    out_stages = reduce_stages(out_even, out_odd, grad_heads)
    gate_up_home = spread(gate_up_sum)

    totals_row = jnp.stack([totals[:, :, 0], totals[:, :, HD]], axis=1)
    totals_row = jnp.concatenate([totals_row, jnp.zeros((seqs, 6, length), f32)], axis=1)
    starts_row = jnp.broadcast_to(starts[:, None, :], (seqs, 8, length))
    grad_q, grad_kv = attn_bwd(
        q_rows, kv_rows, grad_heads, outputs, totals_row, starts_row, span, [out_stages[0]]
    )
    gin_even, gin_odd, qkv_term, head_gains = qkv_bwd(
        at, grad_q, grad_kv, qkv_raw, normed_in, w_qkv, scales, cosine, sine,
        [*out_stages[1:], gate_up_home, down_sum]
    )
    in_stages = reduce_stages(gin_even, gin_odd)
    own_in = block_input.reshape(own_rows, width).astype(f32)
    grad_normed_in = own_sum(gin_even, in_stages).reshape(own_rows, width)
    input_grad = (
        (grad_mid + norm_bwd(own_in, inv_rms(own_in), gain_one, grad_normed_in))
        .astype(bf16)
        .reshape(seqs, span, width)
    )

    def two_terms(array):
        high = array.astype(bf16)
        low = (array - high.astype(f32)).astype(bf16)
        return jnp.concatenate([high, low, jnp.zeros((14, array.shape[1]), bf16)], axis=0)

    gain_rows = two_terms(head_gains[:2].reshape(1, 256))

    def sent_rows(f):
        block = after(block_rows(qkv_term, f, groups * shard), in_stages[0])
        return jnp.concatenate([block, gain_rows], axis=0)

    qkv_parts = line_parts(sent_rows)
    qkv_sum = add_up(sent_rows(me_line), qkv_parts)
    gain_rows = two_terms(qkv_sum[-16:-15] + qkv_sum[-15:-14])
    qkv_sum = qkv_sum[:-16].astype(bf16).reshape(groups, shard, 4 * HD)
    gain_rows = jnp.broadcast_to(gain_rows[None], (groups, *gain_rows.shape))
    query_grad, key_grad, value_grad, gain_one_sum, head_gains = unpack_heads(
        spread(jnp.concatenate([qkv_sum, gain_rows], axis=1)), query_weight, key_weight, value_weight
    )
    head_gains = (head_gains[0] + head_gains[1]).reshape(2, 128)

    residual_own = lax.dynamic_slice_in_dim(residual_mid, me * span, span, 1)
    block_output = after(residual_own + own_sum(out_even, out_stages), qkv_parts[0]).astype(bf16)
    down_grad = after(down_sum.astype(f32), qkv_parts[0]).reshape(part, width)
    output_grad = after(output_sum.astype(f32), qkv_parts[0])
    gate_grad, up_grad, gain_two_sum = unpack_columns(gate_up_home, gate_weight, up_weight, part, qkv_parts[0])

    gain_one_grad = gain_one_sum[:, 0] / attention_gain.astype(f32)
    gain_two_grad = gain_two_sum[:, 0] / feedforward_gain.astype(f32)

    return (
        block_output,
        input_grad,
        gain_one_grad,
        query_grad,
        key_grad,
        value_grad,
        head_gains[0, :HD] + head_gains[0, HD:],
        head_gains[1, :HD],
        output_grad,
        gain_two_grad,
        gate_grad,
        up_grad,
        down_grad,
    )


def solution(mesh):
    shards = P(("fsdp", "seq"), None)
    vector = P(("fsdp", "seq"))
    tokens = P("fsdp", "seq", None)
    return jax.shard_map(
        body,
        mesh=mesh,
        in_specs=(
            tokens,
            P("fsdp", None),
            tokens,
            vector,
            shards,
            shards,
            shards,
            P(),
            P(),
            shards,
            vector,
            shards,
            shards,
            shards,
        ),
        out_specs=(
            tokens,
            tokens,
            vector,
            shards,
            shards,
            shards,
            P(),
            P(),
            shards,
            vector,
            shards,
            shards,
            shards,
        ),
        check_vma=False,
    )
```

```python
import functools

import jax
import jax.numpy as jnp
from jax import lax
from jax.experimental import pallas as pl
from jax.experimental.pallas import tpu as pltpu
from jax.sharding import PartitionSpec as P

H = 16
KV = 8
HD = 64

rope_base = 1000000.0
eps = 1e-05
masked = -1e30
f32 = jnp.float32
bf16 = jnp.bfloat16


def contract(formula, left, right):
    return jnp.einsum(formula, left, right, preferred_element_type=f32)


def matmul(left, right):
    return jnp.dot(left, right, preferred_element_type=f32)


def matmul_nt(left, right):
    return lax.dot_general(left, right, (((1,), (1,)), ((), ())), preferred_element_type=f32)


def matmul_tn(left, right):
    return lax.dot_general(left, right, (((0,), (0,)), ((), ())), preferred_element_type=f32)


def rope_tables(places, head_width):
    half_width = head_width // 2
    inverse = rope_base ** (-(jnp.arange(half_width, dtype=f32) * 2.0) / head_width)
    angles = places.astype(f32)[:, None] * inverse[None, :]
    return (jnp.cos(angles)[:, None, :], jnp.sin(angles)[:, None, :])


def head_prep(raw_rows, gain_row, cosine, sine, head_count):
    row_count = raw_rows.shape[0]
    split_rows = raw_rows.reshape(row_count, head_count, -1)
    factor = lax.rsqrt(jnp.mean(split_rows * split_rows, axis=-1, keepdims=True) + eps)
    normed = split_rows * factor * gain_row
    half_width = normed.shape[-1] // 2
    lower = normed[..., :half_width]
    upper = normed[..., half_width:]
    turned = jnp.concatenate(
        [lower * cosine - upper * sine, upper * cosine + lower * sine], axis=-1
    )
    return turned.reshape(row_count, -1)


def inv_rms(values):
    return lax.rsqrt(jnp.mean(values * values, axis=-1, keepdims=True) + eps)


def norm_bwd(values, factor, gain_row, grad_result):
    normed = values * factor
    grad_normed = grad_result * gain_row
    return factor * (
        grad_normed - normed * jnp.mean(grad_normed * normed, axis=-1, keepdims=True)
    )


def masked_scores(queries, key_rows, doc_start, begin_row, end_row, scaling):
    query_index = jnp.arange(begin_row, end_row, dtype=jnp.int32)
    key_index = jnp.arange(end_row, dtype=jnp.int32)
    allowed = (key_index[None, :] <= query_index[:, None]) & (
        key_index[None, :] >= doc_start[begin_row:end_row, None]
    )
    scores = contract("qhd,khd->hqk", queries[begin_row:end_row], key_rows[:end_row]) * scaling
    return jnp.where(allowed[None, :, :], scores, masked)


def attend_fwd(queries, key_rows, value_rows, doc_start):
    seq_length, head_count, head_width = queries.shape
    block_rows = min(512, seq_length)
    scaling = head_width ** (-0.5)
    out_blocks = []
    total_blocks = []
    for begin_row in range(0, seq_length, block_rows):
        end_row = begin_row + block_rows
        scores = masked_scores(queries, key_rows, doc_start, begin_row, end_row, scaling)
        largest = jnp.max(scores, axis=-1, keepdims=True)
        log_total = largest + jnp.log(jnp.sum(jnp.exp(scores - largest), axis=-1, keepdims=True))
        attn_prob = jnp.exp(scores - log_total).astype(bf16)
        out_blocks.append(contract("hqk,khd->qhd", attn_prob, value_rows[:end_row]).astype(bf16))
        total_blocks.append(log_total[..., 0])
    return (jnp.concatenate(out_blocks, axis=0), jnp.concatenate(total_blocks, axis=1))


def attend_bwd(queries, key_rows, value_rows, outputs, log_totals, grad_result, doc_start):
    seq_length, head_count, head_width = queries.shape
    block_rows = min(512, seq_length)
    scaling = head_width ** (-0.5)
    carried = jnp.sum(grad_result.astype(f32) * outputs.astype(f32), axis=-1).T
    grad_query = []
    grad_key = jnp.zeros((seq_length, head_count, head_width), f32)
    grad_value = jnp.zeros((seq_length, head_count, head_width), f32)
    for begin_row in range(0, seq_length, block_rows):
        end_row = begin_row + block_rows
        scores = masked_scores(queries, key_rows, doc_start, begin_row, end_row, scaling)
        attn_prob = jnp.exp(scores - log_totals[:, begin_row:end_row, None])
        prob_half = attn_prob.astype(bf16)
        grad_rows = grad_result[begin_row:end_row]
        grad_value = grad_value.at[:end_row].add(contract("hqk,qhd->khd", prob_half, grad_rows))
        grad_prob = contract("qhd,khd->hqk", grad_rows, value_rows[:end_row])
        grad_score = (
            attn_prob * (grad_prob - carried[:, begin_row:end_row, None]) * scaling
        ).astype(bf16)
        grad_query.append(contract("hqk,khd->qhd", grad_score, key_rows[:end_row]))
        grad_key = grad_key.at[:end_row].add(
            contract("hqk,qhd->khd", grad_score, queries[begin_row:end_row])
        )
    return (
        jnp.concatenate(grad_query, axis=0).astype(bf16),
        grad_key.astype(bf16),
        grad_value.astype(bf16),
    )


def swap(array, mask):
    groups = lax.axis_size("seq")
    return lax.ppermute(array, "seq", [(i, i ^ mask) for i in range(groups)])


def partner_blocks(block, direct=False):
    got = {0: block, 2: swap(block, 2), 4: swap(block, 4)}
    got[6] = swap(block, 6) if direct else swap(got[4], 2)
    for mask in (0, 2, 4, 6):
        got[mask + 1] = swap(got[mask], 1)
    return [got[j] for j in range(8)]


def gather_seq(block, axis):
    if lax.axis_size("seq") != 8 or block.shape[0] % 2:
        return lax.all_gather(block, "seq", axis=axis, tiled=True)
    me = lax.axis_index("seq")
    width = block.shape[axis]
    shape = list(block.shape)
    shape[axis] = width * 8
    whole = jnp.zeros(shape, block.dtype)
    for j, part in enumerate(partner_blocks(block)):
        whole = lax.dynamic_update_slice_in_dim(whole, part, (me ^ j) * width, axis)
    return whole


def reduce_seq(partial, axis):
    groups = lax.axis_size("seq")
    width = partial.shape[axis] // groups
    if groups != 8 or partial.shape[0] % 2:
        return lax.psum_scatter(partial, "seq", scatter_dimension=axis, tiled=True).astype(f32)
    me = lax.axis_index("seq")
    half = partial.shape[0] // 2

    def piece(j):
        return lax.dynamic_slice_in_dim(partial, (me ^ j) * width, width, axis)

    got = swap(jnp.stack([piece(j) for j in (1, 3, 5, 7)]), 1)
    held = {j: piece(j).astype(f32) + got[j // 2].astype(f32) for j in (0, 2, 4, 6)}
    first = {j: held[j][:half] for j in held}
    second = {j: held[j][half:] for j in held}
    sent_x = swap(jnp.stack([first[2].astype(bf16), first[6].astype(bf16)]), 2)
    sent_y = swap(jnp.stack([second[4].astype(bf16), second[6].astype(bf16)]), 4)
    last_y = swap((first[4] + sent_x[1].astype(f32)).astype(bf16), 4)
    last_x = swap((second[2] + sent_y[1].astype(f32)).astype(bf16), 2)
    own_first = first[0] + sent_x[0].astype(f32) + last_y.astype(f32)
    own_second = second[0] + sent_y[0].astype(f32) + last_x.astype(f32)
    return jnp.concatenate([own_first, own_second], axis=0)


def line_step(array, step):
    size = lax.axis_size("fsdp")
    return lax.ppermute(
        array, "fsdp", [(i, i + step) for i in range(size) if 0 <= i + step < size]
    )


def gather_line(block):
    size = lax.axis_size("fsdp")
    if size != 4:
        return lax.all_gather(block, "fsdp", axis=0, tiled=False)
    me = lax.axis_index("fsdp")
    below, above = [block], [block]
    for _ in range(size - 1):
        below.append(line_step(below[-1], 1))
        above.append(line_step(above[-1], -1))
    whole = jnp.zeros((size,) + block.shape, block.dtype)
    whole = lax.dynamic_update_index_in_dim(whole, block, me, 0)
    for k in range(1, size):
        part = below[k] + above[size - k]
        whole = lax.dynamic_update_index_in_dim(whole, part, lax.rem(me - k + size, size), 0)
    return whole


def reduce_line(partial):
    size = lax.axis_size("fsdp")
    if size != 4:
        return lax.psum_scatter(
            partial.astype(bf16), "fsdp", scatter_dimension=0, tiled=False
        ).astype(f32)
    me = lax.axis_index("fsdp")

    def entry(k):
        return lax.dynamic_index_in_dim(
            partial, lax.rem(me + k + size, size), 0, keepdims=False
        ).astype(f32)

    up, down = entry(size - 1), entry(1 - size)
    for k in range(size - 2, -1, -1):
        got_up = line_step(up.astype(bf16), 1).astype(f32)
        got_down = line_step(down.astype(bf16), -1).astype(f32)
        if k:
            up, down = entry(k) + got_up, entry(-k) + got_down
    return entry(0) + got_up + got_down


def spread(blocks):
    return lax.all_to_all(blocks, "seq", split_axis=0, concat_axis=0, tiled=True)


def sum_everywhere(vector):
    groups, size = lax.axis_size("seq"), lax.axis_size("fsdp")
    if groups != 8 or size != 4:
        return lax.psum(vector, ("fsdp", "seq"))
    for mask in (1, 2, 4):
        vector = vector + swap(vector, mask)
    for mask in (1, 2):
        vector = vector + lax.ppermute(vector, "fsdp", [(i, i ^ mask) for i in range(size)])
    return vector


exact = lax.Precision.HIGHEST


def dot_nt(left, right, precision=None):
    return lax.dot_general(left, right, (((1,), (1,)), ((), ())), precision=precision, preferred_element_type=f32)


def dot_tn(left, right):
    return lax.dot_general(left, right, (((0,), (0,)), ((), ())), preferred_element_type=f32)


def head_mean():
    row = lax.broadcasted_iota(jnp.int32, (128, 128), 0) // HD
    col = lax.broadcasted_iota(jnp.int32, (128, 128), 1) // HD
    return jnp.where(row == col, 1.0 / HD, 0.0).astype(bf16)


def head_average(array):
    high = array.astype(bf16)
    low = (array - high.astype(f32)).astype(bf16)
    mean = head_mean()
    return jnp.dot(high, mean, preferred_element_type=f32) + jnp.dot(low, mean, preferred_element_type=f32)


def lane_index(rows):
    return lax.broadcasted_iota(jnp.int32, (rows, 128), 1)


def half_turn(array, back):
    low = (lane_index(array.shape[0]) % HD) < HD // 2
    ahead = pltpu.roll(array, 128 - HD // 2, 1)
    behind = pltpu.roll(array, HD // 2, 1)
    return jnp.where(low, ahead, -behind) if back else jnp.where(low, -ahead, behind)


def attn_fwd_kernel(block, q_ref, kv_ref, start_ref, *refs):
    out_ref, lse_ref = refs[-2:]
    step = pl.program_id(1)
    steps = kv_ref.shape[1] // block
    lanes = lane_index(block)

    for at in range(steps):
        end = (at + 1) * block

        @pl.when(step == at)
        def _(at=at, end=end):
            k = kv_ref[0, :end, :HD]
            v = kv_ref[0, :end, HD:]
            q_index = at * block + lax.broadcasted_iota(jnp.int32, (block, end), 0)
            k_index = lax.broadcasted_iota(jnp.int32, (block, end), 1)
            allowed = (k_index <= q_index) & (k_index >= start_ref[0][:, :1])
            outs, totals = [], []
            for head in range(2):
                q = q_ref[0, :, head * HD : (head + 1) * HD] * jnp.array(HD ** -0.5, bf16)
                scores = jnp.where(allowed, dot_nt(q, k), masked)
                largest = jnp.max(scores, axis=-1, keepdims=True)
                weights = jnp.exp(scores - largest)
                total = jnp.sum(weights, axis=-1, keepdims=True)
                out = jnp.dot(weights.astype(bf16), v, preferred_element_type=f32) / total
                outs.append(out.astype(bf16))
                totals.append(largest + jnp.log(total))
            out_ref[0] = jnp.concatenate(outs, axis=1)
            lse_ref[0] = jnp.where(lanes < HD, totals[0], totals[1])


def attn_fwd(q, kv, starts, span, earlier):
    seqs, length, _ = q.shape
    block = 2 * span
    rows = lambda b, i: (b, i, 0)
    whole = lambda b, i: (b, 0, 0)
    return pl.pallas_call(
        functools.partial(attn_fwd_kernel, block),
        grid=(seqs, length // block),
        in_specs=[
            pl.BlockSpec((1, block, 128), rows),
            pl.BlockSpec((1, length, 128), whole),
            pl.BlockSpec((1, block, 128), rows),
        ]
        + [pl.BlockSpec(memory_space=pl.ANY)] * len(earlier),
        out_specs=[pl.BlockSpec((1, block, 128), rows), pl.BlockSpec((1, block, 128), rows)],
        out_shape=[
            jax.ShapeDtypeStruct((seqs, length, 128), bf16),
            jax.ShapeDtypeStruct((seqs, length, 128), f32),
        ],
        compiler_params=pltpu.CompilerParams(vmem_limit_bytes=48 << 20),
        cost_estimate=pl.CostEstimate(flops=seqs * length * length * 256, bytes_accessed=seqs * length * 1792, transcendentals=seqs * length * length),
        name="attn_fwd",
    )(q, kv, starts, *earlier)


def attn_bwd_kernel(block, q_ref, kv_ref, do_ref, o_ref, lse_ref, start_ref, *refs):
    dq_ref, dkv_ref, dk_acc, dv_acc = refs[-4:]
    step = pl.program_id(1)
    steps = kv_ref.shape[1] // block

    @pl.when(step == 0)
    def _():
        dk_acc[...] = jnp.zeros_like(dk_acc)
        dv_acc[...] = jnp.zeros_like(dv_acc)

    for at in range(steps):
        end = (at + 1) * block

        @pl.when(step == at)
        def _(at=at, end=end):
            k = kv_ref[0, :end, :HD]
            v = kv_ref[0, :end, HD:]
            k_index = lax.broadcasted_iota(jnp.int32, (end, block), 0)
            q_index = at * block + lax.broadcasted_iota(jnp.int32, (end, block), 1)
            allowed = (k_index <= q_index) & (k_index >= start_ref[0, 0:1, :])
            do_rows = do_ref[...].reshape(block, 128)
            product = do_rows.astype(f32) * o_ref[0].astype(f32)
            dqs = []
            for head in range(2):
                cut = slice(head * HD, (head + 1) * HD)
                q = q_ref[0, :, cut] * jnp.array(HD ** -0.5, bf16)
                do = do_rows[:, cut]
                delta = dot_nt(jnp.ones((8, HD), f32), product[:, cut], exact)[0:1, :]
                scores = jnp.where(allowed, dot_nt(k, q), masked)
                prob = jnp.exp(scores - lse_ref[0, head : head + 1, :])
                dv_acc[:end, :] += jnp.dot(prob.astype(bf16), do, preferred_element_type=f32)
                dscore = (prob * (dot_nt(v, do) - delta)).astype(bf16)
                dk_acc[:end, :] += jnp.dot(dscore, q, preferred_element_type=f32)
                dqs.append(dot_tn(dscore, k) * (HD ** -0.5))
            dq_ref[0] = jnp.concatenate(dqs, axis=1)

    @pl.when(step == steps - 1)
    def _():
        dkv_ref[0] = jnp.concatenate([dk_acc[...], dv_acc[...]], axis=1)


def attn_bwd(q, kv, do, out, lse, starts, span, earlier):
    seqs, length, _ = q.shape
    block = 2 * span
    rows = lambda b, i: (b, i, 0)
    cols = lambda b, i: (b, 0, i)
    whole = lambda b, i: (b, 0, 0)
    return pl.pallas_call(
        functools.partial(attn_bwd_kernel, block),
        grid=(seqs, length // block),
        in_specs=[
            pl.BlockSpec((1, block, 128), rows),
            pl.BlockSpec((1, length, 128), whole),
            pl.BlockSpec((2, 1, span, 128), lambda b, i: (i, b, 0, 0)),
            pl.BlockSpec((1, block, 128), rows),
            pl.BlockSpec((1, 8, block), cols),
            pl.BlockSpec((1, 8, block), cols),
        ]
        + [pl.BlockSpec(memory_space=pl.ANY)] * len(earlier),
        out_specs=[pl.BlockSpec((1, block, 128), rows), pl.BlockSpec((1, length, 128), whole)],
        out_shape=[
            jax.ShapeDtypeStruct((seqs, length, 128), f32),
            jax.ShapeDtypeStruct((seqs, length, 128), f32),
        ],
        scratch_shapes=[pltpu.VMEM((length, HD), f32), pltpu.VMEM((length, HD), f32)],
        compiler_params=pltpu.CompilerParams(vmem_limit_bytes=56 << 20),
        cost_estimate=pl.CostEstimate(flops=seqs * length * length * 640, bytes_accessed=seqs * length * 2560, transcendentals=seqs * length * length),
        name="attn_bwd",
    )(q, kv, do, out, lse, starts, *earlier)


def any_space(count):
    return [pl.BlockSpec(memory_space=pl.ANY)] * count


def pack_kernel(groups, part, gate_ref, up_ref, q_ref, k_ref, v_ref, gain_ref, out_ref):
    size = gate_ref.shape[1] // (groups * part)
    hidden = size * part
    for at, ref in ((0, gate_ref), (hidden, up_ref)):
        whole = ref[...].astype(f32)
        for g in range(groups):
            cuts = [whole[:, (f * groups + g) * part : (f * groups + g + 1) * part] for f in range(size)]
            out_ref[g, :, at : at + hidden] = jnp.concatenate(cuts, axis=1).astype(bf16)
    k, v = k_ref[...].astype(f32), v_ref[...].astype(f32)
    for g in range(groups):
        at = slice(g * HD, (g + 1) * HD)
        out_ref[g, :, 2 * hidden : 2 * hidden + 128] = q_ref[:, g * 128 : (g + 1) * 128]
        both = jnp.concatenate([k[:, at], v[:, at]], axis=1)
        out_ref[g, :, 2 * hidden + 128 : 2 * hidden + 256] = both.astype(bf16)
        out_ref[g, :, 2 * hidden + 256 :] = gain_ref[...]


def pack_columns(gate, up, query, key, value, gains, groups, part):
    shard, total = gate.shape
    return pl.pallas_call(
        functools.partial(pack_kernel, groups, part),
        out_shape=jax.ShapeDtypeStruct((groups, shard, 2 * total // groups + 384), bf16),
        name="pack",
    )(gate, up, query, key, value, gains)


def unpack_kernel(part, home_ref, gate_w_ref, up_w_ref, _, gate_ref, up_ref, sum_ref):
    groups, _, shard, hidden = home_ref.shape
    size = hidden // part
    for which, ref in ((0, gate_ref), (1, up_ref)):
        rows = [home_ref[g, which].astype(f32) for g in range(groups)]
        cuts = [rows[g][:, f * part : (f + 1) * part] for f in range(size) for g in range(groups)]
        ref[...] = jnp.concatenate(cuts, axis=1)
    total = jnp.sum(gate_w_ref[...].astype(f32) * gate_ref[...], axis=1, keepdims=True)
    total += jnp.sum(up_w_ref[...].astype(f32) * up_ref[...], axis=1, keepdims=True)
    sum_ref[...] = jnp.broadcast_to(total, sum_ref.shape)


def unpack_columns(home, gate_w, up_w, part, earlier):
    shape = gate_w.shape
    return pl.pallas_call(
        functools.partial(unpack_kernel, part),
        in_specs=[pl.BlockSpec(memory_space=pltpu.VMEM)] * 3 + any_space(1),
        out_shape=[
            jax.ShapeDtypeStruct(shape, f32),
            jax.ShapeDtypeStruct(shape, f32),
            jax.ShapeDtypeStruct((shape[0], 128), f32),
        ],
        name="unpack",
    )(home, gate_w, up_w, earlier)


def unpack_heads_kernel(home_ref, q_w_ref, k_w_ref, v_w_ref, q_ref, k_ref, v_ref, sum_ref, gain_ref):
    groups, shard = home_ref.shape[0], q_ref.shape[0]
    blocks = [home_ref[g].astype(f32) for g in range(groups)]
    q_ref[...] = jnp.concatenate([block[:shard, : 2 * HD] for block in blocks], axis=1)
    k_ref[...] = jnp.concatenate([block[:shard, 2 * HD : 3 * HD] for block in blocks], axis=1)
    v_ref[...] = jnp.concatenate([block[:shard, 3 * HD :] for block in blocks], axis=1)
    total = 0.0
    for weight, grad in ((q_w_ref, q_ref), (k_w_ref, k_ref), (v_w_ref, v_ref)):
        total += jnp.sum(weight[...].astype(f32) * grad[...], axis=1, keepdims=True)
    sum_ref[...] = jnp.broadcast_to(total, sum_ref.shape)
    gain_ref[...] = sum(block[shard : shard + 8] for block in blocks)


def unpack_heads(home, q_w, k_w, v_w):
    return pl.pallas_call(
        unpack_heads_kernel,
        out_shape=[jax.ShapeDtypeStruct(w.shape, f32) for w in (q_w, k_w, v_w)]
        + [jax.ShapeDtypeStruct((q_w.shape[0], 128), f32), jax.ShapeDtypeStruct((8, home.shape[2]), f32)],
        name="unpack_heads",
    )(home, q_w, k_w, v_w)


def qkv_fwd_kernel(at_ref, *refs):
    x_refs, w_refs = refs[:8], refs[8:12]
    gain_ref, scale_ref, cos_ref, sin_ref, x_out, nm_ref, raw_ref, q_ref, kv_ref, w_ref = refs[12:]
    step = pl.program_id(0)
    shard = w_ref.shape[0] // 32

    @pl.when(step == 0)
    def _():
        for m in range(4):
            for g in range(8):
                row = pl.multiple_of(((at_ref[1] ^ m) * 8 + g) * shard, shard)
                w_ref[pl.ds(row, shard), :] = w_refs[m][g, :, :256]

    for j in range(8):

        @pl.when(step == j)
        def _(j=j):
            x_out[...] = x_refs[j][...]

    x = x_out[...].reshape(-1, x_out.shape[-1]).astype(f32)
    factor = lax.rsqrt(jnp.mean(x * x, axis=-1, keepdims=True) + eps)
    nm = (x * factor * gain_ref[...]).astype(bf16)
    nm_ref[...] = nm.reshape(nm_ref.shape)
    raw = jnp.dot(nm, w_ref[...], preferred_element_type=f32)
    raw_ref[...] = raw.reshape(raw_ref.shape)
    cos = cos_ref[...].reshape(-1, 128)
    sin = sin_ref[...].reshape(-1, 128)

    def prepared(part, scale):
        inv = lax.rsqrt(head_average(part * part) + eps)
        normed = part * inv * scale
        return normed * cos + half_turn(normed, False) * sin

    q = prepared(raw[:, :128], scale_ref[0:1, :])
    kv = prepared(raw[:, 128:], scale_ref[1:2, :])
    kv = jnp.where(lane_index(kv.shape[0]) < HD, kv, raw[:, 128:])
    q_ref[...] = q.astype(bf16).reshape(q_ref.shape)
    kv_ref[...] = kv.astype(bf16).reshape(kv_ref.shape)


def qkv_fwd(at, x_blocks, w_blocks, gain, scales, cosine, sine, earlier):
    seqs, span, width = x_blocks[0].shape
    length = 8 * span
    home = lambda j, m: (0, m[0] ^ j, 0)
    fixed = lambda j, m: (0, 0)
    once = dict(pipeline_mode=pl.Buffered(1))

    def kernel(at_ref, *refs):
        qkv_fwd_kernel(at_ref, *refs[:16], *refs[16 + len(earlier) :])

    return pl.pallas_call(
        kernel,
        grid_spec=pltpu.PrefetchScalarGridSpec(
            num_scalar_prefetch=1,
            grid=(8,),
            in_specs=[pl.BlockSpec((seqs, span, width), lambda j, m: (0, 0, 0), **once)] * 8
            + [pl.BlockSpec(w_blocks[0].shape, lambda j, m: (0, 0, 0), **once)] * 4
            + [
                pl.BlockSpec((1, width), fixed, **once),
                pl.BlockSpec((8, 128), fixed, **once),
                pl.BlockSpec((seqs, span, 128), home),
                pl.BlockSpec((seqs, span, 128), home),
            ]
            + any_space(len(earlier)),
            out_specs=[
                pl.BlockSpec((seqs, span, width), home),
                pl.BlockSpec((seqs, span, width), home),
                pl.BlockSpec((seqs, span, 256), home),
                pl.BlockSpec((seqs, span, 128), home),
                pl.BlockSpec((seqs, span, 128), home),
                pl.BlockSpec((width, 256), fixed),
            ],
        ),
        out_shape=[
            jax.ShapeDtypeStruct((seqs, length, width), bf16),
            jax.ShapeDtypeStruct((seqs, length, width), bf16),
            jax.ShapeDtypeStruct((seqs, length, 256), f32),
            jax.ShapeDtypeStruct((seqs, length, 128), bf16),
            jax.ShapeDtypeStruct((seqs, length, 128), bf16),
            jax.ShapeDtypeStruct((width, 256), bf16),
        ],
        compiler_params=pltpu.CompilerParams(vmem_limit_bytes=40 << 20),
        cost_estimate=pl.CostEstimate(flops=16 * seqs * length * width * 256, bytes_accessed=seqs * length * width * 6, transcendentals=0),
        name="qkv_fwd",
    )(at, *x_blocks, *w_blocks, gain, scales, cosine, sine, *earlier)


def halves_spec(seqs, span, width):
    return pl.BlockSpec((1, seqs, span, width), lambda t, m: ((m[0] ^ t) >> 1, 0, 0, 0))


def store_halves(me, step, value, even_ref, odd_ref):
    odd = ((me ^ step) & 1) == 1

    @pl.when(odd)
    def _():
        odd_ref[...] = value.reshape(odd_ref.shape)

    @pl.when(jnp.logical_not(odd))
    def _():
        even_ref[...] = value.reshape(even_ref.shape)


def ffn_kernel(hidden, padded, at_ref, *refs):
    parts, cot_refs, wd_parts = refs[:8], refs[8:16], refs[16]
    (x_ref, wo_parts, wgu_ref, gain_ref, attn_ref, mid_ref, nm_ref, hid_ref, grads_ref) = refs[17:26]
    gnm_even, gnm_odd, out_even, out_odd, cot_ref, wo_ref, wgu, wd = refs[26:]
    step = pl.program_id(0)

    @pl.when(step == 0)
    def _():
        shard = wo_parts.shape[2]
        part = wd_parts.shape[1] - shard
        wgu[...] = jnp.zeros_like(wgu)
        wgu[:, :hidden] = wgu_ref[:, :hidden]
        wgu[:, padded : padded + hidden] = wgu_ref[:, hidden:]
        wd[hidden:, :] = jnp.zeros((padded - hidden, wd.shape[1]), bf16)
        for f in range(wd_parts.shape[0]):
            wd[f * part : (f + 1) * part, :] = wd_parts[f, :part, :]
            for g in range(8):
                row = (f * 8 + g) * shard
                wo_ref[row : row + shard, :] = wo_parts[g, f]

    for j in range(8):

        @pl.when((at_ref[0] ^ step) == j)
        def _(j=j):
            cot_ref[...] = cot_refs[j][...]

    tile = attn_ref.shape[0] * attn_ref.shape[1]
    width = wo_ref.shape[0]
    for j in range(8):
        at = pl.multiple_of((at_ref[0] ^ j) * 128, 128)
        attn_ref[:, :, pl.ds(at, 128)] = parts[j][...]
    attn = attn_ref[...].reshape(tile, width)
    mid = x_ref[...].reshape(tile, width).astype(f32) + jnp.dot(attn, wo_ref[...], preferred_element_type=f32)
    mid_ref[...] = mid.reshape(mid_ref.shape)
    factor = lax.rsqrt(jnp.mean(mid * mid, axis=-1, keepdims=True) + eps)
    nm = (mid * factor * gain_ref[...]).astype(bf16)
    nm_ref[...] = nm.reshape(nm_ref.shape)
    both = jnp.dot(nm, wgu[...], preferred_element_type=f32)
    gate, up = both[:, :padded], both[:, padded:]
    sigma = jax.nn.sigmoid(gate)
    hid = (gate * sigma * up).astype(bf16)
    hid_ref[...] = hid.reshape(hid_ref.shape)
    grad_hidden = dot_nt(cot_ref[...].reshape(tile, width), wd[...])
    grad_gate = (grad_hidden * up * sigma * (1.0 + gate * (1.0 - sigma))).astype(bf16)
    grad_up = (grad_hidden * gate * sigma).astype(bf16)
    grads = jnp.concatenate([grad_gate, grad_up], axis=1)
    grads_ref[...] = grads.reshape(grads_ref.shape)
    store_halves(at_ref[0], step, dot_nt(grads, wgu[...]).astype(bf16), gnm_even, gnm_odd)
    out = jnp.dot(hid, wd[...], preferred_element_type=f32).astype(bf16)
    store_halves(at_ref[0], step, out, out_even, out_odd)


def ffn(at, parts, cot_blocks, wd_parts, x, wo_parts, w_gate_up, gain):
    seqs, length, width = x.shape
    span = length // 8
    hidden = w_gate_up.shape[1] // 2
    padded = -(-hidden // 128) * 128
    home = lambda t, m: (0, t, 0)
    fixed = lambda t, m: (0, 0)
    once = dict(pipeline_mode=pl.Buffered(1))
    tokens = lambda cols: pl.BlockSpec((seqs, span, cols), home)
    shape = lambda cols, kind: jax.ShapeDtypeStruct((seqs, length, cols), kind)
    half = jax.ShapeDtypeStruct((4, seqs, span, width), bf16)
    return pl.pallas_call(
        functools.partial(ffn_kernel, hidden, padded),
        grid_spec=pltpu.PrefetchScalarGridSpec(
            num_scalar_prefetch=1,
            grid=(8,),
            in_specs=[tokens(128)] * 8
            + [pl.BlockSpec((seqs, span, width), lambda t, m: (0, 0, 0), **once)] * 8
            + [pl.BlockSpec(wd_parts.shape, lambda t, m: (0, 0, 0), **once)]
            + [
                tokens(width),
                pl.BlockSpec(wo_parts.shape, lambda t, m: (0, 0, 0, 0), **once),
                pl.BlockSpec((width, 2 * hidden), fixed, **once),
                pl.BlockSpec((1, width), fixed, **once),
            ],
            out_specs=[tokens(width), tokens(width), tokens(width), tokens(padded), tokens(2 * padded)]
            + [halves_spec(seqs, span, width)] * 4
            + [tokens(width), pl.BlockSpec((width, width), fixed)],
            scratch_shapes=[pltpu.VMEM((width, 2 * padded), bf16), pltpu.VMEM((padded, width), bf16)],
        ),
        out_shape=[shape(width, bf16), shape(width, f32), shape(width, bf16), shape(padded, bf16), shape(2 * padded, bf16)]
        + [half] * 4
        + [shape(width, bf16), jax.ShapeDtypeStruct((width, width), bf16)],
        compiler_params=pltpu.CompilerParams(vmem_limit_bytes=60 << 20),
        cost_estimate=pl.CostEstimate(flops=seqs * length * width * (2 * width + 12 * padded), bytes_accessed=seqs * length * width * 20, transcendentals=seqs * length * padded),
        name="ffn",
    )(at, *parts, *cot_blocks, wd_parts, x, wo_parts, w_gate_up, gain)


def product_kernel(cuts, left_ref, right_ref, *refs):
    out_ref, total = refs[-2:]
    step = pl.program_id(0)
    value = dot_tn(left_ref[...], right_ref[...])

    @pl.when(step == 0)
    def _():
        total[...] = value

    @pl.when(step > 0)
    def _():
        total[...] += value

    @pl.when(step == pl.num_programs(0) - 1)
    def _():
        size, blocks, _, count, _ = out_ref.shape
        for f in range(size):
            for g in range(blocks):
                row = (f * blocks + g) * count
                for i, (begin, end) in enumerate(cuts):
                    out_ref[f, g, i] = total[row : row + count, begin:end].astype(bf16)


def product(left, right, split, cuts, cost, earlier=()):
    rows = left.shape[0]
    shape = (split[0], split[1], len(cuts), split[2], cuts[0][1] - cuts[0][0])
    tile = 512
    at = lambda i: (i, 0)
    return pl.pallas_call(
        functools.partial(product_kernel, cuts),
        grid=(rows // tile,),
        in_specs=[pl.BlockSpec((tile, left.shape[1]), at), pl.BlockSpec((tile, right.shape[1]), at)]
        + any_space(len(earlier)),
        out_specs=pl.BlockSpec(shape, lambda i: (0, 0, 0, 0, 0)),
        out_shape=jax.ShapeDtypeStruct(shape, bf16),
        scratch_shapes=[pltpu.VMEM((left.shape[1], right.shape[1]), f32)],
        compiler_params=pltpu.CompilerParams(vmem_limit_bytes=48 << 20),
        cost_estimate=pl.CostEstimate(flops=cost, bytes_accessed=cost, transcendentals=0),
        name="product",
    )(left, right, *earlier)


def mid_kernel(at_ref, mid_ref, cot_ref, gain_ref, wo_ref, even_ref, got_ref, *refs):
    grad_ref, half_ref, out_ref = refs[-3:]
    seqs, span, width = cot_ref.shape
    grad_nm = even_ref[0].astype(f32) + got_ref[0].astype(f32)
    for part_ref in refs[:3]:
        grad_nm += part_ref[...].astype(f32)
    grad_nm = grad_nm.reshape(seqs * span, width)
    mid = mid_ref[...].reshape(seqs * span, width)
    factor = lax.rsqrt(jnp.mean(mid * mid, axis=-1, keepdims=True) + eps)
    normed = mid * factor
    scaled = grad_nm * gain_ref[...]
    grad = cot_ref[...].reshape(seqs * span, width).astype(f32) + factor * (
        scaled - normed * jnp.mean(scaled * normed, axis=-1, keepdims=True)
    )
    grad_ref[...] = grad
    half = grad.astype(bf16)
    half_ref[...] = half
    out = dot_nt(half, wo_ref[...]).astype(bf16)
    for g in range(8):
        out_ref[g] = out[:, g * 128 : (g + 1) * 128].reshape(seqs, span, 128)


def mid_bwd(at, mid, cot, gain, w_out, even, stages, earlier):
    seqs, span, width = cot.shape
    first = lambda *s: pl.BlockSpec((1,) + s, lambda i, m: (0,) * (len(s) + 1))
    full = lambda *s: pl.BlockSpec(s, lambda i, m: (0,) * len(s))
    rows = seqs * span
    return pl.pallas_call(
        mid_kernel,
        grid_spec=pltpu.PrefetchScalarGridSpec(
            num_scalar_prefetch=1,
            grid=(1,),
            in_specs=[
                pl.BlockSpec((seqs, span, width), lambda i, m: (0, m[0], 0)),
                full(seqs, span, width),
                full(1, width),
                full(width, width),
                first(seqs, span, width),
                first(seqs, span, width),
                full(seqs, span, width),
                full(seqs, span, width),
                full(seqs, span, width),
            ]
            + any_space(len(earlier)),
            out_specs=[full(rows, width), full(rows, width), full(8, seqs, span, 128)],
        ),
        out_shape=[
            jax.ShapeDtypeStruct((rows, width), f32),
            jax.ShapeDtypeStruct((rows, width), bf16),
            jax.ShapeDtypeStruct((8, seqs, span, 128), bf16),
        ],
        compiler_params=pltpu.CompilerParams(vmem_limit_bytes=40 << 20),
        cost_estimate=pl.CostEstimate(flops=2 * rows * width * width, bytes_accessed=rows * width * 20, transcendentals=0),
        name="mid_bwd",
    )(at, mid, cot, gain, w_out, even, *stages, *earlier)


def qkv_bwd_kernel(at_ref, dq_ref, dkv_ref, raw_ref, nm_ref, w_ref, scale_ref, cos_ref, sin_ref, *refs):
    even_ref, odd_ref, dw_ref, dscale_ref, dw_acc = refs[-5:]
    step = pl.program_id(0)
    seqs, span, width = nm_ref.shape
    tile = seqs * span

    @pl.when(step == 0)
    def _():
        dw_acc[...] = jnp.zeros_like(dw_acc)
        dscale_ref[...] = jnp.zeros_like(dscale_ref)

    cos, sin = cos_ref[...].reshape(tile, 128), sin_ref[...].reshape(tile, 128)
    def back(raw, grad, scale):
        inv = lax.rsqrt(head_average(raw * raw) + eps)
        normed = raw * inv
        turned = grad * cos + half_turn(grad * sin, True)
        grad_normed = turned * scale
        grad_raw = inv * (grad_normed - normed * head_average(grad_normed * normed))
        return grad_raw, jnp.sum(turned * normed, axis=0, keepdims=True)

    raw = raw_ref[...].reshape(tile, 256)
    grad_kv = dkv_ref[...].reshape(tile, 128)
    dq, q_scale = back(raw[:, :128], dq_ref[...].reshape(tile, 128), scale_ref[0:1, :])
    dkv, k_scale = back(raw[:, 128:], grad_kv, scale_ref[1:2, :])
    dkv = jnp.where(lane_index(tile) < HD, dkv, grad_kv)
    grad = jnp.concatenate([dq.astype(bf16), dkv.astype(bf16)], axis=1)
    dscale_ref[0:1, :] += q_scale
    dscale_ref[1:2, :] += k_scale
    store_halves(at_ref[0], step, dot_nt(grad, w_ref[...]).astype(bf16), even_ref, odd_ref)
    dw_acc[...] += dot_tn(nm_ref[...].reshape(tile, width), grad)

    @pl.when(step == pl.num_programs(0) - 1)
    def _():
        dw_ref[...] = dw_acc[...].astype(bf16)


def qkv_bwd(at, dq, dkv, raw, nm, w_qkv, scales, cosine, sine, earlier):
    seqs, length, width = nm.shape
    span = length // 8
    tokens = lambda cols: pl.BlockSpec((seqs, span, cols), lambda t, m: (0, t, 0))
    fixed = lambda t, m: (0, 0)
    half = jax.ShapeDtypeStruct((4, seqs, span, width), bf16)
    return pl.pallas_call(
        qkv_bwd_kernel,
        grid_spec=pltpu.PrefetchScalarGridSpec(
            num_scalar_prefetch=1,
            grid=(8,),
            in_specs=[
                tokens(128),
                tokens(128),
                tokens(256),
                tokens(width),
                pl.BlockSpec((width, 256), fixed),
                pl.BlockSpec((8, 128), fixed),
                tokens(128),
                tokens(128),
            ]
            + any_space(len(earlier)),
            out_specs=[halves_spec(seqs, span, width)] * 2
            + [pl.BlockSpec((width, 256), fixed), pl.BlockSpec((8, 128), fixed)],
            scratch_shapes=[pltpu.VMEM((width, 256), f32)],
        ),
        out_shape=[
            half,
            half,
            jax.ShapeDtypeStruct((width, 256), bf16),
            jax.ShapeDtypeStruct((8, 128), f32),
        ],
        compiler_params=pltpu.CompilerParams(vmem_limit_bytes=48 << 20),
        cost_estimate=pl.CostEstimate(flops=16 * seqs * length * width * 256, bytes_accessed=seqs * length * width * 6, transcendentals=0),
        name="qkv_bwd",
    )(at, dq, dkv, raw, nm, w_qkv, scales, cosine, sine, *earlier)


def plain_body(
    block_input,
    positions,
    cotangent,
    attention_gain,
    query_weight,
    key_weight,
    value_weight,
    query_gain,
    key_gain,
    output_weight,
    feedforward_gain,
    gate_weight,
    up_weight,
    down_weight,
):
    seq_count, span, width = block_input.shape
    groups = lax.axis_size("seq")
    size = lax.axis_size("fsdp")
    me = lax.axis_index("seq")
    length = span * groups
    rows = seq_count * length
    own_rows = seq_count * span
    shard = query_weight.shape[0]
    heads = H // groups
    kv_heads = max(1, KV // groups)
    copies = max(1, groups // KV)
    q_cols, k_cols = heads * HD, kv_heads * HD
    qkv_cols = q_cols + 2 * k_cols
    part = gate_weight.shape[1] // (groups * size)
    hidden_cols = part * size

    x_full = gather_seq(block_input, 1)

    def columns(weight, col_copies):
        shaped = weight.reshape(shard, -1, 1, HD)
        shaped = jnp.broadcast_to(shaped, (shard, shaped.shape[1], col_copies, HD))
        return shaped.reshape(shard, groups, -1)

    packed = jnp.concatenate(
        [
            columns(query_weight, 1),
            columns(key_weight, copies),
            columns(value_weight, copies),
        ],
        axis=2,
    ).transpose(1, 0, 2)
    gains = jnp.concatenate([attention_gain, feedforward_gain])
    gain_rows = jnp.zeros((16, qkv_cols), bf16).at[0, : 2 * shard].set(gains)
    packed = jnp.concatenate(
        [packed, jnp.broadcast_to(gain_rows[None], (groups, 16, qkv_cols))], axis=1
    )
    packed = gather_line(spread(packed))
    w_qkv = packed[:, :, :shard, :].reshape(width, qkv_cols)
    gain_one = packed[:, :, shard, :shard].reshape(width).astype(f32)
    gain_two = packed[:, :, shard, shard : 2 * shard].reshape(width).astype(f32)

    out_full = lax.all_gather(output_weight, ("fsdp", "seq"), axis=0, tiled=True)

    def ff_columns(weight):
        shaped = weight.reshape(shard, size, groups, part)
        return shaped.transpose(2, 0, 1, 3).reshape(groups, shard, hidden_cols)

    w_gate_up = gather_line(
        spread(jnp.concatenate([ff_columns(gate_weight), ff_columns(up_weight)], axis=2))
    ).reshape(width, 2 * hidden_cols)
    w_gate = w_gate_up[:, :hidden_cols]
    w_up = w_gate_up[:, hidden_cols:]
    w_down = gather_line(down_weight).reshape(hidden_cols, width)

    cot_full = gather_seq(cotangent, 1).reshape(rows, width)

    residual_in = x_full.reshape(rows, width).astype(f32)
    factor_one = inv_rms(residual_in)
    normed_in = (residual_in * factor_one * gain_one).astype(bf16)
    qkv_raw = matmul(normed_in, w_qkv)
    query_raw = qkv_raw[:, :q_cols]
    key_raw = qkv_raw[:, q_cols : q_cols + k_cols]
    value_rows = qkv_raw[:, q_cols + k_cols :].astype(bf16)
    cosine, sine = rope_tables(positions.reshape(rows), HD)
    query_scale = query_gain.astype(f32)
    key_scale = key_gain.astype(f32)

    def query_side(raw_rows, gain_row):
        return head_prep(raw_rows, gain_row, cosine, sine, heads)

    def key_side(raw_rows, gain_row):
        return head_prep(raw_rows, gain_row, cosine, sine, kv_heads)

    def head_view(packed_rows):
        shaped = packed_rows.reshape(seq_count, length, -1, HD)
        return jnp.repeat(shaped, heads // shaped.shape[2], axis=2)

    queries = query_side(query_raw, query_scale).astype(bf16).reshape(seq_count, length, heads, HD)
    keys = head_view(key_side(key_raw, key_scale).astype(bf16))
    values = head_view(value_rows)
    doc_start = jnp.arange(length, dtype=jnp.int32)[None, :] - positions
    outputs, log_totals = jax.vmap(attend_fwd)(queries, keys, values, doc_start)

    attn_full = gather_seq(outputs.reshape(seq_count, length, q_cols), 2)
    attn_rows = attn_full.reshape(rows, width)
    residual_mid = residual_in + matmul(attn_rows, out_full)
    factor_two = inv_rms(residual_mid)
    normed_mid = (residual_mid * factor_two * gain_two).astype(bf16)

    def own(array):
        shaped = array.reshape(seq_count, length, -1)
        return lax.dynamic_slice_in_dim(shaped, me * span, span, 1).reshape(own_rows, -1)

    gate_rows = matmul(normed_mid, w_gate)
    up_rows = matmul(normed_mid, w_up)
    sigma = jax.nn.sigmoid(gate_rows)
    hidden = (gate_rows * sigma * up_rows).astype(bf16)
    grad_hidden = matmul_nt(cot_full, w_down)
    grad_gate = (grad_hidden * up_rows * sigma * (1.0 + gate_rows * (1.0 - sigma))).astype(bf16)
    grad_up = (grad_hidden * gate_rows * sigma).astype(bf16)
    grad_normed_part = (matmul_nt(grad_gate, w_gate) + matmul_nt(grad_up, w_up)).astype(bf16)
    grad_normed_mid = reduce_seq(grad_normed_part.reshape(seq_count, length, width), 1)
    grad_normed_mid = grad_normed_mid.reshape(own_rows, width)

    residual_own = own(residual_mid)
    cot_rows = cotangent.reshape(own_rows, width).astype(f32)
    grad_mid = cot_rows + norm_bwd(residual_own, own(factor_two), gain_two, grad_normed_mid)
    grad_mid_half = grad_mid.astype(bf16)
    grad_attn_out = matmul_nt(grad_mid_half, out_full).astype(bf16)
    grad_heads = lax.all_to_all(
        grad_attn_out.reshape(seq_count, span, width), "seq", split_axis=2, concat_axis=1, tiled=True
    )

    grad_query_heads, grad_key_heads, grad_value_heads = jax.vmap(attend_bwd)(
        queries,
        keys,
        values,
        outputs,
        log_totals,
        grad_heads.reshape(seq_count, length, heads, HD),
        doc_start,
    )

    def fold(packed_rows):
        shaped = packed_rows.reshape(rows, kv_heads, -1, HD).astype(f32)
        return jnp.sum(shaped, axis=2).reshape(rows, k_cols)

    _, query_back = jax.vjp(query_side, query_raw, query_scale)
    grad_query_raw, query_gain_term = query_back(grad_query_heads.reshape(rows, q_cols).astype(f32))
    _, key_back = jax.vjp(key_side, key_raw, key_scale)
    grad_key_raw, key_gain_term = key_back(fold(grad_key_heads))
    grad_qkv = jnp.concatenate(
        [
            grad_query_raw.astype(bf16),
            grad_key_raw.astype(bf16),
            fold(grad_value_heads).astype(bf16),
        ],
        axis=1,
    )
    grad_in_part = matmul_nt(grad_qkv, w_qkv).astype(bf16)
    grad_normed_in = reduce_seq(grad_in_part.reshape(seq_count, length, width), 1)
    grad_normed_in = grad_normed_in.reshape(own_rows, width)
    own_in = block_input.reshape(own_rows, width).astype(f32)
    input_grad = (
        (grad_mid + norm_bwd(own_in, inv_rms(own_in), gain_one, grad_normed_in))
        .astype(bf16)
        .reshape(seq_count, span, width)
    )

    result_part = matmul(hidden, w_down).astype(bf16).reshape(seq_count, length, width)
    block_output = (
        (residual_own + reduce_seq(result_part, 1).reshape(own_rows, width))
        .astype(bf16)
        .reshape(seq_count, span, width)
    )

    down_grad = reduce_line(matmul_tn(hidden, cot_full).reshape(size, part, width))
    gate_up_term = matmul_tn(normed_mid, jnp.concatenate([grad_gate, grad_up], axis=1))
    gate_up_term = reduce_line(gate_up_term.reshape(size, groups * shard, 2 * hidden_cols))
    gate_up_home = spread(gate_up_term.astype(bf16).reshape(groups, shard, 2 * hidden_cols))

    def ff_home(columns_home):
        shaped = columns_home.astype(f32).reshape(groups, shard, size, part)
        return shaped.transpose(1, 2, 0, 3).reshape(shard, groups * size * part)

    gate_grad = ff_home(gate_up_home[:, :, :hidden_cols])
    up_grad = ff_home(gate_up_home[:, :, hidden_cols:])

    output_term = matmul_tn(own(attn_rows), grad_mid_half).astype(bf16)
    output_grad = lax.psum_scatter(
        output_term, ("fsdp", "seq"), scatter_dimension=0, tiled=True
    ).astype(f32)

    qkv_term = reduce_line(matmul_tn(normed_in, grad_qkv).reshape(size, groups * shard, qkv_cols))
    qkv_home = spread(qkv_term.astype(bf16).reshape(groups, shard, qkv_cols)).astype(f32)

    def home(block, col_copies):
        shaped = block.transpose(1, 0, 2).reshape(shard, -1, col_copies, HD)
        return jnp.sum(shaped, axis=2).reshape(shard, -1)

    query_grad = home(qkv_home[:, :, :q_cols], 1)
    key_grad = home(qkv_home[:, :, q_cols : q_cols + k_cols], copies)
    value_grad = home(qkv_home[:, :, q_cols + k_cols :], copies)

    def weighted(weight, grad):
        return jnp.sum(weight.astype(f32) * grad, axis=1)

    gain_one_grad = (
        weighted(query_weight, query_grad)
        + weighted(key_weight, key_grad)
        + weighted(value_weight, value_grad)
    ) / attention_gain.astype(f32)
    gain_two_grad = (
        weighted(gate_weight, gate_grad) + weighted(up_weight, up_grad)
    ) / feedforward_gain.astype(f32)

    head_gains = sum_everywhere(jnp.concatenate([query_gain_term, key_gain_term])[None])[0]
    return (
        block_output,
        input_grad,
        gain_one_grad,
        query_grad,
        key_grad,
        value_grad,
        head_gains[:HD],
        head_gains[HD:],
        output_grad,
        gain_two_grad,
        gate_grad,
        up_grad,
        down_grad,
    )


def after(array, earlier):
    first = earlier.reshape(-1)[0] if earlier.ndim == 1 else earlier[(0,) * earlier.ndim]
    return array + jnp.minimum(jnp.abs(first), 0).astype(array.dtype)


def swap_line(array, mask):
    size = lax.axis_size("fsdp")
    return lax.ppermute(array, "fsdp", [(i, i ^ mask) for i in range(size)])


def line_blocks(block):
    return [block] + [swap_line(block, m) for m in (1, 2, 3)]


def line_parts(block_of):
    me = lax.axis_index("fsdp")
    return [swap_line(block_of(me ^ m), m) for m in (1, 2, 3)]


def add_up(own, others):
    total = own.astype(f32)
    for other in others:
        total = total + other.astype(f32)
    return total


def reduce_stages(even, odd, earlier=()):
    got = swap(odd, 1)

    def sent(i):
        total = even[i].astype(f32) + got[i].astype(f32)
        for array in earlier:
            total = after(total, array)
        return swap(total.astype(bf16), 2 * i)

    return got, sent(1), sent(2), sent(3)


def own_sum(even, stages):
    total = even[0].astype(f32) + stages[0][0].astype(f32)
    for part in stages[1:]:
        total = total + part.astype(f32)
    return total


def body(
    block_input,
    positions,
    cotangent,
    attention_gain,
    query_weight,
    key_weight,
    value_weight,
    query_gain,
    key_gain,
    output_weight,
    feedforward_gain,
    gate_weight,
    up_weight,
    down_weight,
):
    seqs, span, width = block_input.shape
    groups = lax.axis_size("seq")
    size = lax.axis_size("fsdp")
    if not (groups == 8 and size == 4 and seqs % 2 == 0 and span % 64 == 0):
        return plain_body(
            block_input,
            positions,
            cotangent,
            attention_gain,
            query_weight,
            key_weight,
            value_weight,
            query_gain,
            key_gain,
            output_weight,
            feedforward_gain,
            gate_weight,
            up_weight,
            down_weight,
        )
    me = lax.axis_index("seq")
    me_line = lax.axis_index("fsdp")
    at = jnp.stack([me, me_line]).astype(jnp.int32)
    length = span * groups
    rows = seqs * length
    own_rows = seqs * span
    shard = query_weight.shape[0]
    part = gate_weight.shape[1] // (groups * size)
    hidden_cols = part * size
    padded = -(-hidden_cols // 128) * 128

    gains = jnp.concatenate([attention_gain, feedforward_gain])
    gains = jnp.zeros((shard, 128), bf16).at[0, : 2 * shard].set(gains)
    packed = spread(
        pack_columns(gate_weight, up_weight, query_weight, key_weight, value_weight, gains, groups, part)
    )
    x_blocks = partner_blocks(block_input, direct=True)
    qkv_blocks = line_blocks(packed[:, :, 2 * hidden_cols :])
    gains = [block[:, 0, 256 : 256 + 2 * shard].astype(f32) for block in qkv_blocks]
    gains = jnp.stack(
        [sum(jnp.where((me_line ^ m) == f, gains[m], 0.0) for m in range(size)) for f in range(size)]
    )
    gain_one = gains[:, :, :shard].reshape(1, width)
    gain_two = gains[:, :, shard:].reshape(1, width)
    inverse = rope_base ** (-(jnp.arange(HD // 2, dtype=f32) * 2.0) / HD)
    angles = positions.astype(f32)[:, :, None] * jnp.tile(inverse, 4)[None, None, :]
    cosine, sine = jnp.cos(angles), jnp.sin(angles)
    down_parts = lax.all_gather(
        jnp.concatenate([down_weight, output_weight], axis=0), "fsdp", axis=0, tiled=False
    )
    wo_parts = lax.all_gather(down_parts[:, part:], "seq", axis=0, tiled=False)
    w_gate_up = packed[:, :, : 2 * hidden_cols]
    for block in [*qkv_blocks[1:], x_blocks[2], x_blocks[4], x_blocks[6], cosine, sine]:
        w_gate_up = after(w_gate_up, block)
    w_gate_up = lax.all_gather(w_gate_up, "fsdp", axis=0, tiled=False).reshape(width, 2 * hidden_cols)
    cot_blocks = {0: cotangent}
    for mask in (2, 4):
        cot_blocks[mask] = swap(after(cotangent, x_blocks[6]), mask)
    cot_blocks[6] = swap(cot_blocks[2], 4)
    for mask in (0, 2, 4, 6):
        cot_blocks[mask + 1] = swap(cot_blocks[mask], 1)

    scales = jnp.concatenate(
        [jnp.tile(query_gain, 2)[None], jnp.tile(key_gain, 2)[None], jnp.zeros((6, 128), bf16)]
    ).astype(f32)
    starts = jnp.arange(length, dtype=jnp.int32)[None, :] - positions
    x_full, normed_in, qkv_raw, q_rows, kv_rows, w_qkv = qkv_fwd(
        at, x_blocks, qkv_blocks, gain_one, scales, cosine, sine, []
    )
    starts_wide = jnp.broadcast_to(starts[:, :, None], (seqs, length, 128))
    outputs, totals = attn_fwd(q_rows, kv_rows, starts_wide, span, [cot_blocks[2], cot_blocks[4]])

    (attn_rows, residual_mid, normed_mid, hidden, ff_grads, gnm_even, gnm_odd, out_even, out_odd, cot_full, w_out) = ffn(
        at,
        partner_blocks(outputs),
        [cot_blocks[j] for j in range(8)],
        down_parts,
        x_full,
        wo_parts,
        w_gate_up,
        gain_two,
    )
    flat = lambda array: array.reshape(rows, -1)

    mid_stages = reduce_stages(gnm_even, gnm_odd)
    cuts = ((0, hidden_cols), (padded, padded + hidden_cols))
    down_term = product(
        flat(hidden), flat(cot_full), (size, 1, part), ((0, width),), 16 * rows * width
    )
    grad_mid, grad_mid_half, grad_attn_out = mid_bwd(
        at, residual_mid, cotangent, gain_two, w_out, gnm_even, mid_stages, [down_term]
    )
    grad_heads = spread(grad_attn_out)
    gate_up_term = product(
        flat(normed_mid), flat(ff_grads), (size, groups, shard), cuts, 32 * rows * width, [grad_mid_half]
    )

    def block_rows(term, f, count):
        return lax.dynamic_slice_in_dim(term, f * count, count, term.ndim - 2)

    gate_up_sum = lax.psum_scatter(gate_up_term, "fsdp", scatter_dimension=0, tiled=False)
    down_sum = lax.psum_scatter(down_term, "fsdp", scatter_dimension=0, tiled=False)
    attn_own = lax.dynamic_slice_in_dim(attn_rows, me * span, span, 1).reshape(own_rows, width)
    output_term = matmul_tn(attn_own, grad_mid_half).astype(bf16)
    output_term = output_term.reshape(size, groups, shard, width).transpose(1, 0, 2, 3)
    output_term = lax.psum_scatter(output_term, "seq", scatter_dimension=0, tiled=False)
    output_sum = lax.psum_scatter(output_term, "fsdp", scatter_dimension=0, tiled=False)
    out_stages = reduce_stages(out_even, out_odd, [grad_heads, gate_up_term])
    gate_up_home = spread(gate_up_sum)

    totals_row = jnp.stack([totals[:, :, 0], totals[:, :, HD]], axis=1)
    totals_row = jnp.concatenate([totals_row, jnp.zeros((seqs, 6, length), f32)], axis=1)
    starts_row = jnp.broadcast_to(starts[:, None, :], (seqs, 8, length))
    grad_q, grad_kv = attn_bwd(
        q_rows, kv_rows, grad_heads, outputs, totals_row, starts_row, span, [out_stages[0], gate_up_term]
    )
    gin_even, gin_odd, qkv_term, head_gains = qkv_bwd(
        at, grad_q, grad_kv, qkv_raw, normed_in, w_qkv, scales, cosine, sine,
        [*out_stages[1:], down_sum]
    )
    in_stages = reduce_stages(gin_even, gin_odd)
    own_in = block_input.reshape(own_rows, width).astype(f32)
    grad_normed_in = own_sum(gin_even, in_stages).reshape(own_rows, width)
    input_grad = (
        (grad_mid + norm_bwd(own_in, inv_rms(own_in), gain_one, grad_normed_in))
        .astype(bf16)
        .reshape(seqs, span, width)
    )

    def two_terms(array):
        high = array.astype(bf16)
        low = (array - high.astype(f32)).astype(bf16)
        return jnp.concatenate([high, low, jnp.zeros((14, array.shape[1]), bf16)], axis=0)

    gain_rows = two_terms(head_gains[:2].reshape(1, 256))

    def sent_rows(f):
        block = after(block_rows(qkv_term, f, groups * shard), in_stages[0])
        return jnp.concatenate([block, gain_rows], axis=0)

    qkv_parts = line_parts(sent_rows)
    qkv_sum = add_up(sent_rows(me_line), qkv_parts)
    gain_rows = two_terms(qkv_sum[-16:-15] + qkv_sum[-15:-14])
    qkv_sum = qkv_sum[:-16].astype(bf16).reshape(groups, shard, 4 * HD)
    gain_rows = jnp.broadcast_to(gain_rows[None], (groups, *gain_rows.shape))
    query_grad, key_grad, value_grad, gain_one_sum, head_gains = unpack_heads(
        spread(jnp.concatenate([qkv_sum, gain_rows], axis=1)), query_weight, key_weight, value_weight
    )
    head_gains = (head_gains[0] + head_gains[1]).reshape(2, 128)

    residual_own = lax.dynamic_slice_in_dim(residual_mid, me * span, span, 1)
    block_output = after(residual_own + own_sum(out_even, out_stages), qkv_parts[0]).astype(bf16)
    down_grad = after(down_sum.astype(f32), qkv_parts[0]).reshape(part, width)
    output_grad = after(output_sum.astype(f32), qkv_parts[0])
    gate_grad, up_grad, gain_two_sum = unpack_columns(gate_up_home, gate_weight, up_weight, part, qkv_parts[0])

    gain_one_grad = gain_one_sum[:, 0] / attention_gain.astype(f32)
    gain_two_grad = gain_two_sum[:, 0] / feedforward_gain.astype(f32)

    return (
        block_output,
        input_grad,
        gain_one_grad,
        query_grad,
        key_grad,
        value_grad,
        head_gains[0, :HD] + head_gains[0, HD:],
        head_gains[1, :HD],
        output_grad,
        gain_two_grad,
        gate_grad,
        up_grad,
        down_grad,
    )


def solution(mesh):
    shards = P(("fsdp", "seq"), None)
    vector = P(("fsdp", "seq"))
    tokens = P("fsdp", "seq", None)
    return jax.shard_map(
        body,
        mesh=mesh,
        in_specs=(
            tokens,
            P("fsdp", None),
            tokens,
            vector,
            shards,
            shards,
            shards,
            P(),
            P(),
            shards,
            vector,
            shards,
            shards,
            shards,
        ),
        out_specs=(
            tokens,
            tokens,
            vector,
            shards,
            shards,
            shards,
            P(),
            P(),
            shards,
            vector,
            shards,
            shards,
            shards,
        ),
        check_vma=False,
    )
```

```python
import functools

import jax
import jax.numpy as jnp
from jax import lax
from jax.experimental import pallas as pl
from jax.experimental.pallas import tpu as pltpu
from jax.sharding import PartitionSpec as P

H = 16
KV = 8
HD = 64

rope_base = 1000000.0
eps = 1e-05
masked = -1e30
f32 = jnp.float32
bf16 = jnp.bfloat16


def contract(formula, left, right):
    return jnp.einsum(formula, left, right, preferred_element_type=f32)


def matmul(left, right):
    return jnp.dot(left, right, preferred_element_type=f32)


def matmul_nt(left, right):
    return lax.dot_general(left, right, (((1,), (1,)), ((), ())), preferred_element_type=f32)


def matmul_tn(left, right):
    return lax.dot_general(left, right, (((0,), (0,)), ((), ())), preferred_element_type=f32)


def rope_tables(places, head_width):
    half_width = head_width // 2
    inverse = rope_base ** (-(jnp.arange(half_width, dtype=f32) * 2.0) / head_width)
    angles = places.astype(f32)[:, None] * inverse[None, :]
    return (jnp.cos(angles)[:, None, :], jnp.sin(angles)[:, None, :])


def head_prep(raw_rows, gain_row, cosine, sine, head_count):
    row_count = raw_rows.shape[0]
    split_rows = raw_rows.reshape(row_count, head_count, -1)
    factor = lax.rsqrt(jnp.mean(split_rows * split_rows, axis=-1, keepdims=True) + eps)
    normed = split_rows * factor * gain_row
    half_width = normed.shape[-1] // 2
    lower = normed[..., :half_width]
    upper = normed[..., half_width:]
    turned = jnp.concatenate(
        [lower * cosine - upper * sine, upper * cosine + lower * sine], axis=-1
    )
    return turned.reshape(row_count, -1)


def inv_rms(values):
    return lax.rsqrt(jnp.mean(values * values, axis=-1, keepdims=True) + eps)


def norm_bwd(values, factor, gain_row, grad_result):
    normed = values * factor
    grad_normed = grad_result * gain_row
    return factor * (
        grad_normed - normed * jnp.mean(grad_normed * normed, axis=-1, keepdims=True)
    )


def masked_scores(queries, key_rows, doc_start, begin_row, end_row, scaling):
    query_index = jnp.arange(begin_row, end_row, dtype=jnp.int32)
    key_index = jnp.arange(end_row, dtype=jnp.int32)
    allowed = (key_index[None, :] <= query_index[:, None]) & (
        key_index[None, :] >= doc_start[begin_row:end_row, None]
    )
    scores = contract("qhd,khd->hqk", queries[begin_row:end_row], key_rows[:end_row]) * scaling
    return jnp.where(allowed[None, :, :], scores, masked)


def attend_fwd(queries, key_rows, value_rows, doc_start):
    seq_length, head_count, head_width = queries.shape
    block_rows = min(512, seq_length)
    scaling = head_width ** (-0.5)
    out_blocks = []
    total_blocks = []
    for begin_row in range(0, seq_length, block_rows):
        end_row = begin_row + block_rows
        scores = masked_scores(queries, key_rows, doc_start, begin_row, end_row, scaling)
        largest = jnp.max(scores, axis=-1, keepdims=True)
        log_total = largest + jnp.log(jnp.sum(jnp.exp(scores - largest), axis=-1, keepdims=True))
        attn_prob = jnp.exp(scores - log_total).astype(bf16)
        out_blocks.append(contract("hqk,khd->qhd", attn_prob, value_rows[:end_row]).astype(bf16))
        total_blocks.append(log_total[..., 0])
    return (jnp.concatenate(out_blocks, axis=0), jnp.concatenate(total_blocks, axis=1))


def attend_bwd(queries, key_rows, value_rows, outputs, log_totals, grad_result, doc_start):
    seq_length, head_count, head_width = queries.shape
    block_rows = min(512, seq_length)
    scaling = head_width ** (-0.5)
    carried = jnp.sum(grad_result.astype(f32) * outputs.astype(f32), axis=-1).T
    grad_query = []
    grad_key = jnp.zeros((seq_length, head_count, head_width), f32)
    grad_value = jnp.zeros((seq_length, head_count, head_width), f32)
    for begin_row in range(0, seq_length, block_rows):
        end_row = begin_row + block_rows
        scores = masked_scores(queries, key_rows, doc_start, begin_row, end_row, scaling)
        attn_prob = jnp.exp(scores - log_totals[:, begin_row:end_row, None])
        prob_half = attn_prob.astype(bf16)
        grad_rows = grad_result[begin_row:end_row]
        grad_value = grad_value.at[:end_row].add(contract("hqk,qhd->khd", prob_half, grad_rows))
        grad_prob = contract("qhd,khd->hqk", grad_rows, value_rows[:end_row])
        grad_score = (
            attn_prob * (grad_prob - carried[:, begin_row:end_row, None]) * scaling
        ).astype(bf16)
        grad_query.append(contract("hqk,khd->qhd", grad_score, key_rows[:end_row]))
        grad_key = grad_key.at[:end_row].add(
            contract("hqk,qhd->khd", grad_score, queries[begin_row:end_row])
        )
    return (
        jnp.concatenate(grad_query, axis=0).astype(bf16),
        grad_key.astype(bf16),
        grad_value.astype(bf16),
    )


def swap(array, mask):
    groups = lax.axis_size("seq")
    return lax.ppermute(array, "seq", [(i, i ^ mask) for i in range(groups)])


def partner_blocks(block, direct=False):
    got = {0: block, 2: swap(block, 2), 4: swap(block, 4)}
    got[6] = swap(block, 6) if direct else swap(got[4], 2)
    for mask in (0, 2, 4, 6):
        got[mask + 1] = swap(got[mask], 1)
    return [got[j] for j in range(8)]


def gather_seq(block, axis):
    if lax.axis_size("seq") != 8 or block.shape[0] % 2:
        return lax.all_gather(block, "seq", axis=axis, tiled=True)
    me = lax.axis_index("seq")
    width = block.shape[axis]
    shape = list(block.shape)
    shape[axis] = width * 8
    whole = jnp.zeros(shape, block.dtype)
    for j, part in enumerate(partner_blocks(block)):
        whole = lax.dynamic_update_slice_in_dim(whole, part, (me ^ j) * width, axis)
    return whole


def reduce_seq(partial, axis):
    groups = lax.axis_size("seq")
    width = partial.shape[axis] // groups
    if groups != 8 or partial.shape[0] % 2:
        return lax.psum_scatter(partial, "seq", scatter_dimension=axis, tiled=True).astype(f32)
    me = lax.axis_index("seq")
    half = partial.shape[0] // 2

    def piece(j):
        return lax.dynamic_slice_in_dim(partial, (me ^ j) * width, width, axis)

    got = swap(jnp.stack([piece(j) for j in (1, 3, 5, 7)]), 1)
    held = {j: piece(j).astype(f32) + got[j // 2].astype(f32) for j in (0, 2, 4, 6)}
    first = {j: held[j][:half] for j in held}
    second = {j: held[j][half:] for j in held}
    sent_x = swap(jnp.stack([first[2].astype(bf16), first[6].astype(bf16)]), 2)
    sent_y = swap(jnp.stack([second[4].astype(bf16), second[6].astype(bf16)]), 4)
    last_y = swap((first[4] + sent_x[1].astype(f32)).astype(bf16), 4)
    last_x = swap((second[2] + sent_y[1].astype(f32)).astype(bf16), 2)
    own_first = first[0] + sent_x[0].astype(f32) + last_y.astype(f32)
    own_second = second[0] + sent_y[0].astype(f32) + last_x.astype(f32)
    return jnp.concatenate([own_first, own_second], axis=0)


def line_step(array, step):
    size = lax.axis_size("fsdp")
    return lax.ppermute(
        array, "fsdp", [(i, i + step) for i in range(size) if 0 <= i + step < size]
    )


def gather_line(block):
    size = lax.axis_size("fsdp")
    if size != 4:
        return lax.all_gather(block, "fsdp", axis=0, tiled=False)
    me = lax.axis_index("fsdp")
    below, above = [block], [block]
    for _ in range(size - 1):
        below.append(line_step(below[-1], 1))
        above.append(line_step(above[-1], -1))
    whole = jnp.zeros((size,) + block.shape, block.dtype)
    whole = lax.dynamic_update_index_in_dim(whole, block, me, 0)
    for k in range(1, size):
        part = below[k] + above[size - k]
        whole = lax.dynamic_update_index_in_dim(whole, part, lax.rem(me - k + size, size), 0)
    return whole


def reduce_line(partial):
    size = lax.axis_size("fsdp")
    if size != 4:
        return lax.psum_scatter(
            partial.astype(bf16), "fsdp", scatter_dimension=0, tiled=False
        ).astype(f32)
    me = lax.axis_index("fsdp")

    def entry(k):
        return lax.dynamic_index_in_dim(
            partial, lax.rem(me + k + size, size), 0, keepdims=False
        ).astype(f32)

    up, down = entry(size - 1), entry(1 - size)
    for k in range(size - 2, -1, -1):
        got_up = line_step(up.astype(bf16), 1).astype(f32)
        got_down = line_step(down.astype(bf16), -1).astype(f32)
        if k:
            up, down = entry(k) + got_up, entry(-k) + got_down
    return entry(0) + got_up + got_down


def spread(blocks):
    return lax.all_to_all(blocks, "seq", split_axis=0, concat_axis=0, tiled=True)


def sum_everywhere(vector):
    groups, size = lax.axis_size("seq"), lax.axis_size("fsdp")
    if groups != 8 or size != 4:
        return lax.psum(vector, ("fsdp", "seq"))
    for mask in (1, 2, 4):
        vector = vector + swap(vector, mask)
    for mask in (1, 2):
        vector = vector + lax.ppermute(vector, "fsdp", [(i, i ^ mask) for i in range(size)])
    return vector


exact = lax.Precision.HIGHEST


def dot_nt(left, right, precision=None):
    return lax.dot_general(left, right, (((1,), (1,)), ((), ())), precision=precision, preferred_element_type=f32)


def dot_tn(left, right):
    return lax.dot_general(left, right, (((0,), (0,)), ((), ())), preferred_element_type=f32)


def head_mean():
    row = lax.broadcasted_iota(jnp.int32, (128, 128), 0) // HD
    col = lax.broadcasted_iota(jnp.int32, (128, 128), 1) // HD
    return jnp.where(row == col, 1.0 / HD, 0.0).astype(bf16)


def head_average(array):
    high = array.astype(bf16)
    low = (array - high.astype(f32)).astype(bf16)
    mean = head_mean()
    return jnp.dot(high, mean, preferred_element_type=f32) + jnp.dot(low, mean, preferred_element_type=f32)


def lane_index(rows):
    return lax.broadcasted_iota(jnp.int32, (rows, 128), 1)


def half_turn(array, back):
    low = (lane_index(array.shape[0]) % HD) < HD // 2
    ahead = pltpu.roll(array, 128 - HD // 2, 1)
    behind = pltpu.roll(array, HD // 2, 1)
    return jnp.where(low, ahead, -behind) if back else jnp.where(low, -ahead, behind)


def attn_fwd_kernel(block, q_ref, kv_ref, start_ref, *refs):
    out_ref, lse_ref = refs[-2:]
    step = pl.program_id(1)
    steps = kv_ref.shape[1] // block
    lanes = lane_index(block)

    for at in range(steps):
        end = (at + 1) * block

        @pl.when(step == at)
        def _(at=at, end=end):
            k = kv_ref[0, :end, :HD]
            v = kv_ref[0, :end, HD:]
            q_index = at * block + lax.broadcasted_iota(jnp.int32, (block, end), 0)
            k_index = lax.broadcasted_iota(jnp.int32, (block, end), 1)
            allowed = (k_index <= q_index) & (k_index >= start_ref[0][:, :1])
            outs, totals = [], []
            for head in range(2):
                q = q_ref[0, :, head * HD : (head + 1) * HD] * jnp.array(HD ** -0.5, bf16)
                scores = jnp.where(allowed, dot_nt(q, k), masked)
                largest = jnp.max(scores, axis=-1, keepdims=True)
                weights = jnp.exp(scores - largest)
                total = jnp.sum(weights, axis=-1, keepdims=True)
                out = jnp.dot(weights.astype(bf16), v, preferred_element_type=f32) / total
                outs.append(out.astype(bf16))
                totals.append(largest + jnp.log(total))
            out_ref[0] = jnp.concatenate(outs, axis=1)
            lse_ref[0] = jnp.where(lanes < HD, totals[0], totals[1])


def attn_fwd(q, kv, starts, span, earlier):
    seqs, length, _ = q.shape
    block = 2 * span
    rows = lambda b, i: (b, i, 0)
    whole = lambda b, i: (b, 0, 0)
    return pl.pallas_call(
        functools.partial(attn_fwd_kernel, block),
        grid=(seqs, length // block),
        in_specs=[
            pl.BlockSpec((1, block, 128), rows),
            pl.BlockSpec((1, length, 128), whole),
            pl.BlockSpec((1, block, 128), rows),
        ]
        + [pl.BlockSpec(memory_space=pl.ANY)] * len(earlier),
        out_specs=[pl.BlockSpec((1, block, 128), rows), pl.BlockSpec((1, block, 128), rows)],
        out_shape=[
            jax.ShapeDtypeStruct((seqs, length, 128), bf16),
            jax.ShapeDtypeStruct((seqs, length, 128), f32),
        ],
        compiler_params=pltpu.CompilerParams(vmem_limit_bytes=48 << 20),
        cost_estimate=pl.CostEstimate(flops=seqs * length * length * 256, bytes_accessed=seqs * length * 1792, transcendentals=seqs * length * length),
        name="attn_fwd",
    )(q, kv, starts, *earlier)


def attn_bwd_kernel(block, q_ref, kv_ref, do_ref, o_ref, lse_ref, start_ref, *refs):
    dq_ref, dkv_ref, dk_acc, dv_acc = refs[-4:]
    step = pl.program_id(1)
    steps = kv_ref.shape[1] // block

    @pl.when(step == 0)
    def _():
        dk_acc[...] = jnp.zeros_like(dk_acc)
        dv_acc[...] = jnp.zeros_like(dv_acc)

    for at in range(steps):
        end = (at + 1) * block

        @pl.when(step == at)
        def _(at=at, end=end):
            k = kv_ref[0, :end, :HD]
            v = kv_ref[0, :end, HD:]
            k_index = lax.broadcasted_iota(jnp.int32, (end, block), 0)
            q_index = at * block + lax.broadcasted_iota(jnp.int32, (end, block), 1)
            allowed = (k_index <= q_index) & (k_index >= start_ref[0, 0:1, :])
            do_rows = do_ref[...].reshape(block, 128)
            product = do_rows.astype(f32) * o_ref[0].astype(f32)
            dqs = []
            for head in range(2):
                cut = slice(head * HD, (head + 1) * HD)
                q = q_ref[0, :, cut] * jnp.array(HD ** -0.5, bf16)
                do = do_rows[:, cut]
                delta = dot_nt(jnp.ones((8, HD), f32), product[:, cut], exact)[0:1, :]
                scores = jnp.where(allowed, dot_nt(k, q), masked)
                prob = jnp.exp(scores - lse_ref[0, head : head + 1, :])
                dv_acc[:end, :] += jnp.dot(prob.astype(bf16), do, preferred_element_type=f32)
                dscore = (prob * (dot_nt(v, do) - delta)).astype(bf16)
                dk_acc[:end, :] += jnp.dot(dscore, q, preferred_element_type=f32)
                dqs.append(dot_tn(dscore, k) * (HD ** -0.5))
            dq_ref[0] = jnp.concatenate(dqs, axis=1)

    @pl.when(step == steps - 1)
    def _():
        dkv_ref[0] = jnp.concatenate([dk_acc[...], dv_acc[...]], axis=1)


def attn_bwd(q, kv, do, out, lse, starts, span, earlier):
    seqs, length, _ = q.shape
    block = 2 * span
    rows = lambda b, i: (b, i, 0)
    cols = lambda b, i: (b, 0, i)
    whole = lambda b, i: (b, 0, 0)
    return pl.pallas_call(
        functools.partial(attn_bwd_kernel, block),
        grid=(seqs, length // block),
        in_specs=[
            pl.BlockSpec((1, block, 128), rows),
            pl.BlockSpec((1, length, 128), whole),
            pl.BlockSpec((2, 1, span, 128), lambda b, i: (i, b, 0, 0)),
            pl.BlockSpec((1, block, 128), rows),
            pl.BlockSpec((1, 8, block), cols),
            pl.BlockSpec((1, 8, block), cols),
        ]
        + [pl.BlockSpec(memory_space=pl.ANY)] * len(earlier),
        out_specs=[pl.BlockSpec((1, block, 128), rows), pl.BlockSpec((1, length, 128), whole)],
        out_shape=[
            jax.ShapeDtypeStruct((seqs, length, 128), f32),
            jax.ShapeDtypeStruct((seqs, length, 128), f32),
        ],
        scratch_shapes=[pltpu.VMEM((length, HD), f32), pltpu.VMEM((length, HD), f32)],
        compiler_params=pltpu.CompilerParams(vmem_limit_bytes=56 << 20),
        cost_estimate=pl.CostEstimate(flops=seqs * length * length * 8192, bytes_accessed=seqs * length * 2560, transcendentals=seqs * length * length),
        name="attn_bwd",
    )(q, kv, do, out, lse, starts, *earlier)


def any_space(count):
    return [pl.BlockSpec(memory_space=pl.ANY)] * count


def pack_kernel(groups, part, gate_ref, up_ref, q_ref, k_ref, v_ref, gain_ref, out_ref):
    size = gate_ref.shape[1] // (groups * part)
    hidden = size * part
    for at, ref in ((0, gate_ref), (hidden, up_ref)):
        whole = ref[...].astype(f32)
        for g in range(groups):
            cuts = [whole[:, (f * groups + g) * part : (f * groups + g + 1) * part] for f in range(size)]
            out_ref[g, :, at : at + hidden] = jnp.concatenate(cuts, axis=1).astype(bf16)
    k, v = k_ref[...].astype(f32), v_ref[...].astype(f32)
    for g in range(groups):
        at = slice(g * HD, (g + 1) * HD)
        out_ref[g, :, 2 * hidden : 2 * hidden + 128] = q_ref[:, g * 128 : (g + 1) * 128]
        both = jnp.concatenate([k[:, at], v[:, at]], axis=1)
        out_ref[g, :, 2 * hidden + 128 : 2 * hidden + 256] = both.astype(bf16)
        out_ref[g, :, 2 * hidden + 256 :] = gain_ref[...]


def pack_columns(gate, up, query, key, value, gains, groups, part):
    shard, total = gate.shape
    return pl.pallas_call(
        functools.partial(pack_kernel, groups, part),
        out_shape=jax.ShapeDtypeStruct((groups, shard, 2 * total // groups + 384), bf16),
        name="pack",
    )(gate, up, query, key, value, gains)


def unpack_kernel(part, home_ref, gate_w_ref, up_w_ref, _, gate_ref, up_ref, sum_ref):
    groups, _, shard, hidden = home_ref.shape
    size = hidden // part
    for which, ref in ((0, gate_ref), (1, up_ref)):
        rows = [home_ref[g, which].astype(f32) for g in range(groups)]
        cuts = [rows[g][:, f * part : (f + 1) * part] for f in range(size) for g in range(groups)]
        ref[...] = jnp.concatenate(cuts, axis=1)
    total = jnp.sum(gate_w_ref[...].astype(f32) * gate_ref[...], axis=1, keepdims=True)
    total += jnp.sum(up_w_ref[...].astype(f32) * up_ref[...], axis=1, keepdims=True)
    sum_ref[...] = jnp.broadcast_to(total, sum_ref.shape)


def unpack_columns(home, gate_w, up_w, part, earlier):
    shape = gate_w.shape
    return pl.pallas_call(
        functools.partial(unpack_kernel, part),
        in_specs=[pl.BlockSpec(memory_space=pltpu.VMEM)] * 3 + any_space(1),
        out_shape=[
            jax.ShapeDtypeStruct(shape, f32),
            jax.ShapeDtypeStruct(shape, f32),
            jax.ShapeDtypeStruct((shape[0], 128), f32),
        ],
        name="unpack",
    )(home, gate_w, up_w, earlier)


def unpack_heads_kernel(home_ref, q_w_ref, k_w_ref, v_w_ref, q_ref, k_ref, v_ref, sum_ref, gain_ref):
    groups, shard = home_ref.shape[0], q_ref.shape[0]
    blocks = [home_ref[g].astype(f32) for g in range(groups)]
    q_ref[...] = jnp.concatenate([block[:shard, : 2 * HD] for block in blocks], axis=1)
    k_ref[...] = jnp.concatenate([block[:shard, 2 * HD : 3 * HD] for block in blocks], axis=1)
    v_ref[...] = jnp.concatenate([block[:shard, 3 * HD :] for block in blocks], axis=1)
    total = 0.0
    for weight, grad in ((q_w_ref, q_ref), (k_w_ref, k_ref), (v_w_ref, v_ref)):
        total += jnp.sum(weight[...].astype(f32) * grad[...], axis=1, keepdims=True)
    sum_ref[...] = jnp.broadcast_to(total, sum_ref.shape)
    gain_ref[...] = sum(block[shard : shard + 8] for block in blocks)


def unpack_heads(home, q_w, k_w, v_w):
    return pl.pallas_call(
        unpack_heads_kernel,
        out_shape=[jax.ShapeDtypeStruct(w.shape, f32) for w in (q_w, k_w, v_w)]
        + [jax.ShapeDtypeStruct((q_w.shape[0], 128), f32), jax.ShapeDtypeStruct((8, home.shape[2]), f32)],
        name="unpack_heads",
    )(home, q_w, k_w, v_w)


def qkv_fwd_kernel(at_ref, *refs):
    x_refs, w_refs = refs[:8], refs[8:12]
    gain_ref, scale_ref, cos_ref, sin_ref, x_out, nm_ref, raw_ref, q_ref, kv_ref, w_ref = refs[12:]
    step = pl.program_id(0)
    shard = w_ref.shape[0] // 32

    @pl.when(step == 0)
    def _():
        for m in range(4):
            for g in range(8):
                row = pl.multiple_of(((at_ref[1] ^ m) * 8 + g) * shard, shard)
                w_ref[pl.ds(row, shard), :] = w_refs[m][g, :, :256]

    for j in range(8):

        @pl.when(step == j)
        def _(j=j):
            x_out[...] = x_refs[j][...]

    x = x_out[...].reshape(-1, x_out.shape[-1]).astype(f32)
    factor = lax.rsqrt(jnp.mean(x * x, axis=-1, keepdims=True) + eps)
    nm = (x * factor * gain_ref[...]).astype(bf16)
    nm_ref[...] = nm.reshape(nm_ref.shape)
    raw = jnp.dot(nm, w_ref[...], preferred_element_type=f32)
    raw_ref[...] = raw.reshape(raw_ref.shape)
    cos = cos_ref[...].reshape(-1, 128)
    sin = sin_ref[...].reshape(-1, 128)

    def prepared(part, scale):
        inv = lax.rsqrt(head_average(part * part) + eps)
        normed = part * inv * scale
        return normed * cos + half_turn(normed, False) * sin

    q = prepared(raw[:, :128], scale_ref[0:1, :])
    kv = prepared(raw[:, 128:], scale_ref[1:2, :])
    kv = jnp.where(lane_index(kv.shape[0]) < HD, kv, raw[:, 128:])
    q_ref[...] = q.astype(bf16).reshape(q_ref.shape)
    kv_ref[...] = kv.astype(bf16).reshape(kv_ref.shape)


def qkv_fwd(at, x_blocks, w_blocks, gain, scales, cosine, sine, earlier):
    seqs, span, width = x_blocks[0].shape
    length = 8 * span
    home = lambda j, m: (0, m[0] ^ j, 0)
    fixed = lambda j, m: (0, 0)
    once = dict(pipeline_mode=pl.Buffered(1))

    def kernel(at_ref, *refs):
        qkv_fwd_kernel(at_ref, *refs[:16], *refs[16 + len(earlier) :])

    return pl.pallas_call(
        kernel,
        grid_spec=pltpu.PrefetchScalarGridSpec(
            num_scalar_prefetch=1,
            grid=(8,),
            in_specs=[pl.BlockSpec((seqs, span, width), lambda j, m: (0, 0, 0), **once)] * 8
            + [pl.BlockSpec(w_blocks[0].shape, lambda j, m: (0, 0, 0), **once)] * 4
            + [
                pl.BlockSpec((1, width), fixed, **once),
                pl.BlockSpec((8, 128), fixed, **once),
                pl.BlockSpec((seqs, span, 128), home),
                pl.BlockSpec((seqs, span, 128), home),
            ]
            + any_space(len(earlier)),
            out_specs=[
                pl.BlockSpec((seqs, span, width), home),
                pl.BlockSpec((seqs, span, width), home),
                pl.BlockSpec((seqs, span, 256), home),
                pl.BlockSpec((seqs, span, 128), home),
                pl.BlockSpec((seqs, span, 128), home),
                pl.BlockSpec((width, 256), fixed),
            ],
        ),
        out_shape=[
            jax.ShapeDtypeStruct((seqs, length, width), bf16),
            jax.ShapeDtypeStruct((seqs, length, width), bf16),
            jax.ShapeDtypeStruct((seqs, length, 256), f32),
            jax.ShapeDtypeStruct((seqs, length, 128), bf16),
            jax.ShapeDtypeStruct((seqs, length, 128), bf16),
            jax.ShapeDtypeStruct((width, 256), bf16),
        ],
        compiler_params=pltpu.CompilerParams(vmem_limit_bytes=40 << 20),
        cost_estimate=pl.CostEstimate(flops=16 * seqs * length * width * 256, bytes_accessed=seqs * length * width * 6, transcendentals=0),
        name="qkv_fwd",
    )(at, *x_blocks, *w_blocks, gain, scales, cosine, sine, *earlier)


def halves_spec(seqs, span, width):
    return pl.BlockSpec((1, seqs, span, width), lambda t, m: ((m[0] ^ t) >> 1, 0, 0, 0))


def store_halves(me, step, value, even_ref, odd_ref):
    odd = ((me ^ step) & 1) == 1

    @pl.when(odd)
    def _():
        odd_ref[...] = value.reshape(odd_ref.shape)

    @pl.when(jnp.logical_not(odd))
    def _():
        even_ref[...] = value.reshape(even_ref.shape)


def ffn_kernel(hidden, padded, at_ref, *refs):
    parts, cot_refs, wd_parts = refs[:8], refs[8:16], refs[16]
    (x_ref, wo_parts, wgu_ref, gain_ref, attn_ref, mid_ref, nm_ref, hid_ref, grads_ref) = refs[17:26]
    gnm_even, gnm_odd, out_even, out_odd, cot_ref, wo_ref, wgu, wd = refs[26:]
    step = pl.program_id(0)

    @pl.when(step == 0)
    def _():
        shard = wo_parts.shape[2]
        part = wd_parts.shape[1] - shard
        wgu[...] = jnp.zeros_like(wgu)
        wgu[:, :hidden] = wgu_ref[:, :hidden]
        wgu[:, padded : padded + hidden] = wgu_ref[:, hidden:]
        wd[hidden:, :] = jnp.zeros((padded - hidden, wd.shape[1]), bf16)
        for f in range(wd_parts.shape[0]):
            wd[f * part : (f + 1) * part, :] = wd_parts[f, :part, :]
            for g in range(8):
                row = (f * 8 + g) * shard
                wo_ref[row : row + shard, :] = wo_parts[g, f]

    for j in range(8):

        @pl.when((at_ref[0] ^ step) == j)
        def _(j=j):
            cot_ref[...] = cot_refs[j][...]

    tile = attn_ref.shape[0] * attn_ref.shape[1]
    width = wo_ref.shape[0]
    for j in range(8):
        at = pl.multiple_of((at_ref[0] ^ j) * 128, 128)
        attn_ref[:, :, pl.ds(at, 128)] = parts[j][...]
    attn = attn_ref[...].reshape(tile, width)
    mid = x_ref[...].reshape(tile, width).astype(f32) + jnp.dot(attn, wo_ref[...], preferred_element_type=f32)
    mid_ref[...] = mid.reshape(mid_ref.shape)
    factor = lax.rsqrt(jnp.mean(mid * mid, axis=-1, keepdims=True) + eps)
    nm = (mid * factor * gain_ref[...]).astype(bf16)
    nm_ref[...] = nm.reshape(nm_ref.shape)
    both = jnp.dot(nm, wgu[...], preferred_element_type=f32)
    gate, up = both[:, :padded], both[:, padded:]
    sigma = jax.nn.sigmoid(gate)
    hid = (gate * sigma * up).astype(bf16)
    hid_ref[...] = hid.reshape(hid_ref.shape)
    grad_hidden = dot_nt(cot_ref[...].reshape(tile, width), wd[...])
    grad_gate = (grad_hidden * up * sigma * (1.0 + gate * (1.0 - sigma))).astype(bf16)
    grad_up = (grad_hidden * gate * sigma).astype(bf16)
    grads = jnp.concatenate([grad_gate, grad_up], axis=1)
    grads_ref[...] = grads.reshape(grads_ref.shape)
    store_halves(at_ref[0], step, dot_nt(grads, wgu[...]).astype(bf16), gnm_even, gnm_odd)
    out = jnp.dot(hid, wd[...], preferred_element_type=f32).astype(bf16)
    store_halves(at_ref[0], step, out, out_even, out_odd)


def ffn(at, parts, cot_blocks, wd_parts, x, wo_parts, w_gate_up, gain):
    seqs, length, width = x.shape
    span = length // 8
    hidden = w_gate_up.shape[1] // 2
    padded = -(-hidden // 128) * 128
    home = lambda t, m: (0, t, 0)
    fixed = lambda t, m: (0, 0)
    once = dict(pipeline_mode=pl.Buffered(1))
    tokens = lambda cols: pl.BlockSpec((seqs, span, cols), home)
    shape = lambda cols, kind: jax.ShapeDtypeStruct((seqs, length, cols), kind)
    half = jax.ShapeDtypeStruct((4, seqs, span, width), bf16)
    return pl.pallas_call(
        functools.partial(ffn_kernel, hidden, padded),
        grid_spec=pltpu.PrefetchScalarGridSpec(
            num_scalar_prefetch=1,
            grid=(8,),
            in_specs=[tokens(128)] * 8
            + [pl.BlockSpec((seqs, span, width), lambda t, m: (0, 0, 0), **once)] * 8
            + [pl.BlockSpec(wd_parts.shape, lambda t, m: (0, 0, 0), **once)]
            + [
                tokens(width),
                pl.BlockSpec(wo_parts.shape, lambda t, m: (0, 0, 0, 0), **once),
                pl.BlockSpec((width, 2 * hidden), fixed, **once),
                pl.BlockSpec((1, width), fixed, **once),
            ],
            out_specs=[tokens(width), tokens(width), tokens(width), tokens(padded), tokens(2 * padded)]
            + [halves_spec(seqs, span, width)] * 4
            + [tokens(width), pl.BlockSpec((width, width), fixed)],
            scratch_shapes=[pltpu.VMEM((width, 2 * padded), bf16), pltpu.VMEM((padded, width), bf16)],
        ),
        out_shape=[shape(width, bf16), shape(width, f32), shape(width, bf16), shape(padded, bf16), shape(2 * padded, bf16)]
        + [half] * 4
        + [shape(width, bf16), jax.ShapeDtypeStruct((width, width), bf16)],
        compiler_params=pltpu.CompilerParams(vmem_limit_bytes=60 << 20),
        cost_estimate=pl.CostEstimate(flops=seqs * length * width * (2 * width + 12 * padded), bytes_accessed=seqs * length * width * 20, transcendentals=seqs * length * padded),
        name="ffn",
    )(at, *parts, *cot_blocks, wd_parts, x, wo_parts, w_gate_up, gain)


def product_kernel(cuts, left_ref, right_ref, *refs):
    out_ref, total = refs[-2:]
    step = pl.program_id(0)
    value = dot_tn(left_ref[...], right_ref[...])

    @pl.when(step == 0)
    def _():
        total[...] = value

    @pl.when(step > 0)
    def _():
        total[...] += value

    @pl.when(step == pl.num_programs(0) - 1)
    def _():
        size, blocks, _, count, _ = out_ref.shape
        for f in range(size):
            for g in range(blocks):
                row = (f * blocks + g) * count
                for i, (begin, end) in enumerate(cuts):
                    out_ref[f, g, i] = total[row : row + count, begin:end].astype(bf16)


def product(left, right, split, cuts, cost, earlier=()):
    rows = left.shape[0]
    shape = (split[0], split[1], len(cuts), split[2], cuts[0][1] - cuts[0][0])
    tile = 512
    at = lambda i: (i, 0)
    return pl.pallas_call(
        functools.partial(product_kernel, cuts),
        grid=(rows // tile,),
        in_specs=[pl.BlockSpec((tile, left.shape[1]), at), pl.BlockSpec((tile, right.shape[1]), at)]
        + any_space(len(earlier)),
        out_specs=pl.BlockSpec(shape, lambda i: (0, 0, 0, 0, 0)),
        out_shape=jax.ShapeDtypeStruct(shape, bf16),
        scratch_shapes=[pltpu.VMEM((left.shape[1], right.shape[1]), f32)],
        compiler_params=pltpu.CompilerParams(vmem_limit_bytes=48 << 20),
        cost_estimate=pl.CostEstimate(flops=cost, bytes_accessed=cost, transcendentals=0),
        name="product",
    )(left, right, *earlier)


def mid_kernel(at_ref, mid_ref, cot_ref, gain_ref, wo_ref, even_ref, got_ref, *refs):
    grad_ref, half_ref, out_ref = refs[-3:]
    seqs, span, width = cot_ref.shape
    grad_nm = even_ref[0].astype(f32) + got_ref[0].astype(f32)
    for part_ref in refs[:3]:
        grad_nm += part_ref[...].astype(f32)
    grad_nm = grad_nm.reshape(seqs * span, width)
    mid = mid_ref[...].reshape(seqs * span, width)
    factor = lax.rsqrt(jnp.mean(mid * mid, axis=-1, keepdims=True) + eps)
    normed = mid * factor
    scaled = grad_nm * gain_ref[...]
    grad = cot_ref[...].reshape(seqs * span, width).astype(f32) + factor * (
        scaled - normed * jnp.mean(scaled * normed, axis=-1, keepdims=True)
    )
    grad_ref[...] = grad
    half = grad.astype(bf16)
    half_ref[...] = half
    out = dot_nt(half, wo_ref[...]).astype(bf16)
    for g in range(8):
        out_ref[g] = out[:, g * 128 : (g + 1) * 128].reshape(seqs, span, 128)


def mid_bwd(at, mid, cot, gain, w_out, even, stages, earlier):
    seqs, span, width = cot.shape
    first = lambda *s: pl.BlockSpec((1,) + s, lambda i, m: (0,) * (len(s) + 1))
    full = lambda *s: pl.BlockSpec(s, lambda i, m: (0,) * len(s))
    rows = seqs * span
    return pl.pallas_call(
        mid_kernel,
        grid_spec=pltpu.PrefetchScalarGridSpec(
            num_scalar_prefetch=1,
            grid=(1,),
            in_specs=[
                pl.BlockSpec((seqs, span, width), lambda i, m: (0, m[0], 0)),
                full(seqs, span, width),
                full(1, width),
                full(width, width),
                first(seqs, span, width),
                first(seqs, span, width),
                full(seqs, span, width),
                full(seqs, span, width),
                full(seqs, span, width),
            ]
            + any_space(len(earlier)),
            out_specs=[full(rows, width), full(rows, width), full(8, seqs, span, 128)],
        ),
        out_shape=[
            jax.ShapeDtypeStruct((rows, width), f32),
            jax.ShapeDtypeStruct((rows, width), bf16),
            jax.ShapeDtypeStruct((8, seqs, span, 128), bf16),
        ],
        compiler_params=pltpu.CompilerParams(vmem_limit_bytes=40 << 20),
        cost_estimate=pl.CostEstimate(flops=2 * rows * width * width, bytes_accessed=rows * width * 20, transcendentals=0),
        name="mid_bwd",
    )(at, mid, cot, gain, w_out, even, *stages, *earlier)


def qkv_bwd_kernel(at_ref, dq_ref, dkv_ref, raw_ref, nm_ref, w_ref, scale_ref, cos_ref, sin_ref, *refs):
    even_ref, odd_ref, dw_ref, dscale_ref, dw_acc = refs[-5:]
    step = pl.program_id(0)
    seqs, span, width = nm_ref.shape
    tile = seqs * span

    @pl.when(step == 0)
    def _():
        dw_acc[...] = jnp.zeros_like(dw_acc)
        dscale_ref[...] = jnp.zeros_like(dscale_ref)

    cos, sin = cos_ref[...].reshape(tile, 128), sin_ref[...].reshape(tile, 128)
    def back(raw, grad, scale):
        inv = lax.rsqrt(head_average(raw * raw) + eps)
        normed = raw * inv
        turned = grad * cos + half_turn(grad * sin, True)
        grad_normed = turned * scale
        grad_raw = inv * (grad_normed - normed * head_average(grad_normed * normed))
        return grad_raw, jnp.sum(turned * normed, axis=0, keepdims=True)

    raw = raw_ref[...].reshape(tile, 256)
    grad_kv = dkv_ref[...].reshape(tile, 128)
    dq, q_scale = back(raw[:, :128], dq_ref[...].reshape(tile, 128), scale_ref[0:1, :])
    dkv, k_scale = back(raw[:, 128:], grad_kv, scale_ref[1:2, :])
    dkv = jnp.where(lane_index(tile) < HD, dkv, grad_kv)
    grad = jnp.concatenate([dq.astype(bf16), dkv.astype(bf16)], axis=1)
    dscale_ref[0:1, :] += q_scale
    dscale_ref[1:2, :] += k_scale
    store_halves(at_ref[0], step, dot_nt(grad, w_ref[...]).astype(bf16), even_ref, odd_ref)
    dw_acc[...] += dot_tn(nm_ref[...].reshape(tile, width), grad)

    @pl.when(step == pl.num_programs(0) - 1)
    def _():
        dw_ref[...] = dw_acc[...].astype(bf16)


def qkv_bwd(at, dq, dkv, raw, nm, w_qkv, scales, cosine, sine, earlier):
    seqs, length, width = nm.shape
    span = length // 8
    tokens = lambda cols: pl.BlockSpec((seqs, span, cols), lambda t, m: (0, t, 0))
    fixed = lambda t, m: (0, 0)
    half = jax.ShapeDtypeStruct((4, seqs, span, width), bf16)
    return pl.pallas_call(
        qkv_bwd_kernel,
        grid_spec=pltpu.PrefetchScalarGridSpec(
            num_scalar_prefetch=1,
            grid=(8,),
            in_specs=[
                tokens(128),
                tokens(128),
                tokens(256),
                tokens(width),
                pl.BlockSpec((width, 256), fixed),
                pl.BlockSpec((8, 128), fixed),
                tokens(128),
                tokens(128),
            ]
            + any_space(len(earlier)),
            out_specs=[halves_spec(seqs, span, width)] * 2
            + [pl.BlockSpec((width, 256), fixed), pl.BlockSpec((8, 128), fixed)],
            scratch_shapes=[pltpu.VMEM((width, 256), f32)],
        ),
        out_shape=[
            half,
            half,
            jax.ShapeDtypeStruct((width, 256), bf16),
            jax.ShapeDtypeStruct((8, 128), f32),
        ],
        compiler_params=pltpu.CompilerParams(vmem_limit_bytes=48 << 20),
        cost_estimate=pl.CostEstimate(flops=16 * seqs * length * width * 256, bytes_accessed=seqs * length * width * 6, transcendentals=0),
        name="qkv_bwd",
    )(at, dq, dkv, raw, nm, w_qkv, scales, cosine, sine, *earlier)


def plain_body(
    block_input,
    positions,
    cotangent,
    attention_gain,
    query_weight,
    key_weight,
    value_weight,
    query_gain,
    key_gain,
    output_weight,
    feedforward_gain,
    gate_weight,
    up_weight,
    down_weight,
):
    seq_count, span, width = block_input.shape
    groups = lax.axis_size("seq")
    size = lax.axis_size("fsdp")
    me = lax.axis_index("seq")
    length = span * groups
    rows = seq_count * length
    own_rows = seq_count * span
    shard = query_weight.shape[0]
    heads = H // groups
    kv_heads = max(1, KV // groups)
    copies = max(1, groups // KV)
    q_cols, k_cols = heads * HD, kv_heads * HD
    qkv_cols = q_cols + 2 * k_cols
    part = gate_weight.shape[1] // (groups * size)
    hidden_cols = part * size

    x_full = gather_seq(block_input, 1)

    def columns(weight, col_copies):
        shaped = weight.reshape(shard, -1, 1, HD)
        shaped = jnp.broadcast_to(shaped, (shard, shaped.shape[1], col_copies, HD))
        return shaped.reshape(shard, groups, -1)

    packed = jnp.concatenate(
        [
            columns(query_weight, 1),
            columns(key_weight, copies),
            columns(value_weight, copies),
        ],
        axis=2,
    ).transpose(1, 0, 2)
    gains = jnp.concatenate([attention_gain, feedforward_gain])
    gain_rows = jnp.zeros((16, qkv_cols), bf16).at[0, : 2 * shard].set(gains)
    packed = jnp.concatenate(
        [packed, jnp.broadcast_to(gain_rows[None], (groups, 16, qkv_cols))], axis=1
    )
    packed = gather_line(spread(packed))
    w_qkv = packed[:, :, :shard, :].reshape(width, qkv_cols)
    gain_one = packed[:, :, shard, :shard].reshape(width).astype(f32)
    gain_two = packed[:, :, shard, shard : 2 * shard].reshape(width).astype(f32)

    out_full = lax.all_gather(output_weight, ("fsdp", "seq"), axis=0, tiled=True)

    def ff_columns(weight):
        shaped = weight.reshape(shard, size, groups, part)
        return shaped.transpose(2, 0, 1, 3).reshape(groups, shard, hidden_cols)

    w_gate_up = gather_line(
        spread(jnp.concatenate([ff_columns(gate_weight), ff_columns(up_weight)], axis=2))
    ).reshape(width, 2 * hidden_cols)
    w_gate = w_gate_up[:, :hidden_cols]
    w_up = w_gate_up[:, hidden_cols:]
    w_down = gather_line(down_weight).reshape(hidden_cols, width)

    cot_full = gather_seq(cotangent, 1).reshape(rows, width)

    residual_in = x_full.reshape(rows, width).astype(f32)
    factor_one = inv_rms(residual_in)
    normed_in = (residual_in * factor_one * gain_one).astype(bf16)
    qkv_raw = matmul(normed_in, w_qkv)
    query_raw = qkv_raw[:, :q_cols]
    key_raw = qkv_raw[:, q_cols : q_cols + k_cols]
    value_rows = qkv_raw[:, q_cols + k_cols :].astype(bf16)
    cosine, sine = rope_tables(positions.reshape(rows), HD)
    query_scale = query_gain.astype(f32)
    key_scale = key_gain.astype(f32)

    def query_side(raw_rows, gain_row):
        return head_prep(raw_rows, gain_row, cosine, sine, heads)

    def key_side(raw_rows, gain_row):
        return head_prep(raw_rows, gain_row, cosine, sine, kv_heads)

    def head_view(packed_rows):
        shaped = packed_rows.reshape(seq_count, length, -1, HD)
        return jnp.repeat(shaped, heads // shaped.shape[2], axis=2)

    queries = query_side(query_raw, query_scale).astype(bf16).reshape(seq_count, length, heads, HD)
    keys = head_view(key_side(key_raw, key_scale).astype(bf16))
    values = head_view(value_rows)
    doc_start = jnp.arange(length, dtype=jnp.int32)[None, :] - positions
    outputs, log_totals = jax.vmap(attend_fwd)(queries, keys, values, doc_start)

    attn_full = gather_seq(outputs.reshape(seq_count, length, q_cols), 2)
    attn_rows = attn_full.reshape(rows, width)
    residual_mid = residual_in + matmul(attn_rows, out_full)
    factor_two = inv_rms(residual_mid)
    normed_mid = (residual_mid * factor_two * gain_two).astype(bf16)

    def own(array):
        shaped = array.reshape(seq_count, length, -1)
        return lax.dynamic_slice_in_dim(shaped, me * span, span, 1).reshape(own_rows, -1)

    gate_rows = matmul(normed_mid, w_gate)
    up_rows = matmul(normed_mid, w_up)
    sigma = jax.nn.sigmoid(gate_rows)
    hidden = (gate_rows * sigma * up_rows).astype(bf16)
    grad_hidden = matmul_nt(cot_full, w_down)
    grad_gate = (grad_hidden * up_rows * sigma * (1.0 + gate_rows * (1.0 - sigma))).astype(bf16)
    grad_up = (grad_hidden * gate_rows * sigma).astype(bf16)
    grad_normed_part = (matmul_nt(grad_gate, w_gate) + matmul_nt(grad_up, w_up)).astype(bf16)
    grad_normed_mid = reduce_seq(grad_normed_part.reshape(seq_count, length, width), 1)
    grad_normed_mid = grad_normed_mid.reshape(own_rows, width)

    residual_own = own(residual_mid)
    cot_rows = cotangent.reshape(own_rows, width).astype(f32)
    grad_mid = cot_rows + norm_bwd(residual_own, own(factor_two), gain_two, grad_normed_mid)
    grad_mid_half = grad_mid.astype(bf16)
    grad_attn_out = matmul_nt(grad_mid_half, out_full).astype(bf16)
    grad_heads = lax.all_to_all(
        grad_attn_out.reshape(seq_count, span, width), "seq", split_axis=2, concat_axis=1, tiled=True
    )

    grad_query_heads, grad_key_heads, grad_value_heads = jax.vmap(attend_bwd)(
        queries,
        keys,
        values,
        outputs,
        log_totals,
        grad_heads.reshape(seq_count, length, heads, HD),
        doc_start,
    )

    def fold(packed_rows):
        shaped = packed_rows.reshape(rows, kv_heads, -1, HD).astype(f32)
        return jnp.sum(shaped, axis=2).reshape(rows, k_cols)

    _, query_back = jax.vjp(query_side, query_raw, query_scale)
    grad_query_raw, query_gain_term = query_back(grad_query_heads.reshape(rows, q_cols).astype(f32))
    _, key_back = jax.vjp(key_side, key_raw, key_scale)
    grad_key_raw, key_gain_term = key_back(fold(grad_key_heads))
    grad_qkv = jnp.concatenate(
        [
            grad_query_raw.astype(bf16),
            grad_key_raw.astype(bf16),
            fold(grad_value_heads).astype(bf16),
        ],
        axis=1,
    )
    grad_in_part = matmul_nt(grad_qkv, w_qkv).astype(bf16)
    grad_normed_in = reduce_seq(grad_in_part.reshape(seq_count, length, width), 1)
    grad_normed_in = grad_normed_in.reshape(own_rows, width)
    own_in = block_input.reshape(own_rows, width).astype(f32)
    input_grad = (
        (grad_mid + norm_bwd(own_in, inv_rms(own_in), gain_one, grad_normed_in))
        .astype(bf16)
        .reshape(seq_count, span, width)
    )

    result_part = matmul(hidden, w_down).astype(bf16).reshape(seq_count, length, width)
    block_output = (
        (residual_own + reduce_seq(result_part, 1).reshape(own_rows, width))
        .astype(bf16)
        .reshape(seq_count, span, width)
    )

    down_grad = reduce_line(matmul_tn(hidden, cot_full).reshape(size, part, width))
    gate_up_term = matmul_tn(normed_mid, jnp.concatenate([grad_gate, grad_up], axis=1))
    gate_up_term = reduce_line(gate_up_term.reshape(size, groups * shard, 2 * hidden_cols))
    gate_up_home = spread(gate_up_term.astype(bf16).reshape(groups, shard, 2 * hidden_cols))

    def ff_home(columns_home):
        shaped = columns_home.astype(f32).reshape(groups, shard, size, part)
        return shaped.transpose(1, 2, 0, 3).reshape(shard, groups * size * part)

    gate_grad = ff_home(gate_up_home[:, :, :hidden_cols])
    up_grad = ff_home(gate_up_home[:, :, hidden_cols:])

    output_term = matmul_tn(own(attn_rows), grad_mid_half).astype(bf16)
    output_grad = lax.psum_scatter(
        output_term, ("fsdp", "seq"), scatter_dimension=0, tiled=True
    ).astype(f32)

    qkv_term = reduce_line(matmul_tn(normed_in, grad_qkv).reshape(size, groups * shard, qkv_cols))
    qkv_home = spread(qkv_term.astype(bf16).reshape(groups, shard, qkv_cols)).astype(f32)

    def home(block, col_copies):
        shaped = block.transpose(1, 0, 2).reshape(shard, -1, col_copies, HD)
        return jnp.sum(shaped, axis=2).reshape(shard, -1)

    query_grad = home(qkv_home[:, :, :q_cols], 1)
    key_grad = home(qkv_home[:, :, q_cols : q_cols + k_cols], copies)
    value_grad = home(qkv_home[:, :, q_cols + k_cols :], copies)

    def weighted(weight, grad):
        return jnp.sum(weight.astype(f32) * grad, axis=1)

    gain_one_grad = (
        weighted(query_weight, query_grad)
        + weighted(key_weight, key_grad)
        + weighted(value_weight, value_grad)
    ) / attention_gain.astype(f32)
    gain_two_grad = (
        weighted(gate_weight, gate_grad) + weighted(up_weight, up_grad)
    ) / feedforward_gain.astype(f32)

    head_gains = sum_everywhere(jnp.concatenate([query_gain_term, key_gain_term])[None])[0]
    return (
        block_output,
        input_grad,
        gain_one_grad,
        query_grad,
        key_grad,
        value_grad,
        head_gains[:HD],
        head_gains[HD:],
        output_grad,
        gain_two_grad,
        gate_grad,
        up_grad,
        down_grad,
    )


def after(array, earlier):
    first = earlier.reshape(-1)[0] if earlier.ndim == 1 else earlier[(0,) * earlier.ndim]
    return array + jnp.minimum(jnp.abs(first), 0).astype(array.dtype)


def swap_line(array, mask):
    size = lax.axis_size("fsdp")
    return lax.ppermute(array, "fsdp", [(i, i ^ mask) for i in range(size)])


def line_blocks(block):
    return [block] + [swap_line(block, m) for m in (1, 2, 3)]


def line_parts(block_of):
    me = lax.axis_index("fsdp")
    return [swap_line(block_of(me ^ m), m) for m in (1, 2, 3)]


def add_up(own, others):
    total = own.astype(f32)
    for other in others:
        total = total + other.astype(f32)
    return total


def reduce_stages(even, odd, earlier=()):
    got = swap(odd, 1)

    def sent(i):
        total = even[i].astype(f32) + got[i].astype(f32)
        for array in earlier:
            total = after(total, array)
        return swap(total.astype(bf16), 2 * i)

    return got, sent(1), sent(2), sent(3)


def own_sum(even, stages):
    total = even[0].astype(f32) + stages[0][0].astype(f32)
    for part in stages[1:]:
        total = total + part.astype(f32)
    return total


def body(
    block_input,
    positions,
    cotangent,
    attention_gain,
    query_weight,
    key_weight,
    value_weight,
    query_gain,
    key_gain,
    output_weight,
    feedforward_gain,
    gate_weight,
    up_weight,
    down_weight,
):
    seqs, span, width = block_input.shape
    groups = lax.axis_size("seq")
    size = lax.axis_size("fsdp")
    if not (groups == 8 and size == 4 and seqs % 2 == 0 and span % 64 == 0):
        return plain_body(
            block_input,
            positions,
            cotangent,
            attention_gain,
            query_weight,
            key_weight,
            value_weight,
            query_gain,
            key_gain,
            output_weight,
            feedforward_gain,
            gate_weight,
            up_weight,
            down_weight,
        )
    me = lax.axis_index("seq")
    me_line = lax.axis_index("fsdp")
    at = jnp.stack([me, me_line]).astype(jnp.int32)
    length = span * groups
    rows = seqs * length
    own_rows = seqs * span
    shard = query_weight.shape[0]
    part = gate_weight.shape[1] // (groups * size)
    hidden_cols = part * size
    padded = -(-hidden_cols // 128) * 128

    gains = jnp.concatenate([attention_gain, feedforward_gain])
    gains = jnp.zeros((shard, 128), bf16).at[0, : 2 * shard].set(gains)
    packed = spread(
        pack_columns(gate_weight, up_weight, query_weight, key_weight, value_weight, gains, groups, part)
    )
    x_blocks = partner_blocks(block_input, direct=True)
    qkv_blocks = line_blocks(packed[:, :, 2 * hidden_cols :])
    gains = [block[:, 0, 256 : 256 + 2 * shard].astype(f32) for block in qkv_blocks]
    gains = jnp.stack(
        [sum(jnp.where((me_line ^ m) == f, gains[m], 0.0) for m in range(size)) for f in range(size)]
    )
    gain_one = gains[:, :, :shard].reshape(1, width)
    gain_two = gains[:, :, shard:].reshape(1, width)
    inverse = rope_base ** (-(jnp.arange(HD // 2, dtype=f32) * 2.0) / HD)
    angles = positions.astype(f32)[:, :, None] * jnp.tile(inverse, 4)[None, None, :]
    cosine, sine = jnp.cos(angles), jnp.sin(angles)
    down_parts = lax.all_gather(
        jnp.concatenate([down_weight, output_weight], axis=0), "fsdp", axis=0, tiled=False
    )
    wo_parts = lax.all_gather(down_parts[:, part:], "seq", axis=0, tiled=False)
    w_gate_up = packed[:, :, : 2 * hidden_cols]
    for block in [*qkv_blocks[1:], x_blocks[2], x_blocks[4], x_blocks[6], cosine, sine]:
        w_gate_up = after(w_gate_up, block)
    w_gate_up = lax.all_gather(w_gate_up, "fsdp", axis=0, tiled=False).reshape(width, 2 * hidden_cols)
    cot_blocks = {0: cotangent}
    for mask in (2, 4):
        cot_blocks[mask] = swap(after(cotangent, x_blocks[6]), mask)
    cot_blocks[6] = swap(cot_blocks[2], 4)
    for mask in (0, 2, 4, 6):
        cot_blocks[mask + 1] = swap(cot_blocks[mask], 1)

    scales = jnp.concatenate(
        [jnp.tile(query_gain, 2)[None], jnp.tile(key_gain, 2)[None], jnp.zeros((6, 128), bf16)]
    ).astype(f32)
    starts = jnp.arange(length, dtype=jnp.int32)[None, :] - positions
    x_full, normed_in, qkv_raw, q_rows, kv_rows, w_qkv = qkv_fwd(
        at, x_blocks, qkv_blocks, gain_one, scales, cosine, sine, []
    )
    starts_wide = jnp.broadcast_to(starts[:, :, None], (seqs, length, 128))
    outputs, totals = attn_fwd(q_rows, kv_rows, starts_wide, span, [cot_blocks[2], cot_blocks[4]])

    (attn_rows, residual_mid, normed_mid, hidden, ff_grads, gnm_even, gnm_odd, out_even, out_odd, cot_full, w_out) = ffn(
        at,
        partner_blocks(outputs),
        [cot_blocks[j] for j in range(8)],
        down_parts,
        x_full,
        wo_parts,
        w_gate_up,
        gain_two,
    )
    flat = lambda array: array.reshape(rows, -1)

    mid_stages = reduce_stages(gnm_even, gnm_odd)
    cuts = ((0, hidden_cols), (padded, padded + hidden_cols))
    down_term = product(
        flat(hidden), flat(cot_full), (size, 1, part), ((0, width),), 16 * rows * width
    )
    grad_mid, grad_mid_half, grad_attn_out = mid_bwd(
        at, residual_mid, cotangent, gain_two, w_out, gnm_even, mid_stages, [down_term]
    )
    grad_heads = spread(grad_attn_out)
    gate_up_term = product(
        flat(normed_mid), flat(ff_grads), (size, groups, shard), cuts, 32 * rows * width, [grad_mid_half]
    )

    def block_rows(term, f, count):
        return lax.dynamic_slice_in_dim(term, f * count, count, term.ndim - 2)

    gate_up_sum = lax.psum_scatter(gate_up_term, "fsdp", scatter_dimension=0, tiled=False)
    down_sum = lax.psum_scatter(down_term, "fsdp", scatter_dimension=0, tiled=False)
    attn_own = lax.dynamic_slice_in_dim(attn_rows, me * span, span, 1).reshape(own_rows, width)
    attn_own = after(attn_own, gate_up_term)
    output_term = matmul_tn(attn_own, grad_mid_half).astype(bf16)
    output_term = output_term.reshape(size, groups, shard, width).transpose(1, 0, 2, 3)
    output_term = lax.psum_scatter(output_term, "seq", scatter_dimension=0, tiled=False)
    out_stages = reduce_stages(out_even, out_odd, [grad_heads, gate_up_term])
    gate_up_home = spread(gate_up_sum)

    totals_row = jnp.stack([totals[:, :, 0], totals[:, :, HD]], axis=1)
    totals_row = jnp.concatenate([totals_row, jnp.zeros((seqs, 6, length), f32)], axis=1)
    starts_row = jnp.broadcast_to(starts[:, None, :], (seqs, 8, length))
    grad_q, grad_kv = attn_bwd(
        q_rows, kv_rows, grad_heads, outputs, totals_row, starts_row, span, [out_stages[0], gate_up_term, down_sum]
    )
    gin_even, gin_odd, qkv_term, head_gains = qkv_bwd(
        at, grad_q, grad_kv, qkv_raw, normed_in, w_qkv, scales, cosine, sine,
        [*out_stages[1:], gate_up_sum]
    )
    in_stages = reduce_stages(gin_even, gin_odd)
    own_in = block_input.reshape(own_rows, width).astype(f32)
    grad_normed_in = own_sum(gin_even, in_stages).reshape(own_rows, width)
    input_grad = (
        (grad_mid + norm_bwd(own_in, inv_rms(own_in), gain_one, grad_normed_in))
        .astype(bf16)
        .reshape(seqs, span, width)
    )

    def two_terms(array):
        high = array.astype(bf16)
        low = (array - high.astype(f32)).astype(bf16)
        return jnp.concatenate([high, low, jnp.zeros((14, array.shape[1]), bf16)], axis=0)

    gain_rows = two_terms(head_gains[:2].reshape(1, 256))

    def sent_rows(f):
        block = after(block_rows(qkv_term, f, groups * shard), in_stages[0])
        return jnp.concatenate([block, gain_rows], axis=0)

    qkv_parts = line_parts(sent_rows)
    qkv_sum = add_up(sent_rows(me_line), qkv_parts)
    gain_rows = two_terms(qkv_sum[-16:-15] + qkv_sum[-15:-14])
    qkv_sum = qkv_sum[:-16].astype(bf16).reshape(groups, shard, 4 * HD)
    gain_rows = jnp.broadcast_to(gain_rows[None], (groups, *gain_rows.shape))
    query_grad, key_grad, value_grad, gain_one_sum, head_gains = unpack_heads(
        spread(jnp.concatenate([qkv_sum, gain_rows], axis=1)), query_weight, key_weight, value_weight
    )
    head_gains = (head_gains[0] + head_gains[1]).reshape(2, 128)

    residual_own = lax.dynamic_slice_in_dim(residual_mid, me * span, span, 1)
    block_output = after(residual_own + own_sum(out_even, out_stages), qkv_parts[0]).astype(bf16)
    down_grad = after(down_sum.astype(f32), qkv_parts[0]).reshape(part, width)
    output_grad = lax.psum_scatter(
        after(output_term, qkv_parts[0]), "fsdp", scatter_dimension=0, tiled=False
    ).astype(f32)
    gate_grad, up_grad, gain_two_sum = unpack_columns(gate_up_home, gate_weight, up_weight, part, qkv_parts[0])

    gain_one_grad = gain_one_sum[:, 0] / attention_gain.astype(f32)
    gain_two_grad = gain_two_sum[:, 0] / feedforward_gain.astype(f32)

    return (
        block_output,
        input_grad,
        gain_one_grad,
        query_grad,
        key_grad,
        value_grad,
        head_gains[0, :HD] + head_gains[0, HD:],
        head_gains[1, :HD],
        output_grad,
        gain_two_grad,
        gate_grad,
        up_grad,
        down_grad,
    )


def solution(mesh):
    shards = P(("fsdp", "seq"), None)
    vector = P(("fsdp", "seq"))
    tokens = P("fsdp", "seq", None)
    return jax.shard_map(
        body,
        mesh=mesh,
        in_specs=(
            tokens,
            P("fsdp", None),
            tokens,
            vector,
            shards,
            shards,
            shards,
            P(),
            P(),
            shards,
            vector,
            shards,
            shards,
            shards,
        ),
        out_specs=(
            tokens,
            tokens,
            vector,
            shards,
            shards,
            shards,
            P(),
            P(),
            shards,
            vector,
            shards,
            shards,
            shards,
        ),
        check_vma=False,
    )
```
